32 devices in a mesh: ctx: 8 (over z, x), fsdp: 4 (over y, core).
Axes of the slice: x: 2, y: 2, z: 4, core: 2. Of those that a mesh axis runs over, the one named last changes fastest.
Arguments:
- tokens: bfloat16 [4, 2048, 768], P('fsdp', 'ctx'), may hold values from -6 to 6
- seq_lengths: int32 [4, 2], P('fsdp'), may hold values from 1024 to 1024, as said below
- deal: int32 [4, 16], P('fsdp'), may hold values from 0 to 15, each once within a row
- w_query: float32 [768, 768], P('fsdp'), may hold values from -0.375 to 0.375
- w_key: float32 [768, 768], P('fsdp'), may hold values from -0.21875 to 0.21875
- w_value: float32 [768, 768], P('fsdp'), may hold values from -0.21875 to 0.21875
- w_attn_out: float32 [768, 768], P('fsdp'), may hold values from -1.75 to 1.75
- b_query: float32 [768], P('fsdp'), may hold values from -1.8 to 1.8
- b_value: float32 [768], P('fsdp'), may hold values from -1.8 to 1.8
- b_attn_out: float32 [768], P('fsdp'), may hold values from -1.8 to 1.8
- norm1_gain: float32 [768], P('fsdp'), may hold values from 0.5 to 1.5
- norm1_bias: float32 [768], P('fsdp'), may hold values from -1.8 to 1.8
- w_in: float32 [768, 3072], P('fsdp'), may hold values from -0.21875 to 0.21875
- b_in: float32 [3072], P('fsdp'), may hold values from -1.8 to 1.8
- w_out: float32 [3072, 768], P('fsdp'), may hold values from -0.109375 to 0.109375
- b_out: float32 [768], P('fsdp'), may hold values from -1.8 to 1.8
- norm2_gain: float32 [768], P('fsdp'), may hold values from 0.5 to 1.5
- norm2_bias: float32 [768], P('fsdp'), may hold values from -1.8 to 1.8
- cotangent: bfloat16 [4, 2048, 768], P('fsdp', 'ctx'), may hold values from -6 to 6
Outputs:
- layer_out: bfloat16 [4, 2048, 768], P('fsdp', 'ctx')
- grad_tokens: float32 [4, 2048, 768], P('fsdp', 'ctx')
- grad_w_query: float32 [768, 768], P('fsdp')
- grad_w_key: float32 [768, 768], P('fsdp')
- grad_w_value: float32 [768, 768], P('fsdp')
- grad_w_attn_out: float32 [768, 768], P('fsdp')
- grad_b_query: float32 [768], P('fsdp')
- grad_b_value: float32 [768], P('fsdp')
- grad_b_attn_out: float32 [768], P('fsdp')
- grad_norm1_gain: float32 [768], P('fsdp')
- grad_norm1_bias: float32 [768], P('fsdp')
- grad_w_in: float32 [768, 3072], P('fsdp')
- grad_b_in: float32 [3072], P('fsdp')
- grad_w_out: float32 [3072, 768], P('fsdp')
- grad_b_out: float32 [768], P('fsdp')
- grad_norm2_gain: float32 [768], P('fsdp')
- grad_norm2_bias: float32 [768], P('fsdp')
The draws below stay inside these ranges and needn't reach their ends.
Inputs may be any that keep to these rules, and one draw needn't show every extreme that they name: `seq_lengths`: row g gives the tokens of the 2 sequences of group g; each sequence starts on a block boundary and is padded to whole blocks, and the padded sequences of a row fill exactly its 16 blocks. `deal`: each row is a permutation of the natural blocks of its group; dealt slot b lies on the device with ctx index b // 2.
All inputs are finite; a program needn't handle non-finite values.
Results may differ from the reference program's by a relative error of at most 0.024.
Values may be sent and summed in bfloat16 or wider, within the bound.
A program may use at most 192 MiB of HBM per device.

```python
import math
import jax
import jax.numpy as jnp
from jax import lax

D = 768
HEADS = 12
HEAD_DIM = 64
FF = 3072
BLOCK = 128
MIN_BLOCKS = 8
NSEQ = 2
GROUP_TOK = 2048
GROUPS = 4
NB = 16


def draw_seq_lengths(key, part):
    spare = NB - NSEQ * MIN_BLOCKS
    cut_key = jax.random.fold_in(key, 11)
    tail_key = jax.random.fold_in(key, 23)
    cuts = jnp.sort(jax.random.randint(cut_key, (GROUPS, NSEQ - 1), 0, spare + 1), axis=1).astype(jnp.int32)
    group_index = jnp.arange(GROUPS, dtype=jnp.int32)[:, None]
    cuts = jnp.where(group_index == 0, 0, cuts).astype(jnp.int32)
    edges = jnp.concatenate([jnp.zeros((GROUPS, 1), jnp.int32), cuts, jnp.full((GROUPS, 1), spare, jnp.int32)], axis=1)
    blocks = MIN_BLOCKS + edges[:, 1:] - edges[:, :-1]
    tails = jax.random.randint(tail_key, (GROUPS, NSEQ), 1, BLOCK + 1).astype(jnp.int32)
    tails = jnp.where(blocks > MIN_BLOCKS, tails, BLOCK)
    seq_index = jnp.arange(NSEQ, dtype=jnp.int32)[None, :]
    tails = jnp.where((group_index == 0) & (seq_index == NSEQ - 1), BLOCK, tails)
    return ((blocks - 1) * BLOCK + tails).astype(jnp.int32)


def level_of(stream_key, shape, shards, smallest, largest):
    level = 1.0
    for dim, parts in shards:
        draws = jax.random.uniform(jax.random.fold_in(jax.random.fold_in(stream_key, 6), dim), (parts,), jnp.float32, smallest / len(shards), largest / len(shards))
        level = level * jnp.repeat(jnp.exp(draws), shape[dim] // parts).reshape((-1,) + (1,) * (len(shape) - 1 - dim))
    return level


def gaussian(key, dims, scale, limit, shards=(), held_as=jnp.bfloat16):
    drawn = jax.random.normal(key, dims, jnp.float32) * scale
    if len(shards) > 0:
        drawn = level_of(key, dims, shards, -0.22, 0.18) * drawn
    return jnp.clip(drawn, min=-limit, max=limit).astype(held_as)


def setup_inputs(seed: int = 0) -> dict:
    seeds = jax.random.split(jax.random.key(seed), 20)
    return {
        "tokens": gaussian(seeds[0], (GROUPS, GROUP_TOK, D), 1.0, 6.0, ((0, 4), (1, 8))),
        "seq_lengths": draw_seq_lengths(jax.random.fold_in(seeds[19], 71), 0),
        "deal": jax.vmap(lambda own: jax.random.permutation(own, NB))(jax.random.split(seeds[2], GROUPS)).reshape((GROUPS, NB)).astype(jnp.int32),
        "w_query": gaussian(seeds[3], (D, D), (D // 3) ** -0.5, 0.375, ((0, 4),), jnp.float32),
        "w_key": gaussian(seeds[4], (D, D), D ** -0.5, 0.21875, ((0, 4),), jnp.float32),
        "w_value": gaussian(seeds[5], (D, D), D ** -0.5, 0.21875, ((0, 4),), jnp.float32),
        "w_attn_out": gaussian(seeds[6], (D, D), (D // 64) ** -0.5, 1.75, ((0, 4),), jnp.float32),
        "b_query": gaussian(seeds[7], (D,), 0.3, 1.8, ((0, 4),), jnp.float32),
        "b_value": gaussian(seeds[8], (D,), 0.3, 1.8, ((0, 4),), jnp.float32),
        "b_attn_out": gaussian(seeds[9], (D,), 0.3, 1.8, ((0, 4),), jnp.float32),
        "norm1_gain": jnp.clip(1.0 + 0.1 * jax.random.normal(seeds[10], (D,), jnp.float32), 0.5, 1.5),
        "norm1_bias": gaussian(seeds[11], (D,), 0.3, 1.8, ((0, 4),), jnp.float32),
        "w_in": gaussian(seeds[12], (D, FF), D ** -0.5, 0.21875, ((0, 4),), jnp.float32),
        "b_in": gaussian(seeds[13], (FF,), 0.3, 1.8, ((0, 4),), jnp.float32),
        "w_out": gaussian(seeds[14], (FF, D), FF ** -0.5, 0.109375, ((0, 4),), jnp.float32),
        "b_out": gaussian(seeds[15], (D,), 0.3, 1.8, ((0, 4),), jnp.float32),
        "norm2_gain": jnp.clip(1.0 + 0.1 * jax.random.normal(seeds[16], (D,), jnp.float32), 0.5, 1.5),
        "norm2_bias": gaussian(seeds[17], (D,), 0.3, 1.8, ((0, 4),), jnp.float32),
        "cotangent": gaussian(seeds[18], (GROUPS, GROUP_TOK, D), 1.0, 6.0, ((0, 4), (1, 8))),
    }


EPSILON = 1e-12
NEG_FILL = -1e+30

@jax.custom_vjp
def low(v):
    return lax.optimization_barrier(v.astype(jnp.bfloat16)).astype(jnp.float32)

@jax.custom_vjp
def low_back(v):
    return v

def low_keep(v):
    return (low(v), None)

def low_pass(kept, grad):
    return (grad,)

def back_keep(v):
    return (v, None)

def back_low(kept, grad):
    return (low(grad),)
low.defvjp(low_keep, low_pass)
low_back.defvjp(back_keep, back_low)

def block_codes(lengths, deal_row):
    padded = ((lengths + BLOCK - 1) // BLOCK * BLOCK).astype(jnp.int32)
    seq_ends = jnp.cumsum(padded).astype(jnp.int32)
    offsets = jnp.tile(jnp.arange(BLOCK, dtype=jnp.int32), deal_row.shape[0])
    natural = (jnp.repeat(deal_row * BLOCK, BLOCK) + offsets).astype(jnp.int32)
    passed = (natural[:, None] >= seq_ends[None, :]).astype(jnp.int32)
    seq_ids = lax.optimization_barrier(jnp.sum(passed, axis=1)).astype(jnp.int32)
    begins = lax.optimization_barrier(jnp.sum(passed * padded[None, :], axis=1)).astype(jnp.int32)
    owners = (seq_ids[:, None] == jnp.arange(lengths.shape[0], dtype=jnp.int32)[None, :]).astype(jnp.int32)
    own_length = lax.optimization_barrier(jnp.sum(owners * lengths[None, :], axis=1)).astype(jnp.int32)
    key_codes = jnp.where(natural - begins < own_length, seq_ids, -1).astype(jnp.int32)
    return (seq_ids, key_codes)

def high_dot(left, right):
    return jnp.dot(left, right, precision=lax.Precision.HIGHEST, preferred_element_type=jnp.float32)

def layer_norm(residual, gain, shift):
    centre = residual - lax.optimization_barrier(jnp.mean(residual, axis=-1, keepdims=True))
    spread = lax.optimization_barrier(jnp.mean(centre * centre, axis=-1, keepdims=True))
    return centre * lax.rsqrt(spread + EPSILON) * gain + shift

def group_forward(params, inputs, query_ids, key_codes):
    query_weight, key_weight, value_weight, mix_weight, query_bias, value_bias, mix_bias, gain_one, shift_one, inner_weight, inner_bias, outer_weight, outer_bias, gain_two, shift_two = params
    rows = inputs.shape[0]
    width = math.gcd(rows, 512)
    scale = HEAD_DIM ** (-0.5)
    query = low(low_back(high_dot(inputs, query_weight) + query_bias))
    keys = low(low_back(high_dot(inputs, key_weight)))
    values = low(low_back(high_dot(inputs, value_weight) + value_bias))
    key_heads = keys.reshape(rows, HEADS, HEAD_DIM)
    value_heads = values.reshape(rows, HEADS, HEAD_DIM)

    def attend(block):
        query_part, id_part = block
        query_heads = query_part.reshape(width, HEADS, HEAD_DIM)
        scores = jnp.einsum('qhd,khd->hqk', query_heads, key_heads, precision=lax.Precision.HIGHEST, preferred_element_type=jnp.float32) * scale
        scores = jnp.where((id_part[:, None] == key_codes[None, :])[None], scores, NEG_FILL)
        scores = low_back(scores)
        shifted = jnp.exp(scores - lax.optimization_barrier(jnp.max(scores, axis=-1, keepdims=True)))
        probs = shifted / lax.optimization_barrier(jnp.sum(shifted, axis=-1, keepdims=True))
        mixed = jnp.einsum('hqk,khd->qhd', low(probs), value_heads, precision=lax.Precision.HIGHEST, preferred_element_type=jnp.float32)
        return mixed.reshape(width, HEADS * HEAD_DIM)
    attended = lax.map(jax.checkpoint(attend), (query.reshape(rows // width, width, HEADS * HEAD_DIM), query_ids.reshape(rows // width, width)))
    attn_in = low(low_back(attended.reshape(rows, HEADS * HEAD_DIM)))
    residual_one = inputs + low_back(high_dot(attn_in, mix_weight) + mix_bias)
    normal_one = layer_norm(residual_one, gain_one, shift_one)
    pre_act = low_back(high_dot(low(normal_one), inner_weight) + inner_bias)
    hidden = low(jax.nn.gelu(pre_act, approximate=False))
    residual_two = normal_one + low_back(high_dot(hidden, outer_weight) + outer_bias)
    return layer_norm(residual_two, gain_two, shift_two)

def reference(tokens, seq_lengths, deal, w_query, w_key, w_value, w_attn_out, b_query, b_value, b_attn_out, norm1_gain, norm1_bias, w_in, b_in, w_out, b_out, norm2_gain, norm2_bias, cotangent):
    ids_all, codes_all = jax.vmap(block_codes)(seq_lengths, deal)
    weights = (w_query, w_key, w_value, w_attn_out, b_query, b_value, b_attn_out, norm1_gain, norm1_bias, w_in, b_in, w_out, b_out, norm2_gain, norm2_bias)

    def forward(params, inputs):
        rounded = tuple((low(item) for item in params))

        def one_group(block):
            group_inputs, group_ids, group_codes = block
            return group_forward(rounded, group_inputs, group_ids, group_codes)
        return lax.map(jax.checkpoint(one_group), (inputs, ids_all, codes_all))
    layer_out, pull = jax.vjp(forward, weights, tokens.astype(jnp.float32))
    grads, grad_tokens = pull(cotangent.astype(jnp.float32))
    return (layer_out.astype(jnp.bfloat16), grad_tokens, grads[0], grads[1], grads[2], grads[3], grads[4], grads[5], grads[6], grads[7], grads[8], grads[9], grads[10], grads[11], grads[12], grads[13], grads[14])
```

```python
import functools

import jax
import jax.numpy as jnp
from jax import lax
from jax.experimental import pallas as pl
from jax.experimental.pallas import tpu as pltpu
from jax.sharding import PartitionSpec as P

HEADS = 12
HEAD_DIM = 64
BLOCK = 128


EPSILON = 1e-12
NEG_FILL = -1e30


def block_codes(lengths, deal_row):
    padded = (lengths + BLOCK - 1) // BLOCK * BLOCK
    seq_ends = jnp.cumsum(padded)
    offsets = jnp.tile(jnp.arange(BLOCK, dtype=jnp.int32), deal_row.shape[0])
    natural = jnp.repeat(deal_row * BLOCK, BLOCK) + offsets
    passed = (natural[:, None] >= seq_ends[None, :]).astype(jnp.int32)
    seq_ids = jnp.sum(passed, axis=1)
    begins = jnp.sum(passed * padded[None, :], axis=1)
    owners = (seq_ids[:, None] == jnp.arange(lengths.shape[0], dtype=jnp.int32)[None, :]).astype(
        jnp.int32
    )
    own_length = jnp.sum(owners * lengths[None, :], axis=1)
    key_codes = jnp.where(natural - begins < own_length, seq_ids, -1)
    return (seq_ids, key_codes)


def to_half(value):
    return value.astype(jnp.bfloat16)


def exact_gelu(value):
    return jax.nn.gelu(value, approximate=False)


def split_heads(matrix):
    return matrix.reshape(matrix.shape[0], HEADS, HEAD_DIM)


def sub_width(rows):
    width = rows
    while width > 1024 and width % 2 == 0:
        width = width // 2
    return width


def add_rows(total, term, at_row):
    current = lax.dynamic_slice_in_dim(total, at_row, term.shape[0])
    return lax.dynamic_update_slice_in_dim(total, current + term, at_row, 0)


def norm_forward(residual, gain, shift):
    centre = residual - jnp.mean(residual, axis=-1, keepdims=True)
    spread = jnp.mean(centre * centre, axis=-1, keepdims=True)
    inverse = lax.rsqrt(spread + EPSILON)
    normed = centre * inverse
    return (normed * gain + shift, normed, inverse)


def norm_backward(upstream, gain, normed, inverse):
    scaled = upstream * gain
    across = jnp.mean(scaled, axis=-1, keepdims=True)
    along = jnp.mean(scaled * normed, axis=-1, keepdims=True)
    grad_residual = inverse * (scaled - across - normed * along)
    return (grad_residual, jnp.sum(upstream * normed, axis=0), jnp.sum(upstream, axis=0))


def score_grads(
    query_heads, grad_heads, key_part, value_part, query_ids, code_part, log_totals, delta, scale
):
    scores = (
        jnp.einsum("qhd,khd->hqk", query_heads, key_part, preferred_element_type=jnp.float32)
        * scale
    )
    scores = jnp.where((query_ids[:, None] == code_part[None, :])[None], scores, NEG_FILL)
    probs = jnp.exp(scores - log_totals[:, :, None])
    grad_probs = jnp.einsum(
        "qhd,khd->hqk", grad_heads, value_part, preferred_element_type=jnp.float32
    )
    grad_scores = (probs * (grad_probs - delta[:, :, None])).astype(jnp.bfloat16)
    return (probs, grad_scores)


def attend_forward(query_heads, query_ids, key_codes_all, scale, carry, piece):
    keys, values = piece
    rows = keys.shape[0]
    width = sub_width(rows)

    def one_block(state, offset):
        running, totals, accum = state
        key_part = split_heads(lax.dynamic_slice_in_dim(keys, offset, width))
        value_part = split_heads(lax.dynamic_slice_in_dim(values, offset, width))
        code_part = lax.dynamic_slice_in_dim(key_codes_all, offset, width)
        scores = (
            jnp.einsum("qhd,khd->hqk", query_heads, key_part, preferred_element_type=jnp.float32)
            * scale
        )
        scores = jnp.where((query_ids[:, None] == code_part[None, :])[None], scores, NEG_FILL)
        newest = jnp.maximum(running, jnp.max(scores, axis=-1))
        factor = jnp.exp(running - newest)
        weights = jnp.exp(scores - newest[:, :, None])
        totals = totals * factor + jnp.sum(weights, axis=-1)
        mixed = jnp.einsum(
            "hqk,khd->qhd",
            weights.astype(jnp.bfloat16),
            value_part,
            preferred_element_type=jnp.float32,
        )
        accum = accum * jnp.transpose(factor)[:, :, None] + mixed
        return ((newest, totals, accum), None)

    carry, unused = lax.scan(one_block, carry, jnp.arange(rows // width, dtype=jnp.int32) * width)
    return carry


def attend_back(
    query_heads, grad_heads, query_ids, key_codes_all, log_totals, delta, scale, carry, piece
):
    keys, values = piece
    rows = keys.shape[0]
    width = sub_width(rows)

    def one_block(state, offset):
        grad_query, grad_keys_all, grad_values_all = state
        key_part = split_heads(lax.dynamic_slice_in_dim(keys, offset, width))
        value_part = split_heads(lax.dynamic_slice_in_dim(values, offset, width))
        code_part = lax.dynamic_slice_in_dim(key_codes_all, offset, width)
        probs, grad_scores = score_grads(
            query_heads,
            grad_heads,
            key_part,
            value_part,
            query_ids,
            code_part,
            log_totals,
            delta,
            scale,
        )
        grad_query = (
            grad_query
            + jnp.einsum("hqk,khd->qhd", grad_scores, key_part, preferred_element_type=jnp.float32)
            * scale
        )
        key_term = (
            jnp.einsum("hqk,qhd->khd", grad_scores, query_heads, preferred_element_type=jnp.float32)
            * scale
        )
        value_term = jnp.einsum(
            "hqk,qhd->khd",
            probs.astype(jnp.bfloat16),
            grad_heads,
            preferred_element_type=jnp.float32,
        )
        grad_keys_all = add_rows(grad_keys_all, key_term.reshape(width, HEADS * HEAD_DIM), offset)
        grad_values_all = add_rows(
            grad_values_all, value_term.reshape(width, HEADS * HEAD_DIM), offset
        )
        return ((grad_query, grad_keys_all, grad_values_all), None)

    carry, unused = lax.scan(one_block, carry, jnp.arange(rows // width, dtype=jnp.int32) * width)
    return carry

MESH=pl.DeviceIdType.MESH
F32=jnp.float32; BF=jnp.bfloat16

def places():
    c=lax.axis_index("ctx"); f=lax.axis_index("fsdp")
    z=c//2; x=c%2; y=f//2; k=f%2
    return c,f,z,x,y,k

def add_strips(rows, fn, step=16):
    @pl.loop(0, rows//step)
    def _(i):
        fn(pl.ds(pl.multiple_of(i*step,step),step))

def reduce_kernel(chunks, n_in, n_out, *refs):
    n=len(chunks)
    ins=refs[:n_in]; outs=refs[n_in:n_in+n_out]
    scr=refs[n_in+n_out:]
    loc=scr[0:n]; rc=scr[n:2*n]; ry=scr[2*n:3*n]; rx=scr[3*n:4*n]; cb=scr[4*n:5*n]; rz=scr[5*n:6*n]; res=scr[6*n:7*n]
    (s_load,s_out,c_s,c_r,y_s,y_r,x_s,x_r,z_s,z_r,g_s,g_r,h_s,h_r)=scr[7*n:]
    c,f,z,x,y,k=places()
    sib=(c,y*2+(1-k)); yp=(c,(1-y)*2+k); xp=(z*2+(1-x),f)
    zp=[(((z+d)%4)*2+x,f) for d in (1,2,3)]
    bar=pltpu.get_barrier_semaphore()
    for p in [sib,yp,xp]+zp:
        pl.semaphore_signal(bar,inc=1,device_id=p,device_id_type=MESH)
    pl.semaphore_wait(bar,6)
    def remote(src,dst,ss,rs,dev):
        return pltpu.make_async_remote_copy(src_ref=src,dst_ref=dst,send_sem=ss,recv_sem=rs,device_id=dev,device_id_type=MESH)
    def cp_load(i,yy):
        ii,slab,_,_,_,_=chunks[i]
        return pltpu.make_async_copy(slab(ins[ii],yy*2+k),loc[i].at[yy],s_load.at[i,yy])
    def cp_c(i,yy):
        ii,slab,_,_,_,_=chunks[i]
        return remote(slab(ins[ii],yy*2+(1-k)),rc[i].at[yy],c_s.at[i,yy],c_r.at[i,yy],sib)
    def cp_y(i): return remote(loc[i].at[1-y],ry[i],y_s.at[i],y_r.at[i],yp)
    def xhalf(i,xx):
        w=chunks[i][5]//2
        return pl.ds(pl.multiple_of(xx*w,128),w)
    def zrows(i,zz):
        r=chunks[i][4]//4
        return pl.ds(pl.multiple_of(zz*r,r),r)
    def cp_x(i): return remote(loc[i].at[y,:,xhalf(i,1-x)],rx[i],x_s.at[i],x_r.at[i],xp)
    def cp_z(i,d): return remote(cb[i].at[zrows(i,(z+d)%4)],rz[i].at[d-1],z_s.at[i,d-1],z_r.at[i,d-1],zp[d-1])
    def cp_g(i,d): return remote(res[i].at[x,zrows(i,z)],res[i].at[x,zrows(i,z)],g_s.at[i,d-1],g_r.at[i,d-1],zp[d-1])
    def cp_g_in(i,d):
        zz=(z+4-d)%4
        return remote(res[i].at[x,zrows(i,zz)],res[i].at[x,zrows(i,zz)],g_s.at[i,d-1],g_r.at[i,d-1],zp[d-1])
    def cp_h(i): return remote(res[i].at[x],res[i].at[x],h_s.at[i],h_r.at[i],xp)
    def cp_h_in(i): return remote(res[i].at[1-x],res[i].at[1-x],h_s.at[i],h_r.at[i],xp)
    def cp_out(i,xx):
        _,_,oi,osl,r,w=chunks[i]
        return pltpu.make_async_copy(res[i].at[xx],osl(outs[oi],xx),s_out.at[i,xx])
    def start0(i):
        for yy in (0,1):
            cp_load(i,yy).start(); cp_c(i,yy).start()
    def stage1(i):
        for yy in (0,1):
            cp_load(i,yy).wait(); cp_c(i,yy).wait()
        r=chunks[i][4]
        def go(s):
            for yy in (0,1):
                loc[i][yy,s]=(loc[i][yy,s].astype(F32)+rc[i][yy,s].astype(F32)).astype(BF)
        add_strips(r,go)
        cp_y(i).start()
    def stage2(i):
        cp_y(i).wait()
        r=chunks[i][4]
        def go(s):
            loc[i][y,s]=(loc[i][y,s].astype(F32)+ry[i][s].astype(F32)).astype(BF)
        add_strips(r,go)
        cp_x(i).start()
    def stage3(i):
        cp_x(i).wait()
        def go(s):
            cb[i][s]=(loc[i][y,s,xhalf(i,x)].astype(F32)+rx[i][s].astype(F32)).astype(BF)
        add_strips(chunks[i][4],go)
        for d in (1,2,3): cp_z(i,d).start()
    def stage4(i):
        for d in (1,2,3): cp_z(i,d).wait()
        r=chunks[i][4]//4
        def go(j):
            o=pl.multiple_of(z*r+j*16,16)
            s=pl.ds(pl.multiple_of(j*16,16),16)
            v=cb[i][pl.ds(o,16)].astype(F32)
            for d in range(3): v=v+rz[i][d,s].astype(F32)
            res[i][x,pl.ds(o,16)]=v.astype(BF)
        pl.loop(0,r//16)(go)
        for d in (1,2,3): cp_g(i,d).start()
    def stage5(i):
        for d in (1,2,3):
            cp_g(i,d).wait_send(); cp_g_in(i,d).wait_recv()
        cp_h(i).start()
        cp_out(i,x).start()
    def stage6(i):
        cp_h(i).wait_send(); cp_h_in(i).wait_recv()
        cp_out(i,1-x).start()
    start0(0); start0(1)
    stages=[stage1,stage2,stage3,stage4,stage5,stage6]
    for t in range(n+5):
        if t+2<n: start0(t+2)
        for s,st in enumerate(stages):
            if 0<=t-s<n: st(t-s)
    for i in range(n):
        for xx in (0,1): cp_out(i,xx).wait()

def reduce_grads(gq,gk,gv,go,gin,gout,gvec,cid=1):
    ins=[gq,gk,gv,go,gin,gout,gvec]
    d=gq.shape[0]//4
    w=gq.shape[1]
    chunks=[]
    fo=gout.shape[0]//4
    for j in range(fo//d):
        chunks.append((5,lambda r,f,j=j:r.at[pl.ds(pl.multiple_of(f*fo+j*d,d),d)],5,
            lambda o,xx,j=j:o.at[pl.ds(j*d,d),pl.ds(pl.multiple_of(xx*(w//2),128),w//2)],d,w))
    for j in range(gin.shape[1]//w):
        chunks.append((4,lambda r,f,j=j:r.at[pl.ds(pl.multiple_of(f*d,d),d),pl.ds(j*w,w)],4,
            lambda o,xx,j=j:o.at[:,pl.ds(pl.multiple_of(j*w+xx*(w//2),128),w//2)],d,w))
    for m in (3,0,1,2):
        chunks.append((m,lambda r,f:r.at[pl.ds(pl.multiple_of(f*d,d),d)],m,
            lambda o,xx:o.at[:,pl.ds(pl.multiple_of(xx*(w//2),128),w//2)],d,w))
    vr=gvec.shape[0]//4; vw=gvec.shape[1]
    chunks.append((6,lambda r,f:r.at[pl.ds(pl.multiple_of(f*vr,vr),vr)],6,
            lambda o,xx:o.at[:,pl.ds(pl.multiple_of(xx*(vw//2),128),vw//2)],vr,vw))
    n=len(chunks)
    scr=[]
    scr+=[pltpu.VMEM((2,c[4],c[5]),BF) for c in chunks]
    scr+=[pltpu.VMEM((2,c[4],c[5]),BF) for c in chunks]
    scr+=[pltpu.VMEM((c[4],c[5]),BF) for c in chunks]
    scr+=[pltpu.VMEM((c[4],c[5]//2),BF) for c in chunks]
    scr+=[pltpu.VMEM((c[4],c[5]//2),BF) for c in chunks]
    scr+=[pltpu.VMEM((3,c[4]//4,c[5]//2),BF) for c in chunks]
    scr+=[pltpu.VMEM((2,c[4],c[5]//2),BF) for c in chunks]
    D=pltpu.SemaphoreType.DMA
    scr+=[D((n,2)),D((n,2)),D((n,2)),D((n,2)),D((n,)),D((n,)),D((n,)),D((n,)),D((n,3)),D((n,3)),D((n,3)),D((n,3)),D((n,)),D((n,))]
    outs=[jax.ShapeDtypeStruct((a.shape[0]//4,a.shape[1]),BF) for a in ins]
    return pl.pallas_call(functools.partial(reduce_kernel,chunks,7,7),out_shape=outs,
        in_specs=[pl.BlockSpec(memory_space=pl.ANY)]*7,out_specs=[pl.BlockSpec(memory_space=pl.ANY)]*7,
        scratch_shapes=scr,compiler_params=pltpu.CompilerParams(collective_id=cid,has_side_effects=True,vmem_limit_bytes=56*2**20),
        cost_estimate=pl.CostEstimate(flops=10**7,bytes_accessed=2*10**8,transcendentals=0),name="grad_reduce")(*ins)


def in_order(matrices, vectors, inner_bias):
    return (
        matrices[0],
        matrices[1],
        matrices[2],
        matrices[3],
        vectors[0],
        vectors[1],
        vectors[2],
        vectors[3],
        vectors[4],
        matrices[4],
        inner_bias,
        matrices[5],
        vectors[5],
        vectors[6],
        vectors[7],
    )


def reduce_plain(matrices, vectors, inner_bias):
    out = []
    for item in in_order(matrices, vectors, inner_bias):
        share = lax.psum_scatter(item.astype(jnp.bfloat16), "fsdp", scatter_dimension=0, tiled=True)
        out.append(lax.psum(share, "ctx").astype(jnp.float32))
    return tuple(out)


def reduce_fast(matrices, vectors, inner_bias):
    width = vectors[0].shape[0]
    stacked = jnp.transpose(jnp.stack(vectors).reshape(8, 4, width // 4), (1, 0, 2)).reshape(4, 2 * width)
    packed = jnp.concatenate([stacked, inner_bias.reshape(4, -1)], axis=1)
    used = packed.shape[1]
    packed = jnp.pad(packed, ((0, 0), (0, 64 * 256 - used))).astype(jnp.bfloat16).reshape(256, 256)
    done = reduce_grads(*[to_half(item) for item in matrices], packed)
    done = [item.astype(jnp.float32) for item in done]
    flat = done[6].reshape(-1)[:used]
    rows = flat[: 2 * width].reshape(8, width // 4)
    return in_order(done[:6], [rows[i] for i in range(8)], flat[2 * width :])


def body(
    fast,
    tokens,
    seq_lengths,
    deal,
    w_query,
    w_key,
    w_value,
    w_attn_out,
    b_query,
    b_value,
    b_attn_out,
    norm1_gain,
    norm1_bias,
    w_in,
    b_in,
    w_out,
    b_out,
    norm2_gain,
    norm2_bias,
    cotangent,
):
    gathered = (
        lax.all_gather(to_half(w_query), "fsdp", axis=0, tiled=True),
        lax.all_gather(to_half(w_key), "fsdp", axis=0, tiled=True),
        lax.all_gather(to_half(w_value), "fsdp", axis=0, tiled=True),
        lax.all_gather(to_half(w_attn_out), "fsdp", axis=0, tiled=True),
        lax.all_gather(to_half(b_query), "fsdp", axis=0, tiled=True),
        lax.all_gather(to_half(b_value), "fsdp", axis=0, tiled=True),
        lax.all_gather(to_half(b_attn_out), "fsdp", axis=0, tiled=True),
        lax.all_gather(to_half(norm1_gain), "fsdp", axis=0, tiled=True),
        lax.all_gather(to_half(norm1_bias), "fsdp", axis=0, tiled=True),
        lax.all_gather(to_half(w_in), "fsdp", axis=0, tiled=True),
        lax.all_gather(to_half(b_in), "fsdp", axis=0, tiled=True),
        lax.all_gather(to_half(w_out), "fsdp", axis=0, tiled=True),
        lax.all_gather(to_half(b_out), "fsdp", axis=0, tiled=True),
        lax.all_gather(to_half(norm2_gain), "fsdp", axis=0, tiled=True),
        lax.all_gather(to_half(norm2_bias), "fsdp", axis=0, tiled=True),
    )
    (
        query_weight,
        key_weight,
        value_weight,
        mix_weight,
        query_bias,
        value_bias,
        mix_bias,
        gain_one,
        shift_one,
        inner_weight,
        inner_bias,
        outer_weight,
        outer_bias,
        gain_two,
        shift_two,
    ) = gathered
    scale = HEAD_DIM ** (-0.5)
    inputs = tokens[0]
    rows = inputs.shape[0]
    query_ids_all, key_codes_all = block_codes(seq_lengths[0], deal[0])
    first_row = lax.axis_index("ctx") * rows
    query_ids = lax.dynamic_slice_in_dim(query_ids_all, first_row, rows)
    query = (
        jnp.dot(inputs, query_weight, preferred_element_type=jnp.float32)
        + query_bias.astype(jnp.float32)
    ).astype(jnp.bfloat16)
    keys = jnp.dot(inputs, key_weight, preferred_element_type=jnp.float32).astype(jnp.bfloat16)
    values = (
        jnp.dot(inputs, value_weight, preferred_element_type=jnp.float32)
        + value_bias.astype(jnp.float32)
    ).astype(jnp.bfloat16)
    query_heads = split_heads(query)
    start_state = (
        jnp.full((HEADS, rows), NEG_FILL, jnp.float32),
        jnp.zeros((HEADS, rows), jnp.float32),
        jnp.zeros((rows, HEADS, HEAD_DIM), jnp.float32),
    )
    running, totals, accum = attend_forward(
        query_heads,
        query_ids,
        key_codes_all,
        scale,
        start_state,
        (
            lax.all_gather(keys, "ctx", axis=0, tiled=True),
            lax.all_gather(values, "ctx", axis=0, tiled=True),
        ),
    )
    out_heads = accum / jnp.transpose(totals)[:, :, None]
    log_totals = running + jnp.log(totals)
    attn_in = out_heads.reshape(rows, HEADS * HEAD_DIM).astype(jnp.bfloat16)
    residual_one = (
        inputs.astype(jnp.float32)
        + jnp.dot(attn_in, mix_weight, preferred_element_type=jnp.float32)
        + mix_bias.astype(jnp.float32)
    )
    normal_one, normed_one, inverse_one = norm_forward(
        residual_one, gain_one.astype(jnp.float32), shift_one.astype(jnp.float32)
    )
    normal_half = normal_one.astype(jnp.bfloat16)
    pre_act = jnp.dot(
        normal_half, inner_weight, preferred_element_type=jnp.float32
    ) + inner_bias.astype(jnp.float32)
    activated, gelu_pull = jax.vjp(exact_gelu, pre_act)
    hidden = activated.astype(jnp.bfloat16)
    residual_two = (
        normal_one
        + jnp.dot(hidden, outer_weight, preferred_element_type=jnp.float32)
        + outer_bias.astype(jnp.float32)
    )
    layer_out, normed_two, inverse_two = norm_forward(
        residual_two, gain_two.astype(jnp.float32), shift_two.astype(jnp.float32)
    )
    upstream = cotangent[0].astype(jnp.float32)
    grad_two, grad_gain_two, grad_shift_two = norm_backward(
        upstream, gain_two.astype(jnp.float32), normed_two, inverse_two
    )
    grad_branch = grad_two.astype(jnp.bfloat16)
    grad_outer_bias = jnp.sum(grad_branch.astype(jnp.float32), axis=0)
    grad_outer = jnp.einsum("tf,td->fd", hidden, grad_branch, preferred_element_type=jnp.float32)
    grad_hidden = jnp.einsum(
        "td,fd->tf", grad_branch, outer_weight, preferred_element_type=jnp.float32
    )
    grad_pre = gelu_pull(grad_hidden)[0].astype(jnp.bfloat16)
    grad_inner_bias = jnp.sum(grad_pre.astype(jnp.float32), axis=0)
    grad_inner = jnp.einsum("td,tf->df", normal_half, grad_pre, preferred_element_type=jnp.float32)
    grad_normal = grad_two + jnp.einsum(
        "tf,df->td", grad_pre, inner_weight, preferred_element_type=jnp.float32
    )
    grad_one, grad_gain_one, grad_shift_one = norm_backward(
        grad_normal, gain_one.astype(jnp.float32), normed_one, inverse_one
    )
    grad_attn = grad_one.astype(jnp.bfloat16)
    grad_mix_bias = jnp.sum(grad_attn.astype(jnp.float32), axis=0)
    grad_mix = jnp.einsum("td,te->de", attn_in, grad_attn, preferred_element_type=jnp.float32)
    grad_mixed = jnp.einsum(
        "te,de->td", grad_attn, mix_weight, preferred_element_type=jnp.float32
    ).astype(jnp.bfloat16)
    grad_heads = split_heads(grad_mixed)
    delta = jnp.einsum("qhd,qhd->hq", grad_heads.astype(jnp.float32), out_heads)
    group_rows = key_codes_all.shape[0]
    start_back = (
        jnp.zeros((rows, HEADS, HEAD_DIM), jnp.float32),
        jnp.zeros((group_rows, HEADS * HEAD_DIM), jnp.float32),
        jnp.zeros((group_rows, HEADS * HEAD_DIM), jnp.float32),
    )
    grad_query_heads, grad_keys_all, grad_values_all = attend_back(
        query_heads,
        grad_heads,
        query_ids,
        key_codes_all,
        log_totals,
        delta,
        scale,
        start_back,
        (
            lax.all_gather(keys, "ctx", axis=0, tiled=True),
            lax.all_gather(values, "ctx", axis=0, tiled=True),
        ),
    )
    grad_keys_flat, grad_values_flat = (
        lax.psum_scatter(
            grad_keys_all.astype(jnp.bfloat16), "ctx", scatter_dimension=0, tiled=True
        ).astype(jnp.float32),
        lax.psum_scatter(
            grad_values_all.astype(jnp.bfloat16), "ctx", scatter_dimension=0, tiled=True
        ).astype(jnp.float32),
    )
    grad_query_half = grad_query_heads.reshape(rows, HEADS * HEAD_DIM).astype(jnp.bfloat16)
    grad_keys_half = grad_keys_flat.astype(jnp.bfloat16)
    grad_values_half = grad_values_flat.astype(jnp.bfloat16)
    grad_query_weight = jnp.einsum(
        "td,te->de", inputs, grad_query_half, preferred_element_type=jnp.float32
    )
    grad_key_weight = jnp.einsum(
        "td,te->de", inputs, grad_keys_half, preferred_element_type=jnp.float32
    )
    grad_value_weight = jnp.einsum(
        "td,te->de", inputs, grad_values_half, preferred_element_type=jnp.float32
    )
    grad_query_bias = jnp.sum(grad_query_half.astype(jnp.float32), axis=0)
    grad_value_bias = jnp.sum(grad_values_half.astype(jnp.float32), axis=0)
    grad_inputs = (
        grad_one
        + jnp.einsum("te,de->td", grad_query_half, query_weight, preferred_element_type=jnp.float32)
        + jnp.einsum("te,de->td", grad_keys_half, key_weight, preferred_element_type=jnp.float32)
        + jnp.einsum(
            "te,de->td", grad_values_half, value_weight, preferred_element_type=jnp.float32
        )
    )
    matrices = (
        grad_query_weight,
        grad_key_weight,
        grad_value_weight,
        grad_mix,
        grad_inner,
        grad_outer,
    )
    vectors = (
        grad_query_bias,
        grad_value_bias,
        grad_mix_bias,
        grad_gain_one,
        grad_shift_one,
        grad_outer_bias,
        grad_gain_two,
        grad_shift_two,
    )
    if fast:
        summed = reduce_fast(matrices, vectors, grad_inner_bias)
    else:
        summed = reduce_plain(matrices, vectors, grad_inner_bias)
    return (
        layer_out.astype(jnp.bfloat16)[None],
        grad_inputs[None],
        summed[0],
        summed[1],
        summed[2],
        summed[3],
        summed[4],
        summed[5],
        summed[6],
        summed[7],
        summed[8],
        summed[9],
        summed[10],
        summed[11],
        summed[12],
        summed[13],
        summed[14],
    )


def solution(mesh):
    placed = (
        P("fsdp", "ctx", None),
        P("fsdp", None),
        P("fsdp", None),
        P("fsdp", None),
        P("fsdp", None),
        P("fsdp", None),
        P("fsdp", None),
        P("fsdp"),
        P("fsdp"),
        P("fsdp"),
        P("fsdp"),
        P("fsdp"),
        P("fsdp", None),
        P("fsdp"),
        P("fsdp", None),
        P("fsdp"),
        P("fsdp"),
        P("fsdp"),
        P("fsdp", "ctx", None),
    )
    fast = dict(mesh.shape) == {"ctx": 8, "fsdp": 4}
    return jax.shard_map(
        functools.partial(body, fast),
        mesh=mesh,
        in_specs=placed,
        out_specs=(
            P("fsdp", "ctx", None),
            P("fsdp", "ctx", None),
            P("fsdp", None),
            P("fsdp", None),
            P("fsdp", None),
            P("fsdp", None),
            P("fsdp"),
            P("fsdp"),
            P("fsdp"),
            P("fsdp"),
            P("fsdp"),
            P("fsdp", None),
            P("fsdp"),
            P("fsdp", None),
            P("fsdp"),
            P("fsdp"),
            P("fsdp"),
        ),
        check_vma=False,
    )
```

```python
import functools

import jax
import jax.numpy as jnp
from jax import lax
from jax.experimental import pallas as pl
from jax.experimental.pallas import tpu as pltpu
from jax.sharding import PartitionSpec as P

HEADS = 12
HEAD_DIM = 64
BLOCK = 128


EPSILON = 1e-12
NEG_FILL = -1e30


def block_codes(lengths, deal_row):
    padded = (lengths + BLOCK - 1) // BLOCK * BLOCK
    seq_ends = jnp.cumsum(padded)
    offsets = jnp.tile(jnp.arange(BLOCK, dtype=jnp.int32), deal_row.shape[0])
    natural = jnp.repeat(deal_row * BLOCK, BLOCK) + offsets
    passed = (natural[:, None] >= seq_ends[None, :]).astype(jnp.int32)
    seq_ids = jnp.sum(passed, axis=1)
    begins = jnp.sum(passed * padded[None, :], axis=1)
    owners = (seq_ids[:, None] == jnp.arange(lengths.shape[0], dtype=jnp.int32)[None, :]).astype(
        jnp.int32
    )
    own_length = jnp.sum(owners * lengths[None, :], axis=1)
    key_codes = jnp.where(natural - begins < own_length, seq_ids, -1)
    return (seq_ids, key_codes)


def to_half(value):
    return value.astype(jnp.bfloat16)


def exact_gelu(value):
    return jax.nn.gelu(value, approximate=False)


def split_heads(matrix):
    return matrix.reshape(matrix.shape[0], HEADS, HEAD_DIM)


def sub_width(rows):
    width = rows
    while width > 1024 and width % 2 == 0:
        width = width // 2
    return width


def add_rows(total, term, at_row):
    current = lax.dynamic_slice_in_dim(total, at_row, term.shape[0])
    return lax.dynamic_update_slice_in_dim(total, current + term, at_row, 0)


def norm_forward(residual, gain, shift):
    centre = residual - jnp.mean(residual, axis=-1, keepdims=True)
    spread = jnp.mean(centre * centre, axis=-1, keepdims=True)
    inverse = lax.rsqrt(spread + EPSILON)
    normed = centre * inverse
    return (normed * gain + shift, normed, inverse)


def norm_backward(upstream, gain, normed, inverse):
    scaled = upstream * gain
    across = jnp.mean(scaled, axis=-1, keepdims=True)
    along = jnp.mean(scaled * normed, axis=-1, keepdims=True)
    grad_residual = inverse * (scaled - across - normed * along)
    return (grad_residual, jnp.sum(upstream * normed, axis=0), jnp.sum(upstream, axis=0))


def score_grads(
    query_heads, grad_heads, key_part, value_part, query_ids, code_part, log_totals, delta, scale
):
    scores = (
        jnp.einsum("qhd,khd->hqk", query_heads, key_part, preferred_element_type=jnp.float32)
        * scale
    )
    scores = jnp.where((query_ids[:, None] == code_part[None, :])[None], scores, NEG_FILL)
    probs = jnp.exp(scores - log_totals[:, :, None])
    grad_probs = jnp.einsum(
        "qhd,khd->hqk", grad_heads, value_part, preferred_element_type=jnp.float32
    )
    grad_scores = (probs * (grad_probs - delta[:, :, None])).astype(jnp.bfloat16)
    return (probs, grad_scores)


def attend_forward(query_heads, query_ids, key_codes_all, scale, carry, piece):
    keys, values = piece
    rows = keys.shape[0]
    width = sub_width(rows)

    def one_block(state, offset):
        running, totals, accum = state
        key_part = split_heads(lax.dynamic_slice_in_dim(keys, offset, width))
        value_part = split_heads(lax.dynamic_slice_in_dim(values, offset, width))
        code_part = lax.dynamic_slice_in_dim(key_codes_all, offset, width)
        scores = (
            jnp.einsum("qhd,khd->hqk", query_heads, key_part, preferred_element_type=jnp.float32)
            * scale
        )
        scores = jnp.where((query_ids[:, None] == code_part[None, :])[None], scores, NEG_FILL)
        newest = jnp.maximum(running, jnp.max(scores, axis=-1))
        factor = jnp.exp(running - newest)
        weights = jnp.exp(scores - newest[:, :, None])
        totals = totals * factor + jnp.sum(weights, axis=-1)
        mixed = jnp.einsum(
            "hqk,khd->qhd",
            weights.astype(jnp.bfloat16),
            value_part,
            preferred_element_type=jnp.float32,
        )
        accum = accum * jnp.transpose(factor)[:, :, None] + mixed
        return ((newest, totals, accum), None)

    carry, unused = lax.scan(one_block, carry, jnp.arange(rows // width, dtype=jnp.int32) * width)
    return carry


def attend_back(
    query_heads, grad_heads, query_ids, key_codes_all, log_totals, delta, scale, carry, piece
):
    keys, values = piece
    rows = keys.shape[0]
    width = sub_width(rows)

    def one_block(state, offset):
        grad_query, grad_keys_all, grad_values_all = state
        key_part = split_heads(lax.dynamic_slice_in_dim(keys, offset, width))
        value_part = split_heads(lax.dynamic_slice_in_dim(values, offset, width))
        code_part = lax.dynamic_slice_in_dim(key_codes_all, offset, width)
        probs, grad_scores = score_grads(
            query_heads,
            grad_heads,
            key_part,
            value_part,
            query_ids,
            code_part,
            log_totals,
            delta,
            scale,
        )
        grad_query = (
            grad_query
            + jnp.einsum("hqk,khd->qhd", grad_scores, key_part, preferred_element_type=jnp.float32)
            * scale
        )
        key_term = (
            jnp.einsum("hqk,qhd->khd", grad_scores, query_heads, preferred_element_type=jnp.float32)
            * scale
        )
        value_term = jnp.einsum(
            "hqk,qhd->khd",
            probs.astype(jnp.bfloat16),
            grad_heads,
            preferred_element_type=jnp.float32,
        )
        grad_keys_all = add_rows(grad_keys_all, key_term.reshape(width, HEADS * HEAD_DIM), offset)
        grad_values_all = add_rows(
            grad_values_all, value_term.reshape(width, HEADS * HEAD_DIM), offset
        )
        return ((grad_query, grad_keys_all, grad_values_all), None)

    carry, unused = lax.scan(one_block, carry, jnp.arange(rows // width, dtype=jnp.int32) * width)
    return carry


def body(
    tokens,
    seq_lengths,
    deal,
    w_query,
    w_key,
    w_value,
    w_attn_out,
    b_query,
    b_value,
    b_attn_out,
    norm1_gain,
    norm1_bias,
    w_in,
    b_in,
    w_out,
    b_out,
    norm2_gain,
    norm2_bias,
    cotangent,
):
    gathered = (
        lax.all_gather(to_half(w_query), "fsdp", axis=0, tiled=True),
        lax.all_gather(to_half(w_key), "fsdp", axis=0, tiled=True),
        lax.all_gather(to_half(w_value), "fsdp", axis=0, tiled=True),
        lax.all_gather(to_half(w_attn_out), "fsdp", axis=0, tiled=True),
        lax.all_gather(to_half(b_query), "fsdp", axis=0, tiled=True),
        lax.all_gather(to_half(b_value), "fsdp", axis=0, tiled=True),
        lax.all_gather(to_half(b_attn_out), "fsdp", axis=0, tiled=True),
        lax.all_gather(to_half(norm1_gain), "fsdp", axis=0, tiled=True),
        lax.all_gather(to_half(norm1_bias), "fsdp", axis=0, tiled=True),
        lax.all_gather(to_half(w_in), "fsdp", axis=0, tiled=True),
        lax.all_gather(to_half(b_in), "fsdp", axis=0, tiled=True),
        lax.all_gather(to_half(w_out), "fsdp", axis=0, tiled=True),
        lax.all_gather(to_half(b_out), "fsdp", axis=0, tiled=True),
        lax.all_gather(to_half(norm2_gain), "fsdp", axis=0, tiled=True),
        lax.all_gather(to_half(norm2_bias), "fsdp", axis=0, tiled=True),
    )
    (
        query_weight,
        key_weight,
        value_weight,
        mix_weight,
        query_bias,
        value_bias,
        mix_bias,
        gain_one,
        shift_one,
        inner_weight,
        inner_bias,
        outer_weight,
        outer_bias,
        gain_two,
        shift_two,
    ) = gathered
    scale = HEAD_DIM ** (-0.5)
    inputs = tokens[0]
    rows = inputs.shape[0]
    query_ids_all, key_codes_all = block_codes(seq_lengths[0], deal[0])
    first_row = lax.axis_index("ctx") * rows
    query_ids = lax.dynamic_slice_in_dim(query_ids_all, first_row, rows)
    query = (
        jnp.dot(inputs, query_weight, preferred_element_type=jnp.float32)
        + query_bias.astype(jnp.float32)
    ).astype(jnp.bfloat16)
    keys = jnp.dot(inputs, key_weight, preferred_element_type=jnp.float32).astype(jnp.bfloat16)
    values = (
        jnp.dot(inputs, value_weight, preferred_element_type=jnp.float32)
        + value_bias.astype(jnp.float32)
    ).astype(jnp.bfloat16)
    query_heads = split_heads(query)
    start_state = (
        jnp.full((HEADS, rows), NEG_FILL, jnp.float32),
        jnp.zeros((HEADS, rows), jnp.float32),
        jnp.zeros((rows, HEADS, HEAD_DIM), jnp.float32),
    )
    running, totals, accum = attend_forward(
        query_heads,
        query_ids,
        key_codes_all,
        scale,
        start_state,
        (
            lax.all_gather(keys, "ctx", axis=0, tiled=True),
            lax.all_gather(values, "ctx", axis=0, tiled=True),
        ),
    )
    out_heads = accum / jnp.transpose(totals)[:, :, None]
    log_totals = running + jnp.log(totals)
    attn_in = out_heads.reshape(rows, HEADS * HEAD_DIM).astype(jnp.bfloat16)
    residual_one = (
        inputs.astype(jnp.float32)
        + jnp.dot(attn_in, mix_weight, preferred_element_type=jnp.float32)
        + mix_bias.astype(jnp.float32)
    )
    normal_one, normed_one, inverse_one = norm_forward(
        residual_one, gain_one.astype(jnp.float32), shift_one.astype(jnp.float32)
    )
    normal_half = normal_one.astype(jnp.bfloat16)
    pre_act = jnp.dot(
        normal_half, inner_weight, preferred_element_type=jnp.float32
    ) + inner_bias.astype(jnp.float32)
    activated, gelu_pull = jax.vjp(exact_gelu, pre_act)
    hidden = activated.astype(jnp.bfloat16)
    residual_two = (
        normal_one
        + jnp.dot(hidden, outer_weight, preferred_element_type=jnp.float32)
        + outer_bias.astype(jnp.float32)
    )
    layer_out, normed_two, inverse_two = norm_forward(
        residual_two, gain_two.astype(jnp.float32), shift_two.astype(jnp.float32)
    )
    upstream = cotangent[0].astype(jnp.float32)
    grad_two, grad_gain_two, grad_shift_two = norm_backward(
        upstream, gain_two.astype(jnp.float32), normed_two, inverse_two
    )
    grad_branch = grad_two.astype(jnp.bfloat16)
    grad_outer_bias = jnp.sum(grad_branch.astype(jnp.float32), axis=0)
    grad_outer = jnp.einsum("tf,td->fd", hidden, grad_branch, preferred_element_type=jnp.float32)
    grad_hidden = jnp.einsum(
        "td,fd->tf", grad_branch, outer_weight, preferred_element_type=jnp.float32
    )
    grad_pre = gelu_pull(grad_hidden)[0].astype(jnp.bfloat16)
    grad_inner_bias = jnp.sum(grad_pre.astype(jnp.float32), axis=0)
    grad_inner = jnp.einsum("td,tf->df", normal_half, grad_pre, preferred_element_type=jnp.float32)
    grad_normal = grad_two + jnp.einsum(
        "tf,df->td", grad_pre, inner_weight, preferred_element_type=jnp.float32
    )
    grad_one, grad_gain_one, grad_shift_one = norm_backward(
        grad_normal, gain_one.astype(jnp.float32), normed_one, inverse_one
    )
    grad_attn = grad_one.astype(jnp.bfloat16)
    grad_mix_bias = jnp.sum(grad_attn.astype(jnp.float32), axis=0)
    grad_mix = jnp.einsum("td,te->de", attn_in, grad_attn, preferred_element_type=jnp.float32)
    grad_mixed = jnp.einsum(
        "te,de->td", grad_attn, mix_weight, preferred_element_type=jnp.float32
    ).astype(jnp.bfloat16)
    grad_heads = split_heads(grad_mixed)
    delta = jnp.einsum("qhd,qhd->hq", grad_heads.astype(jnp.float32), out_heads)
    group_rows = key_codes_all.shape[0]
    start_back = (
        jnp.zeros((rows, HEADS, HEAD_DIM), jnp.float32),
        jnp.zeros((group_rows, HEADS * HEAD_DIM), jnp.float32),
        jnp.zeros((group_rows, HEADS * HEAD_DIM), jnp.float32),
    )
    grad_query_heads, grad_keys_all, grad_values_all = attend_back(
        query_heads,
        grad_heads,
        query_ids,
        key_codes_all,
        log_totals,
        delta,
        scale,
        start_back,
        (
            lax.all_gather(keys, "ctx", axis=0, tiled=True),
            lax.all_gather(values, "ctx", axis=0, tiled=True),
        ),
    )
    grad_keys_flat, grad_values_flat = (
        lax.psum_scatter(
            grad_keys_all.astype(jnp.bfloat16), "ctx", scatter_dimension=0, tiled=True
        ).astype(jnp.float32),
        lax.psum_scatter(
            grad_values_all.astype(jnp.bfloat16), "ctx", scatter_dimension=0, tiled=True
        ).astype(jnp.float32),
    )
    grad_query_half = grad_query_heads.reshape(rows, HEADS * HEAD_DIM).astype(jnp.bfloat16)
    grad_keys_half = grad_keys_flat.astype(jnp.bfloat16)
    grad_values_half = grad_values_flat.astype(jnp.bfloat16)
    grad_query_weight = jnp.einsum(
        "td,te->de", inputs, grad_query_half, preferred_element_type=jnp.float32
    )
    grad_key_weight = jnp.einsum(
        "td,te->de", inputs, grad_keys_half, preferred_element_type=jnp.float32
    )
    grad_value_weight = jnp.einsum(
        "td,te->de", inputs, grad_values_half, preferred_element_type=jnp.float32
    )
    grad_query_bias = jnp.sum(grad_query_half.astype(jnp.float32), axis=0)
    grad_value_bias = jnp.sum(grad_values_half.astype(jnp.float32), axis=0)
    grad_inputs = (
        grad_one
        + jnp.einsum("te,de->td", grad_query_half, query_weight, preferred_element_type=jnp.float32)
        + jnp.einsum("te,de->td", grad_keys_half, key_weight, preferred_element_type=jnp.float32)
        + jnp.einsum(
            "te,de->td", grad_values_half, value_weight, preferred_element_type=jnp.float32
        )
    )
    shares = (
        lax.psum_scatter(
            grad_query_weight.astype(jnp.bfloat16), "fsdp", scatter_dimension=0, tiled=True
        ).astype(jnp.float32),
        lax.psum_scatter(
            grad_key_weight.astype(jnp.bfloat16), "fsdp", scatter_dimension=0, tiled=True
        ).astype(jnp.float32),
        lax.psum_scatter(
            grad_value_weight.astype(jnp.bfloat16), "fsdp", scatter_dimension=0, tiled=True
        ).astype(jnp.float32),
        lax.psum_scatter(
            grad_mix.astype(jnp.bfloat16), "fsdp", scatter_dimension=0, tiled=True
        ).astype(jnp.float32),
        lax.psum_scatter(
            grad_query_bias.astype(jnp.bfloat16), "fsdp", scatter_dimension=0, tiled=True
        ).astype(jnp.float32),
        lax.psum_scatter(
            grad_value_bias.astype(jnp.bfloat16), "fsdp", scatter_dimension=0, tiled=True
        ).astype(jnp.float32),
        lax.psum_scatter(
            grad_mix_bias.astype(jnp.bfloat16), "fsdp", scatter_dimension=0, tiled=True
        ).astype(jnp.float32),
        lax.psum_scatter(
            grad_gain_one.astype(jnp.bfloat16), "fsdp", scatter_dimension=0, tiled=True
        ).astype(jnp.float32),
        lax.psum_scatter(
            grad_shift_one.astype(jnp.bfloat16), "fsdp", scatter_dimension=0, tiled=True
        ).astype(jnp.float32),
        lax.psum_scatter(
            grad_inner.astype(jnp.bfloat16), "fsdp", scatter_dimension=0, tiled=True
        ).astype(jnp.float32),
        lax.psum_scatter(
            grad_inner_bias.astype(jnp.bfloat16), "fsdp", scatter_dimension=0, tiled=True
        ).astype(jnp.float32),
        lax.psum_scatter(
            grad_outer.astype(jnp.bfloat16), "fsdp", scatter_dimension=0, tiled=True
        ).astype(jnp.float32),
        lax.psum_scatter(
            grad_outer_bias.astype(jnp.bfloat16), "fsdp", scatter_dimension=0, tiled=True
        ).astype(jnp.float32),
        lax.psum_scatter(
            grad_gain_two.astype(jnp.bfloat16), "fsdp", scatter_dimension=0, tiled=True
        ).astype(jnp.float32),
        lax.psum_scatter(
            grad_shift_two.astype(jnp.bfloat16), "fsdp", scatter_dimension=0, tiled=True
        ).astype(jnp.float32),
    )
    summed = (
        lax.psum(shares[0].astype(jnp.bfloat16), "ctx").astype(jnp.float32),
        lax.psum(shares[1].astype(jnp.bfloat16), "ctx").astype(jnp.float32),
        lax.psum(shares[2].astype(jnp.bfloat16), "ctx").astype(jnp.float32),
        lax.psum(shares[3].astype(jnp.bfloat16), "ctx").astype(jnp.float32),
        lax.psum(shares[4].astype(jnp.bfloat16), "ctx").astype(jnp.float32),
        lax.psum(shares[5].astype(jnp.bfloat16), "ctx").astype(jnp.float32),
        lax.psum(shares[6].astype(jnp.bfloat16), "ctx").astype(jnp.float32),
        lax.psum(shares[7].astype(jnp.bfloat16), "ctx").astype(jnp.float32),
        lax.psum(shares[8].astype(jnp.bfloat16), "ctx").astype(jnp.float32),
        lax.psum(shares[9].astype(jnp.bfloat16), "ctx").astype(jnp.float32),
        lax.psum(shares[10].astype(jnp.bfloat16), "ctx").astype(jnp.float32),
        lax.psum(shares[11].astype(jnp.bfloat16), "ctx").astype(jnp.float32),
        lax.psum(shares[12].astype(jnp.bfloat16), "ctx").astype(jnp.float32),
        lax.psum(shares[13].astype(jnp.bfloat16), "ctx").astype(jnp.float32),
        lax.psum(shares[14].astype(jnp.bfloat16), "ctx").astype(jnp.float32),
    )
    return (
        layer_out.astype(jnp.bfloat16)[None],
        grad_inputs[None],
        summed[0],
        summed[1],
        summed[2],
        summed[3],
        summed[4],
        summed[5],
        summed[6],
        summed[7],
        summed[8],
        summed[9],
        summed[10],
        summed[11],
        summed[12],
        summed[13],
        summed[14],
    )


MESH=pl.DeviceIdType.MESH
F32=jnp.float32; BF=jnp.bfloat16

def places():
    c=lax.axis_index("ctx"); f=lax.axis_index("fsdp")
    z=c//2; x=c%2; y=f//2; k=f%2
    return c,f,z,x,y,k

def add_strips(rows, fn, step=16):
    @pl.loop(0, rows//step)
    def _(i):
        fn(pl.ds(pl.multiple_of(i*step,step),step))

def reduce_kernel(chunks, n_in, n_out, *refs):
    n=len(chunks)
    ins=refs[:n_in]; outs=refs[n_in:n_in+n_out]
    scr=refs[n_in+n_out:]
    loc=scr[0:n]; rc=scr[n:2*n]; ry=scr[2*n:3*n]; rx=scr[3*n:4*n]; cb=scr[4*n:5*n]; rz=scr[5*n:6*n]; res=scr[6*n:7*n]
    (s_load,s_out,c_s,c_r,y_s,y_r,x_s,x_r,z_s,z_r,g_s,g_r,h_s,h_r)=scr[7*n:]
    c,f,z,x,y,k=places()
    sib=(c,y*2+(1-k)); yp=(c,(1-y)*2+k); xp=(z*2+(1-x),f)
    zp=[(((z+d)%4)*2+x,f) for d in (1,2,3)]
    bar=pltpu.get_barrier_semaphore()
    for p in [sib,yp,xp]+zp:
        pl.semaphore_signal(bar,inc=1,device_id=p,device_id_type=MESH)
    pl.semaphore_wait(bar,6)
    def remote(src,dst,ss,rs,dev):
        return pltpu.make_async_remote_copy(src_ref=src,dst_ref=dst,send_sem=ss,recv_sem=rs,device_id=dev,device_id_type=MESH)
    def cp_load(i,yy):
        ii,slab,_,_,_,_=chunks[i]
        return pltpu.make_async_copy(slab(ins[ii],yy*2+k),loc[i].at[yy],s_load.at[i,yy])
    def cp_c(i,yy):
        ii,slab,_,_,_,_=chunks[i]
        return remote(slab(ins[ii],yy*2+(1-k)),rc[i].at[yy],c_s.at[i,yy],c_r.at[i,yy],sib)
    def cp_y(i): return remote(loc[i].at[1-y],ry[i],y_s.at[i],y_r.at[i],yp)
    def xhalf(i,xx):
        w=chunks[i][5]//2
        return pl.ds(pl.multiple_of(xx*w,128),w)
    def zrows(i,zz):
        r=chunks[i][4]//4
        return pl.ds(pl.multiple_of(zz*r,r),r)
    def cp_x(i): return remote(loc[i].at[y,:,xhalf(i,1-x)],rx[i],x_s.at[i],x_r.at[i],xp)
    def cp_z(i,d): return remote(cb[i].at[zrows(i,(z+d)%4)],rz[i].at[d-1],z_s.at[i,d-1],z_r.at[i,d-1],zp[d-1])
    def cp_g(i,d): return remote(res[i].at[x,zrows(i,z)],res[i].at[x,zrows(i,z)],g_s.at[i,d-1],g_r.at[i,d-1],zp[d-1])
    def cp_g_in(i,d):
        zz=(z+4-d)%4
        return remote(res[i].at[x,zrows(i,zz)],res[i].at[x,zrows(i,zz)],g_s.at[i,d-1],g_r.at[i,d-1],zp[d-1])
    def cp_h(i): return remote(res[i].at[x],res[i].at[x],h_s.at[i],h_r.at[i],xp)
    def cp_h_in(i): return remote(res[i].at[1-x],res[i].at[1-x],h_s.at[i],h_r.at[i],xp)
    def cp_out(i,xx):
        _,_,oi,osl,r,w=chunks[i]
        return pltpu.make_async_copy(res[i].at[xx],osl(outs[oi],xx),s_out.at[i,xx])
    def start0(i):
        for yy in (0,1):
            cp_load(i,yy).start(); cp_c(i,yy).start()
    def stage1(i):
        for yy in (0,1):
            cp_load(i,yy).wait(); cp_c(i,yy).wait()
        r=chunks[i][4]
        def go(s):
            for yy in (0,1):
                loc[i][yy,s]=(loc[i][yy,s].astype(F32)+rc[i][yy,s].astype(F32)).astype(BF)
        add_strips(r,go)
        cp_y(i).start()
    def stage2(i):
        cp_y(i).wait()
        r=chunks[i][4]
        def go(s):
            loc[i][y,s]=(loc[i][y,s].astype(F32)+ry[i][s].astype(F32)).astype(BF)
        add_strips(r,go)
        cp_x(i).start()
    def stage3(i):
        cp_x(i).wait()
        def go(s):
            cb[i][s]=(loc[i][y,s,xhalf(i,x)].astype(F32)+rx[i][s].astype(F32)).astype(BF)
        add_strips(chunks[i][4],go)
        for d in (1,2,3): cp_z(i,d).start()
    def stage4(i):
        for d in (1,2,3): cp_z(i,d).wait()
        r=chunks[i][4]//4
        def go(j):
            o=pl.multiple_of(z*r+j*16,16)
            s=pl.ds(pl.multiple_of(j*16,16),16)
            v=cb[i][pl.ds(o,16)].astype(F32)
            for d in range(3): v=v+rz[i][d,s].astype(F32)
            res[i][x,pl.ds(o,16)]=v.astype(BF)
        pl.loop(0,r//16)(go)
        for d in (1,2,3): cp_g(i,d).start()
    def stage5(i):
        for d in (1,2,3):
            cp_g(i,d).wait_send(); cp_g_in(i,d).wait_recv()
        cp_h(i).start()
        cp_out(i,x).start()
    def stage6(i):
        cp_h(i).wait_send(); cp_h_in(i).wait_recv()
        cp_out(i,1-x).start()
    start0(0); start0(1)
    stages=[stage1,stage2,stage3,stage4,stage5,stage6]
    for t in range(n+5):
        if t+2<n: start0(t+2)
        for s,st in enumerate(stages):
            if 0<=t-s<n: st(t-s)
    for i in range(n):
        for xx in (0,1): cp_out(i,xx).wait()


def remote_copy(src, dst, send, recv, device):
    return pltpu.make_async_remote_copy(
        src_ref=src,
        dst_ref=dst,
        send_sem=send,
        recv_sem=recv,
        device_id=device,
        device_id_type=MESH,
    )


def greet(peers):
    barrier = pltpu.get_barrier_semaphore()
    for peer in peers:
        pl.semaphore_signal(barrier, inc=1, device_id=peer, device_id_type=MESH)
    pl.semaphore_wait(barrier, len(peers))


def at_row(value, size):
    return pl.ds(pl.multiple_of(value, 16), size)


def window_start(part):
    return 192 * part - 64 * (part % 2)


def lane_windows(parts):
    first, second, third, fourth = parts
    return jnp.concatenate(
        [
            first[:, :128],
            first[:, 128:] + second[:, :128],
            second[:, 128:],
            third[:, :128],
            third[:, 128:] + fourth[:, :128],
            fourth[:, 128:],
        ],
        axis=1,
    )


GATHER_PIECES = ((True, 3), (True, 3), (False, 1), (True, 2), (False, 4))


def gather_project_kernel(*refs):
    (tok, wq_s, wkv_s, wo_s, win_s, wout_s, vec_s) = refs[:7]
    (qg, kvg, wq_o, wkv_o, wo_o, win_o, wout_o, vec_o) = refs[7:15]
    (wq_v, wkv_v, vec_v, send_kv, send_q) = refs[15:20]
    (own_s, own_r, own_l, y_s, y_r, cy_s, cy_r, x_s, x_r, cx_s, cx_r) = refs[20:31]
    (v_s, v_r, v_l, zk_s, zk_r, zq_s, zq_r, f_s, f_r, l_sem, out_sem) = refs[31:]
    c, f, z, x, y, k = places()
    sib = (c, y * 2 + (1 - k))
    yp = (c, (1 - y) * 2 + k)
    diag = (c, (1 - y) * 2 + (1 - k))
    xp = (z * 2 + (1 - x), f)
    zt = [(z + d) % 4 for d in (1, 2, 3)]
    zp = [(item * 2 + x, f) for item in zt]
    greet([sib, yp, diag, xp] + zp)
    shards = (wq_s, wkv_s, wo_s, win_s, wout_s)
    wholes = (wq_v, wkv_v, wo_o, win_o, wout_o)
    fy = (1 - y) * 2 + k
    first = [0]
    for split, count in GATHER_PIECES:
        first.append(first[-1] + count)

    def piece_rows(u, j, xx):
        rows = shards[u].shape[0]
        split, count = GATHER_PIECES[u]
        if split:
            size = rows // 2 // count
            return xx * (rows // 2) + j * size, size
        size = rows // count
        return j * size, size

    def own(u):
        rows = shards[u].shape[0]
        there = wholes[u].at[at_row(f * rows, rows)]
        return remote_copy(shards[u], there, own_s.at[u], own_r.at[u], sib)

    def keep(u):
        rows = shards[u].shape[0]
        there = wholes[u].at[at_row(f * rows, rows)]
        return pltpu.make_async_copy(shards[u], there, own_l.at[u])

    def over_y(u, j):
        rows = shards[u].shape[0]
        start, size = piece_rows(u, j, x)
        i = first[u] + j
        return remote_copy(
            shards[u].at[at_row(start, size)],
            wholes[u].at[at_row(f * rows + start, size)],
            y_s.at[i],
            y_r.at[i],
            yp,
        )

    def landed(u, j, xx):
        rows = shards[u].shape[0]
        start, size = piece_rows(u, j, xx)
        return wholes[u].at[at_row(fy * rows + start, size)]

    def relay_core(u, j):
        i = first[u] + j
        ref = landed(u, j, x)
        return remote_copy(ref, ref, cy_s.at[i], cy_r.at[i], sib)

    def relay_x(u, j):
        i = first[u] + j
        ref = landed(u, j, x)
        return remote_copy(ref, ref, x_s.at[i], x_r.at[i], xp)

    def relay_core_x(u, j):
        i = first[u] + j
        ref = landed(u, j, 1 - x)
        return remote_copy(ref, ref, cx_s.at[i], cx_r.at[i], sib)

    def on_y(u, j):
        over_y(u, j).wait_recv()
        relay_core(u, j).start()
        if GATHER_PIECES[u][0]:
            relay_x(u, j).start()

    def on_x(u, j):
        if GATHER_PIECES[u][0]:
            relay_x(u, j).wait_recv()
            relay_core_x(u, j).start()

    def finish_recv(u):
        own(u).wait_recv()
        keep(u).wait()
        for j in range(GATHER_PIECES[u][1]):
            relay_core(u, j).wait_recv()
            if GATHER_PIECES[u][0]:
                relay_core_x(u, j).wait_recv()

    def finish_send(u):
        own(u).wait_send()
        for j in range(GATHER_PIECES[u][1]):
            over_y(u, j).wait_send()
            relay_core(u, j).wait_send()
            if GATHER_PIECES[u][0]:
                relay_x(u, j).wait_send()
                relay_core_x(u, j).wait_send()

    def vec(i, device):
        return remote_copy(vec_s, vec_v.at[f], v_s.at[i], v_r.at[i], device)

    for j in range(3):
        over_y(1, j).start()
        over_y(0, j).start()
    vec_peers = (sib, yp, diag)
    for i in range(3):
        vec(i, vec_peers[i]).start()
    vec_keep = pltpu.make_async_copy(vec_s, vec_v.at[f], v_l)
    vec_keep.start()
    for u in (1, 0):
        own(u).start()
        keep(u).start()
    for j in range(3):
        on_y(1, j)
        on_y(0, j)
    for u in (3, 2, 4):
        for j in range(GATHER_PIECES[u][1]):
            over_y(u, j).start()
        own(u).start()
        keep(u).start()
    for j in range(3):
        on_x(1, j)
        on_x(0, j)
    for i in range(3):
        vec(i, vec_peers[i]).wait_recv()
    vec_keep.wait()
    finish_recv(1)

    def z_kv(d):
        return remote_copy(
            send_kv.at[zt[d]], kvg.at[c], zk_s.at[d], zk_r.at[d], zp[d]
        )

    def z_kv_in(d):
        slot = ((z + 3 - d) % 4) * 2 + x
        return remote_copy(kvg.at[slot], kvg.at[slot], zk_s.at[d], zk_r.at[d], zp[d])

    def z_q(d):
        return remote_copy(
            send_q.at[zt[d]], qg.at[z], zq_s.at[d], zq_r.at[d], zp[d]
        )

    def own_x():
        return remote_copy(send_kv.at[z], kvg.at[c], f_s.at[3], f_r.at[3], xp)

    def fwd_x(d):
        slot = ((z + 3 - d) % 4) * 2 + x
        return remote_copy(kvg.at[slot], kvg.at[slot], f_s.at[d], f_r.at[d], xp)

    inputs = tok[...]
    for part in range(4):
        lanes = pl.ds(384 * part, 384)
        made = jnp.dot(inputs, wkv_v[:, lanes], preferred_element_type=jnp.float32)
        made = made + vec_v[part, 1:2, :].astype(jnp.float32)
        send_kv[part] = made.astype(jnp.bfloat16)
    own_x().start()
    for d in (1, 0, 2):
        z_kv(d).start()
    keep_kv = pltpu.make_async_copy(send_kv.at[z], kvg.at[c], l_sem.at[0])
    keep_kv.start()
    finish_recv(0)
    bias = lane_windows([vec_v[part, 0:1, 0:256].astype(jnp.float32) for part in range(4)])
    for part in range(4):
        lanes = pl.ds(window_start(part), 256)
        made = jnp.dot(inputs, wq_v[:, lanes], preferred_element_type=jnp.float32)
        made = made + bias[:, window_start(part) : window_start(part) + 256]
        send_q[part] = made.astype(jnp.bfloat16)
    for d in (1, 0, 2):
        z_q(d).start()
    keep_q = pltpu.make_async_copy(send_q.at[z], qg.at[z], l_sem.at[1])
    keep_q.start()
    outs = (
        pltpu.make_async_copy(wq_v, wq_o, out_sem.at[0]),
        pltpu.make_async_copy(wkv_v, wkv_o, out_sem.at[1]),
        pltpu.make_async_copy(vec_v, vec_o, out_sem.at[2]),
    )
    for item in outs:
        item.start()
    on_y(3, 0)
    z_kv_in(0).wait_recv()
    fwd_x(0).start()
    z_kv_in(2).wait_recv()
    fwd_x(2).start()
    z_kv_in(1).wait_recv()
    fwd_x(1).start()
    on_y(3, 1)
    on_y(2, 0)
    on_x(3, 0)
    on_x(3, 1)
    for j in range(4):
        on_y(4, j)
    for d in range(3):
        z_kv(d).wait_send()
        z_q(d).wait()
        fwd_x(d).wait()
    own_x().wait()
    keep_kv.wait()
    keep_q.wait()
    for u in (2, 3, 4):
        finish_recv(u)
    for u in range(5):
        finish_send(u)
    for i in range(3):
        vec(i, vec_peers[i]).wait_send()
    for item in outs:
        item.wait()


def any_specs(count):
    return [pl.BlockSpec(memory_space=pl.ANY)] * count


def vmem_specs(count):
    return [pl.BlockSpec(memory_space=pltpu.VMEM)] * count


def half(*shape):
    return jax.ShapeDtypeStruct(shape, jnp.bfloat16)


def full(*shape):
    return jax.ShapeDtypeStruct(shape, jnp.float32)


def gather_project(tok, wq, wkv, wo, win, wout, vec):
    rows, width = tok.shape
    d = pltpu.SemaphoreType.DMA
    count = sum(item[1] for item in GATHER_PIECES)
    return pl.pallas_call(
        gather_project_kernel,
        out_shape=[
            half(4, rows, 256),
            half(8, rows, 384),
            half(width, width),
            half(width, 2 * width),
            half(width, width),
            half(width, win.shape[1]),
            half(4 * wout.shape[0], width),
            half(4, 16, 384),
        ],
        in_specs=vmem_specs(1) + any_specs(6),
        out_specs=any_specs(8),
        scratch_shapes=[
            pltpu.VMEM((width, width), jnp.bfloat16),
            pltpu.VMEM((width, 2 * width), jnp.bfloat16),
            pltpu.VMEM((4, 16, 384), jnp.bfloat16),
            pltpu.VMEM((4, rows, 384), jnp.bfloat16),
            pltpu.VMEM((4, rows, 256), jnp.bfloat16),
            d((5,)),
            d((5,)),
            d((5,)),
        ]
        + [d((count,))] * 8
        + [d((3,)), d((3,)), d, d((3,)), d((3,)), d((3,)), d((3,)), d((4,)), d((4,)), d((2,)), d((3,))],
        compiler_params=pltpu.CompilerParams(
            collective_id=2, has_side_effects=True, vmem_limit_bytes=40 * 2**20
        ),
        cost_estimate=pl.CostEstimate(flops=10**9, bytes_accessed=10**8, transcendentals=0),
        name="gather_project",
    )(tok, wq, wkv, wo, win, wout, vec)


def pick(parity, value_side, by_window):
    shape = (384, 256) if not by_window else (256, 384)
    spread = lax.broadcasted_iota(jnp.int32, shape, 0 if not by_window else 1)
    window = lax.broadcasted_iota(jnp.int32, shape, 1 if not by_window else 0)
    lane = spread % 128
    low = 64 if value_side else 0
    target = (spread // 128) * 64 + (lane - low) + 64 * parity
    inside = (lane >= low) & (lane < low + 64)
    return jnp.where(inside & (target == window), 1.0, 0.0)


def dot_nt(left, right):
    return lax.dot_general(
        left, right, (((1,), (1,)), ((), ())), preferred_element_type=jnp.float32
    )


def attention_kernel(deal, lengths, qg, kvg, owin, osave, lse, kvn, kvt, qt):
    c = lax.axis_index("ctx")
    z = c // 2
    x = c % 2
    scale = HEAD_DIM ** (-0.5)
    span = 1024
    for b in range(16):
        natural = pl.multiple_of(deal[b] * BLOCK, BLOCK)
        for h in range(3):
            tile = kvg[b // 2, pl.ds((b % 2) * BLOCK, BLOCK), pl.ds(128 * h, 128)]
            kvn[h, pl.ds(natural, BLOCK), :] = tile
            kvt[h, :, pl.ds(natural, BLOCK)] = jnp.transpose(tile.astype(jnp.float32)).astype(
                jnp.bfloat16
            )
    spread = (pick(z % 2, False, False) * scale).astype(jnp.bfloat16)
    gather = pick(z % 2, True, False).astype(jnp.bfloat16)
    for part in range(4):
        qt[:, pl.ds(256 * part, 256)] = dot_nt(spread, qg[part]).astype(jnp.bfloat16)

    @pl.loop(0, 8)
    def _(b):
        dealt = ((b // 2) * 2 + x) * 2 + b % 2
        seq = deal[dealt] // 8
        start = pl.multiple_of(seq * span, span)
        length = lengths[seq]
        here = pl.ds(pl.multiple_of(b * BLOCK, BLOCK), BLOCK)
        rows = lax.broadcasted_iota(jnp.int32, (span, BLOCK), 0)
        made = []
        for h in range(3):
            scores = jnp.dot(
                kvn[h, pl.ds(start, span), :],
                qt[pl.ds(128 * h, 128), here],
                preferred_element_type=jnp.float32,
            )
            scores = jnp.where(rows < length, scores, NEG_FILL)
            top = jnp.max(scores, axis=0, keepdims=True)
            weights = jnp.exp(scores - top)
            total = jnp.sum(weights, axis=0, keepdims=True)
            mixed = jnp.dot(
                kvt[h, :, pl.ds(start, span)],
                weights.astype(jnp.bfloat16),
                preferred_element_type=jnp.float32,
            )
            mixed = mixed / total
            osave[h, b] = mixed[64:]
            lse[h, b] = jnp.broadcast_to(top + jnp.log(total), (8, BLOCK))
            made.append(jnp.transpose(mixed).astype(jnp.bfloat16))
        joined = jnp.concatenate(made, axis=1)
        owin[b // 2, pl.ds(pl.multiple_of((b % 2) * BLOCK, BLOCK), BLOCK), :] = jnp.dot(
            joined, gather, preferred_element_type=jnp.float32
        ).astype(jnp.bfloat16)


def attention_forward(deal, lengths, qg, kvg):
    smem = [pl.BlockSpec(memory_space=pltpu.SMEM)] * 2
    return pl.pallas_call(
        attention_kernel,
        out_shape=[
            half(4, 256, 256),
            full(3, 8, 64, BLOCK),
            full(3, 8, 8, BLOCK),
            half(3, 2048, 128),
            half(3, 128, 2048),
        ],
        in_specs=smem + vmem_specs(2),
        out_specs=vmem_specs(5),
        scratch_shapes=[pltpu.VMEM((384, 1024), jnp.bfloat16)],
        compiler_params=pltpu.CompilerParams(vmem_limit_bytes=40 * 2**20),
        cost_estimate=pl.CostEstimate(flops=2 * 10**9, bytes_accessed=10**7, transcendentals=3 * 10**6),
        name="attention_forward",
    )(deal, lengths, qg, kvg)


def attention_back_kernel(
    deal, lengths, qg, dog, osave, lse, kvn, kvt, dqwin, dkv, qt, dot_t, qd, acc
):
    c = lax.axis_index("ctx")
    z = c // 2
    x = c % 2
    scale = HEAD_DIM ** (-0.5)
    span = 1024
    spread_q = (pick(z % 2, False, False) * scale).astype(jnp.bfloat16)
    spread_o = pick(z % 2, True, False).astype(jnp.bfloat16)
    gather_q = pick(z % 2, False, False).astype(jnp.bfloat16)
    for part in range(4):
        lanes = pl.ds(256 * part, 256)
        qt[:, lanes] = dot_nt(spread_q, qg[part]).astype(jnp.bfloat16)
        dot_t[:, lanes] = dot_nt(spread_o, dog[part]).astype(jnp.bfloat16)
        q_rows = dot_nt(qg[part], spread_q).astype(jnp.bfloat16)
        o_rows = dot_nt(dog[part], spread_o).astype(jnp.bfloat16)
        for i in range(2):
            qd[2 * part + i, pl.ds(0, BLOCK), :] = q_rows[i * BLOCK : (i + 1) * BLOCK]
            qd[2 * part + i, pl.ds(BLOCK, BLOCK), :] = o_rows[i * BLOCK : (i + 1) * BLOCK]
    for h in range(3):
        acc[h] = jnp.zeros(acc.shape[1:], jnp.float32)

    @pl.loop(0, 8)
    def _(b):
        dealt = ((b // 2) * 2 + x) * 2 + b % 2
        seq = deal[dealt] // 8
        start = pl.multiple_of(seq * span, span)
        length = lengths[seq]
        here = pl.ds(pl.multiple_of(b * BLOCK, BLOCK), BLOCK)
        rows = lax.broadcasted_iota(jnp.int32, (span, BLOCK), 0)
        made = []
        for h in range(3):
            lanes = pl.ds(128 * h, 128)
            part = kvn[h, pl.ds(start, span), :]
            scores = jnp.dot(part, qt[lanes, here], preferred_element_type=jnp.float32)
            scores = jnp.where(rows < length, scores, NEG_FILL)
            probs = jnp.exp(scores - lse[h, b, 0:1, :])
            upstream = dot_t[lanes, here]
            grad_probs = jnp.dot(part, upstream, preferred_element_type=jnp.float32)
            delta = jnp.sum(
                osave[h, b] * upstream[64:].astype(jnp.float32), axis=0, keepdims=True
            )
            grad_scores = (probs * (grad_probs - delta)).astype(jnp.bfloat16)
            grad_query = jnp.dot(
                kvt[h, :, pl.ds(start, span)], grad_scores, preferred_element_type=jnp.float32
            )
            made.append((jnp.transpose(grad_query) * scale).astype(jnp.bfloat16))
            both = jnp.concatenate([grad_scores, probs.astype(jnp.bfloat16)], axis=1)
            acc[h, pl.ds(start, span), :] += jnp.dot(
                both, qd[b, :, lanes], preferred_element_type=jnp.float32
            )
        joined = jnp.concatenate(made, axis=1)
        dqwin[b // 2, pl.ds(pl.multiple_of((b % 2) * BLOCK, BLOCK), BLOCK), :] = jnp.dot(
            joined, gather_q, preferred_element_type=jnp.float32
        ).astype(jnp.bfloat16)

    for b in range(16):
        natural = pl.multiple_of(deal[b] * BLOCK, BLOCK)
        for h in range(3):
            dkv[b // 2, pl.ds((b % 2) * BLOCK, BLOCK), pl.ds(128 * h, 128)] = acc[
                h, pl.ds(natural, BLOCK), :
            ].astype(jnp.bfloat16)


def attention_backward(deal, lengths, qg, dog, osave, lse, kvn, kvt):
    smem = [pl.BlockSpec(memory_space=pltpu.SMEM)] * 2
    return pl.pallas_call(
        attention_back_kernel,
        out_shape=[half(4, 256, 256), half(8, 256, 384)],
        in_specs=smem + vmem_specs(6),
        out_specs=vmem_specs(2),
        scratch_shapes=[
            pltpu.VMEM((384, 1024), jnp.bfloat16),
            pltpu.VMEM((384, 1024), jnp.bfloat16),
            pltpu.VMEM((8, 256, 384), jnp.bfloat16),
            pltpu.VMEM((3, 2048, 128), jnp.float32),
        ],
        compiler_params=pltpu.CompilerParams(vmem_limit_bytes=40 * 2**20),
        cost_estimate=pl.CostEstimate(flops=5 * 10**9, bytes_accessed=10**7, transcendentals=3 * 10**6),
        name="attention_backward",
    )(deal, lengths, qg, dog, osave, lse, kvn, kvt)


def heads_home_kernel(win, out, got, send, recv, local):
    c, f, z, x, y, k = places()
    zt = [(z + d) % 4 for d in (1, 2, 3)]
    zp = [(item * 2 + x, f) for item in zt]
    greet(zp)
    copies = [
        remote_copy(win.at[zt[d]], got.at[z], send.at[d], recv.at[d], zp[d]) for d in range(3)
    ]
    for d in (1, 0, 2):
        copies[d].start()
    keep = pltpu.make_async_copy(win.at[z], got.at[z], local)
    keep.start()
    keep.wait()
    for item in copies:
        item.wait()
    out[...] = lane_windows([got[part] for part in range(4)])


def heads_home(win):
    d = pltpu.SemaphoreType.DMA
    return pl.pallas_call(
        heads_home_kernel,
        out_shape=half(256, 768),
        in_specs=vmem_specs(1),
        out_specs=pl.BlockSpec(memory_space=pltpu.VMEM),
        scratch_shapes=[pltpu.VMEM((4, 256, 256), jnp.bfloat16), d((3,)), d((3,)), d],
        compiler_params=pltpu.CompilerParams(collective_id=3, has_side_effects=True, vmem_limit_bytes=16 * 2**20),
        cost_estimate=pl.CostEstimate(flops=10**6, bytes_accessed=10**7, transcendentals=0),
        name="heads_home",
    )(win)


def heads_away_kernel(rows, out, send, recv, local):
    c, f, z, x, y, k = places()
    zt = [(z + d) % 4 for d in (1, 2, 3)]
    zp = [(item * 2 + x, f) for item in zt]
    greet(zp)

    def lanes(part):
        return pl.ds(pl.multiple_of(window_start(part), 128), 256)

    copies = [
        remote_copy(rows.at[:, lanes(zt[d])], out.at[z], send.at[d], recv.at[d], zp[d])
        for d in range(3)
    ]
    for d in (1, 0, 2):
        copies[d].start()
    keep = pltpu.make_async_copy(rows.at[:, lanes(z)], out.at[z], local)
    keep.start()
    keep.wait()
    for item in copies:
        item.wait()


def heads_away(rows):
    d = pltpu.SemaphoreType.DMA
    return pl.pallas_call(
        heads_away_kernel,
        out_shape=half(4, 256, 256),
        in_specs=vmem_specs(1),
        out_specs=pl.BlockSpec(memory_space=pltpu.VMEM),
        scratch_shapes=[d((3,)), d((3,)), d],
        compiler_params=pltpu.CompilerParams(collective_id=4, has_side_effects=True, vmem_limit_bytes=16 * 2**20),
        cost_estimate=pl.CostEstimate(flops=10**6, bytes_accessed=10**7, transcendentals=0),
        name="heads_away",
    )(rows)


def grads_home_kernel(dqwin, dkv, dq, dkv_out, got_q, theirs, mine, got_kv, q_s, q_r, x_s, x_r, k_s, k_r, l_q, l_k, l_own):
    c, f, z, x, y, k = places()
    zt = [(z + d) % 4 for d in (1, 2, 3)]
    zp = [(item * 2 + x, f) for item in zt]
    xp = (z * 2 + (1 - x), f)
    greet([xp] + zp)

    def over_x(i, part):
        return remote_copy(dkv.at[part * 2 + (1 - x)], theirs.at[i], x_s.at[i], x_r.at[i], xp)

    order = [zt[1], zt[0], zt[2], z]
    where = [1, 0, 2]
    for i in range(4):
        over_x(i, order[i]).start()
        pltpu.make_async_copy(dkv.at[order[i] * 2 + x], mine.at[i], l_k.at[i]).start()

    def q_copy(d):
        return remote_copy(dqwin.at[zt[d]], got_q.at[z], q_s.at[d], q_r.at[d], zp[d])

    for d in (1, 0, 2):
        q_copy(d).start()
    keep_q = pltpu.make_async_copy(dqwin.at[z], got_q.at[z], l_q)
    keep_q.start()

    def kv_copy(i):
        d = where[i]
        return remote_copy(mine.at[i], got_kv.at[z], k_s.at[d], k_r.at[d], zp[d])

    for i in range(4):
        over_x(i, order[i]).wait_recv()
        pltpu.make_async_copy(dkv.at[order[i] * 2 + x], mine.at[i], l_k.at[i]).wait()

        @pl.loop(0, 16)
        def _(j, i=i):
            rows = pl.ds(pl.multiple_of(j * 16, 16), 16)
            mine[i, rows] = (
                mine[i, rows].astype(jnp.float32) + theirs[i, rows].astype(jnp.float32)
            ).astype(jnp.bfloat16)

        if i < 3:
            kv_copy(i).start()
    own = pltpu.make_async_copy(mine.at[3], got_kv.at[z], l_own)
    own.start()
    keep_q.wait()
    for d in range(3):
        q_copy(d).wait()
    dq[...] = lane_windows([got_q[part] for part in range(4)])
    own.wait()
    for i in range(3):
        kv_copy(i).wait()
    for part in range(4):
        dkv_out[:, pl.ds(384 * part, 384)] = got_kv[part]
    for i in range(4):
        over_x(i, order[i]).wait_send()


def grads_home(dqwin, dkv):
    d = pltpu.SemaphoreType.DMA
    return pl.pallas_call(
        grads_home_kernel,
        out_shape=[half(256, 768), half(256, 1536)],
        in_specs=vmem_specs(2),
        out_specs=vmem_specs(2),
        scratch_shapes=[
            pltpu.VMEM((4, 256, 256), jnp.bfloat16),
            pltpu.VMEM((4, 256, 384), jnp.bfloat16),
            pltpu.VMEM((4, 256, 384), jnp.bfloat16),
            pltpu.VMEM((4, 256, 384), jnp.bfloat16),
            d((3,)),
            d((3,)),
            d((4,)),
            d((4,)),
            d((3,)),
            d((3,)),
            d,
            d((4,)),
            d,
        ],
        compiler_params=pltpu.CompilerParams(collective_id=5, has_side_effects=True, vmem_limit_bytes=24 * 2**20),
        cost_estimate=pl.CostEstimate(flops=10**7, bytes_accessed=5 * 10**7, transcendentals=0),
        name="grads_home",
    )(dqwin, dkv)


def reduce_grads(grads):
    chunks = []
    for m, item in enumerate(grads):
        shard = item.shape[0] // 4
        high = min(shard, 192)
        wide = min(item.shape[1], 768)
        for i in range(shard // high):
            for j in range(item.shape[1] // wide):

                def slab(ref, f, i=i, j=j, shard=shard, high=high, wide=wide):
                    rows = pl.ds(pl.multiple_of(f * shard + i * high, high), high)
                    return ref.at[rows, pl.ds(j * wide, wide)]

                def home(ref, xx, i=i, j=j, high=high, wide=wide):
                    lanes = pl.ds(pl.multiple_of(j * wide + xx * (wide // 2), 128), wide // 2)
                    return ref.at[pl.ds(i * high, high), lanes]

                chunks.append((m, slab, m, home, high, wide))
    n = len(chunks)
    count = len(grads)
    scratch = []
    for lead, divide_rows, divide_lanes in (
        ((2,), 1, 1),
        ((2,), 1, 1),
        ((), 1, 1),
        ((), 1, 2),
        ((), 1, 2),
        ((3,), 4, 2),
        ((2,), 1, 2),
    ):
        for item in chunks:
            shape = lead + (item[4] // divide_rows, item[5] // divide_lanes)
            scratch.append(pltpu.VMEM(shape, jnp.bfloat16))
    d = pltpu.SemaphoreType.DMA
    for lanes in (2, 2, 2, 2, 1, 1, 1, 1, 3, 3, 3, 3, 1, 1):
        scratch.append(d((n, lanes)) if lanes > 1 else d((n,)))
    return pl.pallas_call(
        functools.partial(reduce_kernel, chunks, count, count),
        out_shape=[half(item.shape[0] // 4, item.shape[1]) for item in grads],
        in_specs=any_specs(count),
        out_specs=any_specs(count),
        scratch_shapes=scratch,
        compiler_params=pltpu.CompilerParams(
            collective_id=1, has_side_effects=True, vmem_limit_bytes=48 * 2**20
        ),
        cost_estimate=pl.CostEstimate(flops=10**7, bytes_accessed=10**8, transcendentals=0),
        name="grad_reduce",
    )(*grads)


def body_fast(
    tokens,
    seq_lengths,
    deal,
    w_query,
    w_key,
    w_value,
    w_attn_out,
    b_query,
    b_value,
    b_attn_out,
    norm1_gain,
    norm1_bias,
    w_in,
    b_in,
    w_out,
    b_out,
    norm2_gain,
    norm2_bias,
    cotangent,
):
    inputs = tokens[0]
    width = inputs.shape[1]
    part = width // 4
    odd = lax.axis_index("fsdp") % 2 == 1
    pair_shape = (part, HEADS, HEAD_DIM)
    pair_weight = jnp.stack(
        [to_half(w_key).reshape(pair_shape), to_half(w_value).reshape(pair_shape)], axis=2
    ).reshape(part, 2 * width)
    query_row = jnp.where(
        odd, jnp.pad(b_query, (HEAD_DIM, 384 - 256)), jnp.pad(b_query, (0, 384 - 192))
    )
    value_heads = b_value.reshape(3, HEAD_DIM)
    pair_row = jnp.stack([jnp.zeros_like(value_heads), value_heads], axis=1).reshape(384)
    small = [query_row, pair_row]
    for item in (b_attn_out, norm1_gain, norm1_bias, b_out, norm2_gain, norm2_bias):
        small.append(jnp.pad(item, (0, 384 - part)))
    packed = jnp.concatenate(
        [jnp.stack(small), b_in.reshape(2, 384), jnp.zeros((6, 384), jnp.float32)], axis=0
    )
    (
        query_groups,
        pair_groups,
        query_weight,
        pair_weights,
        mix_weight,
        inner_weight,
        outer_weight,
        vectors,
    ) = gather_project(
        inputs,
        to_half(w_query),
        pair_weight,
        to_half(w_attn_out),
        to_half(w_in),
        to_half(w_out),
        to_half(packed),
    )
    vectors = vectors.astype(jnp.float32)
    mix_bias, gain_one, shift_one, outer_bias, gain_two, shift_two = (
        vectors[:, 2 + i, :part].reshape(width) for i in range(6)
    )
    inner_bias = vectors[:, 8:10, :].reshape(4 * width)
    deal_row = deal[0]
    lengths = seq_lengths[0]
    out_windows, out_heads, log_totals, pairs, pairs_turned = attention_forward(
        deal_row, lengths, query_groups, pair_groups
    )
    attn_in = heads_home(out_windows)
    residual_one = (
        inputs.astype(jnp.float32)
        + jnp.dot(attn_in, mix_weight, preferred_element_type=jnp.float32)
        + mix_bias
    )
    normal_one, normed_one, inverse_one = norm_forward(residual_one, gain_one, shift_one)
    normal_half = normal_one.astype(jnp.bfloat16)
    pre_act = jnp.dot(normal_half, inner_weight, preferred_element_type=jnp.float32) + inner_bias
    activated, gelu_pull = jax.vjp(exact_gelu, pre_act)
    hidden = activated.astype(jnp.bfloat16)
    residual_two = (
        normal_one
        + jnp.dot(hidden, outer_weight, preferred_element_type=jnp.float32)
        + outer_bias
    )
    layer_out, normed_two, inverse_two = norm_forward(residual_two, gain_two, shift_two)
    upstream = cotangent[0].astype(jnp.float32)
    grad_two, grad_gain_two, grad_shift_two = norm_backward(
        upstream, gain_two, normed_two, inverse_two
    )
    grad_branch = grad_two.astype(jnp.bfloat16)
    grad_outer_bias = jnp.sum(grad_branch.astype(jnp.float32), axis=0)
    grad_outer = jnp.einsum("tf,td->fd", hidden, grad_branch, preferred_element_type=jnp.float32)
    grad_hidden = jnp.einsum(
        "td,fd->tf", grad_branch, outer_weight, preferred_element_type=jnp.float32
    )
    grad_pre = gelu_pull(grad_hidden)[0].astype(jnp.bfloat16)
    grad_inner_bias = jnp.sum(grad_pre.astype(jnp.float32), axis=0)
    grad_inner = jnp.einsum("td,tf->df", normal_half, grad_pre, preferred_element_type=jnp.float32)
    grad_normal = grad_two + jnp.einsum(
        "tf,df->td", grad_pre, inner_weight, preferred_element_type=jnp.float32
    )
    grad_one, grad_gain_one, grad_shift_one = norm_backward(
        grad_normal, gain_one, normed_one, inverse_one
    )
    grad_attn = grad_one.astype(jnp.bfloat16)
    grad_mix_bias = jnp.sum(grad_attn.astype(jnp.float32), axis=0)
    grad_mix = jnp.einsum("td,te->de", attn_in, grad_attn, preferred_element_type=jnp.float32)
    grad_mixed = jnp.einsum(
        "te,de->td", grad_attn, mix_weight, preferred_element_type=jnp.float32
    ).astype(jnp.bfloat16)
    grad_groups = heads_away(grad_mixed)
    query_back, pairs_back = attention_backward(
        deal_row,
        lengths,
        query_groups,
        grad_groups,
        out_heads,
        log_totals,
        pairs,
        pairs_turned,
    )
    grad_query, grad_pairs = grads_home(query_back, pairs_back)
    grad_query_weight = jnp.einsum(
        "td,te->de", inputs, grad_query, preferred_element_type=jnp.float32
    )
    grad_pair_weight = jnp.einsum(
        "td,te->de", inputs, grad_pairs, preferred_element_type=jnp.float32
    )
    grad_query_bias = jnp.sum(grad_query.astype(jnp.float32), axis=0)
    grad_pair_bias = jnp.sum(grad_pairs.astype(jnp.float32), axis=0)
    grad_value_bias = grad_pair_bias.reshape(HEADS, 2, HEAD_DIM)[:, 1, :].reshape(width)
    grad_inputs = (
        grad_one
        + jnp.einsum("te,de->td", grad_query, query_weight, preferred_element_type=jnp.float32)
        + jnp.einsum("te,de->td", grad_pairs, pair_weights, preferred_element_type=jnp.float32)
    )
    rows = jnp.stack(
        [
            grad_query_bias,
            grad_value_bias,
            grad_mix_bias,
            grad_gain_one,
            grad_shift_one,
            grad_outer_bias,
            grad_gain_two,
            grad_shift_two,
        ]
    )
    shares = jnp.transpose(rows.reshape(8, 4, part), (1, 0, 2)).reshape(4, 2 * width)
    shares = jnp.concatenate([shares, grad_inner_bias.reshape(4, width)], axis=1)
    shares = jnp.pad(shares, ((0, 0), (0, 64 * 256 - 3 * width))).reshape(256, 256)
    (
        sum_query,
        sum_pairs,
        sum_mix,
        sum_inner,
        sum_outer,
        sum_small,
    ) = reduce_grads(
        [
            to_half(grad_query_weight),
            to_half(grad_pair_weight),
            to_half(grad_mix),
            to_half(grad_inner),
            to_half(grad_outer),
            to_half(shares),
        ]
    )
    sum_pairs = sum_pairs.astype(jnp.float32).reshape(part, HEADS, 2, HEAD_DIM)
    flat = sum_small.astype(jnp.float32).reshape(-1)[: 3 * width]
    small = flat[: 2 * width].reshape(8, part)
    return (
        layer_out.astype(jnp.bfloat16)[None],
        grad_inputs[None],
        sum_query.astype(jnp.float32),
        sum_pairs[:, :, 0, :].reshape(part, width),
        sum_pairs[:, :, 1, :].reshape(part, width),
        sum_mix.astype(jnp.float32),
        small[0],
        small[1],
        small[2],
        small[3],
        small[4],
        sum_inner.astype(jnp.float32),
        flat[2 * width :],
        sum_outer.astype(jnp.float32),
        small[5],
        small[6],
        small[7],
    )


def solution(mesh):
    placed = (
        P("fsdp", "ctx", None),
        P("fsdp", None),
        P("fsdp", None),
        P("fsdp", None),
        P("fsdp", None),
        P("fsdp", None),
        P("fsdp", None),
        P("fsdp"),
        P("fsdp"),
        P("fsdp"),
        P("fsdp"),
        P("fsdp"),
        P("fsdp", None),
        P("fsdp"),
        P("fsdp", None),
        P("fsdp"),
        P("fsdp"),
        P("fsdp"),
        P("fsdp", "ctx", None),
    )
    fast = dict(mesh.shape) == {"ctx": 8, "fsdp": 4}
    return jax.shard_map(
        body_fast if fast else body,
        mesh=mesh,
        in_specs=placed,
        out_specs=(
            P("fsdp", "ctx", None),
            P("fsdp", "ctx", None),
            P("fsdp", None),
            P("fsdp", None),
            P("fsdp", None),
            P("fsdp", None),
            P("fsdp"),
            P("fsdp"),
            P("fsdp"),
            P("fsdp"),
            P("fsdp"),
            P("fsdp", None),
            P("fsdp"),
            P("fsdp", None),
            P("fsdp"),
            P("fsdp"),
            P("fsdp"),
        ),
        check_vma=False,
    )
```

```python
import functools

import jax
import jax.numpy as jnp
from jax import lax
from jax.experimental import pallas as pl
from jax.experimental.pallas import tpu as pltpu
from jax.sharding import PartitionSpec as P

HEADS = 12
HEAD_DIM = 64
BLOCK = 128


EPSILON = 1e-12
NEG_FILL = -1e30


def block_codes(lengths, deal_row):
    padded = (lengths + BLOCK - 1) // BLOCK * BLOCK
    seq_ends = jnp.cumsum(padded)
    offsets = jnp.tile(jnp.arange(BLOCK, dtype=jnp.int32), deal_row.shape[0])
    natural = jnp.repeat(deal_row * BLOCK, BLOCK) + offsets
    passed = (natural[:, None] >= seq_ends[None, :]).astype(jnp.int32)
    seq_ids = jnp.sum(passed, axis=1)
    begins = jnp.sum(passed * padded[None, :], axis=1)
    owners = (seq_ids[:, None] == jnp.arange(lengths.shape[0], dtype=jnp.int32)[None, :]).astype(
        jnp.int32
    )
    own_length = jnp.sum(owners * lengths[None, :], axis=1)
    key_codes = jnp.where(natural - begins < own_length, seq_ids, -1)
    return (seq_ids, key_codes)


def to_half(value):
    return value.astype(jnp.bfloat16)


def exact_gelu(value):
    return jax.nn.gelu(value, approximate=False)


def split_heads(matrix):
    return matrix.reshape(matrix.shape[0], HEADS, HEAD_DIM)


def sub_width(rows):
    width = rows
    while width > 1024 and width % 2 == 0:
        width = width // 2
    return width


def add_rows(total, term, at_row):
    current = lax.dynamic_slice_in_dim(total, at_row, term.shape[0])
    return lax.dynamic_update_slice_in_dim(total, current + term, at_row, 0)


def norm_forward(residual, gain, shift):
    centre = residual - jnp.mean(residual, axis=-1, keepdims=True)
    spread = jnp.mean(centre * centre, axis=-1, keepdims=True)
    inverse = lax.rsqrt(spread + EPSILON)
    normed = centre * inverse
    return (normed * gain + shift, normed, inverse)


def norm_backward(upstream, gain, normed, inverse):
    scaled = upstream * gain
    across = jnp.mean(scaled, axis=-1, keepdims=True)
    along = jnp.mean(scaled * normed, axis=-1, keepdims=True)
    grad_residual = inverse * (scaled - across - normed * along)
    return (grad_residual, jnp.sum(upstream * normed, axis=0), jnp.sum(upstream, axis=0))


def score_grads(
    query_heads, grad_heads, key_part, value_part, query_ids, code_part, log_totals, delta, scale
):
    scores = (
        jnp.einsum("qhd,khd->hqk", query_heads, key_part, preferred_element_type=jnp.float32)
        * scale
    )
    scores = jnp.where((query_ids[:, None] == code_part[None, :])[None], scores, NEG_FILL)
    probs = jnp.exp(scores - log_totals[:, :, None])
    grad_probs = jnp.einsum(
        "qhd,khd->hqk", grad_heads, value_part, preferred_element_type=jnp.float32
    )
    grad_scores = (probs * (grad_probs - delta[:, :, None])).astype(jnp.bfloat16)
    return (probs, grad_scores)


def attend_forward(query_heads, query_ids, key_codes_all, scale, carry, piece):
    keys, values = piece
    rows = keys.shape[0]
    width = sub_width(rows)

    def one_block(state, offset):
        running, totals, accum = state
        key_part = split_heads(lax.dynamic_slice_in_dim(keys, offset, width))
        value_part = split_heads(lax.dynamic_slice_in_dim(values, offset, width))
        code_part = lax.dynamic_slice_in_dim(key_codes_all, offset, width)
        scores = (
            jnp.einsum("qhd,khd->hqk", query_heads, key_part, preferred_element_type=jnp.float32)
            * scale
        )
        scores = jnp.where((query_ids[:, None] == code_part[None, :])[None], scores, NEG_FILL)
        newest = jnp.maximum(running, jnp.max(scores, axis=-1))
        factor = jnp.exp(running - newest)
        weights = jnp.exp(scores - newest[:, :, None])
        totals = totals * factor + jnp.sum(weights, axis=-1)
        mixed = jnp.einsum(
            "hqk,khd->qhd",
            weights.astype(jnp.bfloat16),
            value_part,
            preferred_element_type=jnp.float32,
        )
        accum = accum * jnp.transpose(factor)[:, :, None] + mixed
        return ((newest, totals, accum), None)

    carry, unused = lax.scan(one_block, carry, jnp.arange(rows // width, dtype=jnp.int32) * width)
    return carry


def attend_back(
    query_heads, grad_heads, query_ids, key_codes_all, log_totals, delta, scale, carry, piece
):
    keys, values = piece
    rows = keys.shape[0]
    width = sub_width(rows)

    def one_block(state, offset):
        grad_query, grad_keys_all, grad_values_all = state
        key_part = split_heads(lax.dynamic_slice_in_dim(keys, offset, width))
        value_part = split_heads(lax.dynamic_slice_in_dim(values, offset, width))
        code_part = lax.dynamic_slice_in_dim(key_codes_all, offset, width)
        probs, grad_scores = score_grads(
            query_heads,
            grad_heads,
            key_part,
            value_part,
            query_ids,
            code_part,
            log_totals,
            delta,
            scale,
        )
        grad_query = (
            grad_query
            + jnp.einsum("hqk,khd->qhd", grad_scores, key_part, preferred_element_type=jnp.float32)
            * scale
        )
        key_term = (
            jnp.einsum("hqk,qhd->khd", grad_scores, query_heads, preferred_element_type=jnp.float32)
            * scale
        )
        value_term = jnp.einsum(
            "hqk,qhd->khd",
            probs.astype(jnp.bfloat16),
            grad_heads,
            preferred_element_type=jnp.float32,
        )
        grad_keys_all = add_rows(grad_keys_all, key_term.reshape(width, HEADS * HEAD_DIM), offset)
        grad_values_all = add_rows(
            grad_values_all, value_term.reshape(width, HEADS * HEAD_DIM), offset
        )
        return ((grad_query, grad_keys_all, grad_values_all), None)

    carry, unused = lax.scan(one_block, carry, jnp.arange(rows // width, dtype=jnp.int32) * width)
    return carry


def body(
    tokens,
    seq_lengths,
    deal,
    w_query,
    w_key,
    w_value,
    w_attn_out,
    b_query,
    b_value,
    b_attn_out,
    norm1_gain,
    norm1_bias,
    w_in,
    b_in,
    w_out,
    b_out,
    norm2_gain,
    norm2_bias,
    cotangent,
):
    gathered = (
        lax.all_gather(to_half(w_query), "fsdp", axis=0, tiled=True),
        lax.all_gather(to_half(w_key), "fsdp", axis=0, tiled=True),
        lax.all_gather(to_half(w_value), "fsdp", axis=0, tiled=True),
        lax.all_gather(to_half(w_attn_out), "fsdp", axis=0, tiled=True),
        lax.all_gather(to_half(b_query), "fsdp", axis=0, tiled=True),
        lax.all_gather(to_half(b_value), "fsdp", axis=0, tiled=True),
        lax.all_gather(to_half(b_attn_out), "fsdp", axis=0, tiled=True),
        lax.all_gather(to_half(norm1_gain), "fsdp", axis=0, tiled=True),
        lax.all_gather(to_half(norm1_bias), "fsdp", axis=0, tiled=True),
        lax.all_gather(to_half(w_in), "fsdp", axis=0, tiled=True),
        lax.all_gather(to_half(b_in), "fsdp", axis=0, tiled=True),
        lax.all_gather(to_half(w_out), "fsdp", axis=0, tiled=True),
        lax.all_gather(to_half(b_out), "fsdp", axis=0, tiled=True),
        lax.all_gather(to_half(norm2_gain), "fsdp", axis=0, tiled=True),
        lax.all_gather(to_half(norm2_bias), "fsdp", axis=0, tiled=True),
    )
    (
        query_weight,
        key_weight,
        value_weight,
        mix_weight,
        query_bias,
        value_bias,
        mix_bias,
        gain_one,
        shift_one,
        inner_weight,
        inner_bias,
        outer_weight,
        outer_bias,
        gain_two,
        shift_two,
    ) = gathered
    scale = HEAD_DIM ** (-0.5)
    inputs = tokens[0]
    rows = inputs.shape[0]
    query_ids_all, key_codes_all = block_codes(seq_lengths[0], deal[0])
    first_row = lax.axis_index("ctx") * rows
    query_ids = lax.dynamic_slice_in_dim(query_ids_all, first_row, rows)
    query = (
        jnp.dot(inputs, query_weight, preferred_element_type=jnp.float32)
        + query_bias.astype(jnp.float32)
    ).astype(jnp.bfloat16)
    keys = jnp.dot(inputs, key_weight, preferred_element_type=jnp.float32).astype(jnp.bfloat16)
    values = (
        jnp.dot(inputs, value_weight, preferred_element_type=jnp.float32)
        + value_bias.astype(jnp.float32)
    ).astype(jnp.bfloat16)
    query_heads = split_heads(query)
    start_state = (
        jnp.full((HEADS, rows), NEG_FILL, jnp.float32),
        jnp.zeros((HEADS, rows), jnp.float32),
        jnp.zeros((rows, HEADS, HEAD_DIM), jnp.float32),
    )
    running, totals, accum = attend_forward(
        query_heads,
        query_ids,
        key_codes_all,
        scale,
        start_state,
        (
            lax.all_gather(keys, "ctx", axis=0, tiled=True),
            lax.all_gather(values, "ctx", axis=0, tiled=True),
        ),
    )
    out_heads = accum / jnp.transpose(totals)[:, :, None]
    log_totals = running + jnp.log(totals)
    attn_in = out_heads.reshape(rows, HEADS * HEAD_DIM).astype(jnp.bfloat16)
    residual_one = (
        inputs.astype(jnp.float32)
        + jnp.dot(attn_in, mix_weight, preferred_element_type=jnp.float32)
        + mix_bias.astype(jnp.float32)
    )
    normal_one, normed_one, inverse_one = norm_forward(
        residual_one, gain_one.astype(jnp.float32), shift_one.astype(jnp.float32)
    )
    normal_half = normal_one.astype(jnp.bfloat16)
    pre_act = jnp.dot(
        normal_half, inner_weight, preferred_element_type=jnp.float32
    ) + inner_bias.astype(jnp.float32)
    activated, gelu_pull = jax.vjp(exact_gelu, pre_act)
    hidden = activated.astype(jnp.bfloat16)
    residual_two = (
        normal_one
        + jnp.dot(hidden, outer_weight, preferred_element_type=jnp.float32)
        + outer_bias.astype(jnp.float32)
    )
    layer_out, normed_two, inverse_two = norm_forward(
        residual_two, gain_two.astype(jnp.float32), shift_two.astype(jnp.float32)
    )
    upstream = cotangent[0].astype(jnp.float32)
    grad_two, grad_gain_two, grad_shift_two = norm_backward(
        upstream, gain_two.astype(jnp.float32), normed_two, inverse_two
    )
    grad_branch = grad_two.astype(jnp.bfloat16)
    grad_outer_bias = jnp.sum(grad_branch.astype(jnp.float32), axis=0)
    grad_outer = jnp.einsum("tf,td->fd", hidden, grad_branch, preferred_element_type=jnp.float32)
    grad_hidden = jnp.einsum(
        "td,fd->tf", grad_branch, outer_weight, preferred_element_type=jnp.float32
    )
    grad_pre = gelu_pull(grad_hidden)[0].astype(jnp.bfloat16)
    grad_inner_bias = jnp.sum(grad_pre.astype(jnp.float32), axis=0)
    grad_inner = jnp.einsum("td,tf->df", normal_half, grad_pre, preferred_element_type=jnp.float32)
    grad_normal = grad_two + jnp.einsum(
        "tf,df->td", grad_pre, inner_weight, preferred_element_type=jnp.float32
    )
    grad_one, grad_gain_one, grad_shift_one = norm_backward(
        grad_normal, gain_one.astype(jnp.float32), normed_one, inverse_one
    )
    grad_attn = grad_one.astype(jnp.bfloat16)
    grad_mix_bias = jnp.sum(grad_attn.astype(jnp.float32), axis=0)
    grad_mix = jnp.einsum("td,te->de", attn_in, grad_attn, preferred_element_type=jnp.float32)
    grad_mixed = jnp.einsum(
        "te,de->td", grad_attn, mix_weight, preferred_element_type=jnp.float32
    ).astype(jnp.bfloat16)
    grad_heads = split_heads(grad_mixed)
    delta = jnp.einsum("qhd,qhd->hq", grad_heads.astype(jnp.float32), out_heads)
    group_rows = key_codes_all.shape[0]
    start_back = (
        jnp.zeros((rows, HEADS, HEAD_DIM), jnp.float32),
        jnp.zeros((group_rows, HEADS * HEAD_DIM), jnp.float32),
        jnp.zeros((group_rows, HEADS * HEAD_DIM), jnp.float32),
    )
    grad_query_heads, grad_keys_all, grad_values_all = attend_back(
        query_heads,
        grad_heads,
        query_ids,
        key_codes_all,
        log_totals,
        delta,
        scale,
        start_back,
        (
            lax.all_gather(keys, "ctx", axis=0, tiled=True),
            lax.all_gather(values, "ctx", axis=0, tiled=True),
        ),
    )
    grad_keys_flat, grad_values_flat = (
        lax.psum_scatter(
            grad_keys_all.astype(jnp.bfloat16), "ctx", scatter_dimension=0, tiled=True
        ).astype(jnp.float32),
        lax.psum_scatter(
            grad_values_all.astype(jnp.bfloat16), "ctx", scatter_dimension=0, tiled=True
        ).astype(jnp.float32),
    )
    grad_query_half = grad_query_heads.reshape(rows, HEADS * HEAD_DIM).astype(jnp.bfloat16)
    grad_keys_half = grad_keys_flat.astype(jnp.bfloat16)
    grad_values_half = grad_values_flat.astype(jnp.bfloat16)
    grad_query_weight = jnp.einsum(
        "td,te->de", inputs, grad_query_half, preferred_element_type=jnp.float32
    )
    grad_key_weight = jnp.einsum(
        "td,te->de", inputs, grad_keys_half, preferred_element_type=jnp.float32
    )
    grad_value_weight = jnp.einsum(
        "td,te->de", inputs, grad_values_half, preferred_element_type=jnp.float32
    )
    grad_query_bias = jnp.sum(grad_query_half.astype(jnp.float32), axis=0)
    grad_value_bias = jnp.sum(grad_values_half.astype(jnp.float32), axis=0)
    grad_inputs = (
        grad_one
        + jnp.einsum("te,de->td", grad_query_half, query_weight, preferred_element_type=jnp.float32)
        + jnp.einsum("te,de->td", grad_keys_half, key_weight, preferred_element_type=jnp.float32)
        + jnp.einsum(
            "te,de->td", grad_values_half, value_weight, preferred_element_type=jnp.float32
        )
    )
    shares = (
        lax.psum_scatter(
            grad_query_weight.astype(jnp.bfloat16), "fsdp", scatter_dimension=0, tiled=True
        ).astype(jnp.float32),
        lax.psum_scatter(
            grad_key_weight.astype(jnp.bfloat16), "fsdp", scatter_dimension=0, tiled=True
        ).astype(jnp.float32),
        lax.psum_scatter(
            grad_value_weight.astype(jnp.bfloat16), "fsdp", scatter_dimension=0, tiled=True
        ).astype(jnp.float32),
        lax.psum_scatter(
            grad_mix.astype(jnp.bfloat16), "fsdp", scatter_dimension=0, tiled=True
        ).astype(jnp.float32),
        lax.psum_scatter(
            grad_query_bias.astype(jnp.bfloat16), "fsdp", scatter_dimension=0, tiled=True
        ).astype(jnp.float32),
        lax.psum_scatter(
            grad_value_bias.astype(jnp.bfloat16), "fsdp", scatter_dimension=0, tiled=True
        ).astype(jnp.float32),
        lax.psum_scatter(
            grad_mix_bias.astype(jnp.bfloat16), "fsdp", scatter_dimension=0, tiled=True
        ).astype(jnp.float32),
        lax.psum_scatter(
            grad_gain_one.astype(jnp.bfloat16), "fsdp", scatter_dimension=0, tiled=True
        ).astype(jnp.float32),
        lax.psum_scatter(
            grad_shift_one.astype(jnp.bfloat16), "fsdp", scatter_dimension=0, tiled=True
        ).astype(jnp.float32),
        lax.psum_scatter(
            grad_inner.astype(jnp.bfloat16), "fsdp", scatter_dimension=0, tiled=True
        ).astype(jnp.float32),
        lax.psum_scatter(
            grad_inner_bias.astype(jnp.bfloat16), "fsdp", scatter_dimension=0, tiled=True
        ).astype(jnp.float32),
        lax.psum_scatter(
            grad_outer.astype(jnp.bfloat16), "fsdp", scatter_dimension=0, tiled=True
        ).astype(jnp.float32),
        lax.psum_scatter(
            grad_outer_bias.astype(jnp.bfloat16), "fsdp", scatter_dimension=0, tiled=True
        ).astype(jnp.float32),
        lax.psum_scatter(
            grad_gain_two.astype(jnp.bfloat16), "fsdp", scatter_dimension=0, tiled=True
        ).astype(jnp.float32),
        lax.psum_scatter(
            grad_shift_two.astype(jnp.bfloat16), "fsdp", scatter_dimension=0, tiled=True
        ).astype(jnp.float32),
    )
    summed = (
        lax.psum(shares[0].astype(jnp.bfloat16), "ctx").astype(jnp.float32),
        lax.psum(shares[1].astype(jnp.bfloat16), "ctx").astype(jnp.float32),
        lax.psum(shares[2].astype(jnp.bfloat16), "ctx").astype(jnp.float32),
        lax.psum(shares[3].astype(jnp.bfloat16), "ctx").astype(jnp.float32),
        lax.psum(shares[4].astype(jnp.bfloat16), "ctx").astype(jnp.float32),
        lax.psum(shares[5].astype(jnp.bfloat16), "ctx").astype(jnp.float32),
        lax.psum(shares[6].astype(jnp.bfloat16), "ctx").astype(jnp.float32),
        lax.psum(shares[7].astype(jnp.bfloat16), "ctx").astype(jnp.float32),
        lax.psum(shares[8].astype(jnp.bfloat16), "ctx").astype(jnp.float32),
        lax.psum(shares[9].astype(jnp.bfloat16), "ctx").astype(jnp.float32),
        lax.psum(shares[10].astype(jnp.bfloat16), "ctx").astype(jnp.float32),
        lax.psum(shares[11].astype(jnp.bfloat16), "ctx").astype(jnp.float32),
        lax.psum(shares[12].astype(jnp.bfloat16), "ctx").astype(jnp.float32),
        lax.psum(shares[13].astype(jnp.bfloat16), "ctx").astype(jnp.float32),
        lax.psum(shares[14].astype(jnp.bfloat16), "ctx").astype(jnp.float32),
    )
    return (
        layer_out.astype(jnp.bfloat16)[None],
        grad_inputs[None],
        summed[0],
        summed[1],
        summed[2],
        summed[3],
        summed[4],
        summed[5],
        summed[6],
        summed[7],
        summed[8],
        summed[9],
        summed[10],
        summed[11],
        summed[12],
        summed[13],
        summed[14],
    )


MESH=pl.DeviceIdType.MESH
F32=jnp.float32; BF=jnp.bfloat16

def places():
    c=lax.axis_index("ctx"); f=lax.axis_index("fsdp")
    z=c//2; x=c%2; y=f//2; k=f%2
    return c,f,z,x,y,k

def add_strips(rows, fn, step=16):
    @pl.loop(0, rows//step)
    def _(i):
        fn(pl.ds(pl.multiple_of(i*step,step),step))

def remote_copy(src, dst, send, recv, device):
    return pltpu.make_async_remote_copy(
        src_ref=src,
        dst_ref=dst,
        send_sem=send,
        recv_sem=recv,
        device_id=device,
        device_id_type=MESH,
    )


def greet(peers):
    barrier = pltpu.get_barrier_semaphore()
    for peer in peers:
        pl.semaphore_signal(barrier, inc=1, device_id=peer, device_id_type=MESH)
    pl.semaphore_wait(barrier, len(peers))


def at_row(value, size):
    return pl.ds(pl.multiple_of(value, 16), size)


def window_start(part):
    return 192 * part - 64 * (part % 2)


def lane_windows(parts):
    first, second, third, fourth = parts
    return jnp.concatenate(
        [
            first[:, :128],
            first[:, 128:] + second[:, :128],
            second[:, 128:],
            third[:, :128],
            third[:, 128:] + fourth[:, :128],
            fourth[:, 128:],
        ],
        axis=1,
    )


GATHER_PIECES = ((True, 3), (True, 3), (False, 1), (True, 2), (False, 4))


def gather_project_kernel(*refs):
    (tok, wq_s, wkv_s, wo_s, win_s, wout_s, vec_s) = refs[:7]
    (qg, kvg, wq_o, wkv_o, wo_o, win_o, wout_o, vec_o) = refs[7:15]
    (wq_v, wkv_v, vec_v, send_kv, send_q) = refs[15:20]
    (own_s, own_r, own_l, y_s, y_r, cy_s, cy_r, x_s, x_r, cx_s, cx_r) = refs[20:31]
    (v_s, v_r, v_l, zk_s, zk_r, zq_s, zq_r, f_s, f_r, l_sem, out_sem) = refs[31:]
    c, f, z, x, y, k = places()
    sib = (c, y * 2 + (1 - k))
    yp = (c, (1 - y) * 2 + k)
    diag = (c, (1 - y) * 2 + (1 - k))
    xp = (z * 2 + (1 - x), f)
    zt = [(z + d) % 4 for d in (1, 2, 3)]
    zp = [(item * 2 + x, f) for item in zt]
    greet([sib, yp, diag, xp] + zp)
    shards = (wq_s, wkv_s, wo_s, win_s, wout_s)
    wholes = (wq_v, wkv_v, wo_o, win_o, wout_o)
    fy = (1 - y) * 2 + k
    first = [0]
    for split, count in GATHER_PIECES:
        first.append(first[-1] + count)

    def piece_rows(u, j, xx):
        rows = shards[u].shape[0]
        split, count = GATHER_PIECES[u]
        if split:
            size = rows // 2 // count
            return xx * (rows // 2) + j * size, size
        size = rows // count
        return j * size, size

    def own(u):
        rows = shards[u].shape[0]
        there = wholes[u].at[at_row(f * rows, rows)]
        return remote_copy(shards[u], there, own_s.at[u], own_r.at[u], sib)

    def keep(u):
        rows = shards[u].shape[0]
        there = wholes[u].at[at_row(f * rows, rows)]
        return pltpu.make_async_copy(shards[u], there, own_l.at[u])

    def over_y(u, j):
        rows = shards[u].shape[0]
        start, size = piece_rows(u, j, x)
        i = first[u] + j
        return remote_copy(
            shards[u].at[at_row(start, size)],
            wholes[u].at[at_row(f * rows + start, size)],
            y_s.at[i],
            y_r.at[i],
            yp,
        )

    def landed(u, j, xx):
        rows = shards[u].shape[0]
        start, size = piece_rows(u, j, xx)
        return wholes[u].at[at_row(fy * rows + start, size)]

    def relay_core(u, j):
        i = first[u] + j
        ref = landed(u, j, x)
        return remote_copy(ref, ref, cy_s.at[i], cy_r.at[i], sib)

    def relay_x(u, j):
        i = first[u] + j
        ref = landed(u, j, x)
        return remote_copy(ref, ref, x_s.at[i], x_r.at[i], xp)

    def relay_core_x(u, j):
        i = first[u] + j
        ref = landed(u, j, 1 - x)
        return remote_copy(ref, ref, cx_s.at[i], cx_r.at[i], sib)

    def on_y(u, j):
        over_y(u, j).wait_recv()
        relay_core(u, j).start()
        if GATHER_PIECES[u][0]:
            relay_x(u, j).start()

    def on_x(u, j):
        if GATHER_PIECES[u][0]:
            relay_x(u, j).wait_recv()
            relay_core_x(u, j).start()

    def finish_recv(u):
        own(u).wait_recv()
        keep(u).wait()
        for j in range(GATHER_PIECES[u][1]):
            relay_core(u, j).wait_recv()
            if GATHER_PIECES[u][0]:
                relay_core_x(u, j).wait_recv()

    def finish_send(u):
        own(u).wait_send()
        for j in range(GATHER_PIECES[u][1]):
            over_y(u, j).wait_send()
            relay_core(u, j).wait_send()
            if GATHER_PIECES[u][0]:
                relay_x(u, j).wait_send()
                relay_core_x(u, j).wait_send()

    def vec(i, device):
        return remote_copy(vec_s, vec_v.at[f], v_s.at[i], v_r.at[i], device)

    for j in range(3):
        over_y(1, j).start()
        over_y(0, j).start()
    vec_peers = (sib, yp, diag)
    for i in range(3):
        vec(i, vec_peers[i]).start()
    vec_keep = pltpu.make_async_copy(vec_s, vec_v.at[f], v_l)
    vec_keep.start()
    for u in (1, 0):
        own(u).start()
        keep(u).start()
    for j in range(3):
        on_y(1, j)
        on_y(0, j)
    for u in (3, 2, 4):
        for j in range(GATHER_PIECES[u][1]):
            over_y(u, j).start()
        own(u).start()
        keep(u).start()
    for j in range(3):
        on_x(1, j)
        on_x(0, j)
    for i in range(3):
        vec(i, vec_peers[i]).wait_recv()
    vec_keep.wait()
    finish_recv(1)

    def z_kv(d):
        return remote_copy(
            send_kv.at[zt[d]], kvg.at[c], zk_s.at[d], zk_r.at[d], zp[d]
        )

    def z_kv_in(d):
        slot = ((z + 3 - d) % 4) * 2 + x
        return remote_copy(kvg.at[slot], kvg.at[slot], zk_s.at[d], zk_r.at[d], zp[d])

    def z_q(d):
        return remote_copy(
            send_q.at[zt[d]], qg.at[z], zq_s.at[d], zq_r.at[d], zp[d]
        )

    def own_x():
        return remote_copy(send_kv.at[z], kvg.at[c], f_s.at[3], f_r.at[3], xp)

    def fwd_x(d):
        slot = ((z + 3 - d) % 4) * 2 + x
        return remote_copy(kvg.at[slot], kvg.at[slot], f_s.at[d], f_r.at[d], xp)

    inputs = tok[...]
    for part in range(4):
        lanes = pl.ds(384 * part, 384)
        made = jnp.dot(inputs, wkv_v[:, lanes], preferred_element_type=jnp.float32)
        made = made + vec_v[part, 1:2, :].astype(jnp.float32)
        send_kv[part] = made.astype(jnp.bfloat16)
    own_x().start()
    for d in (1, 0, 2):
        z_kv(d).start()
    keep_kv = pltpu.make_async_copy(send_kv.at[z], kvg.at[c], l_sem.at[0])
    keep_kv.start()
    finish_recv(0)
    bias = lane_windows([vec_v[part, 0:1, 0:256].astype(jnp.float32) for part in range(4)])
    for part in range(4):
        lanes = pl.ds(window_start(part), 256)
        made = jnp.dot(inputs, wq_v[:, lanes], preferred_element_type=jnp.float32)
        made = made + bias[:, window_start(part) : window_start(part) + 256]
        send_q[part] = made.astype(jnp.bfloat16)
    for d in (1, 0, 2):
        z_q(d).start()
    keep_q = pltpu.make_async_copy(send_q.at[z], qg.at[z], l_sem.at[1])
    keep_q.start()
    outs = (
        pltpu.make_async_copy(wq_v, wq_o, out_sem.at[0]),
        pltpu.make_async_copy(wkv_v, wkv_o, out_sem.at[1]),
        pltpu.make_async_copy(vec_v, vec_o, out_sem.at[2]),
    )
    for item in outs:
        item.start()
    on_y(3, 0)
    z_kv_in(0).wait_recv()
    fwd_x(0).start()
    z_kv_in(2).wait_recv()
    fwd_x(2).start()
    z_kv_in(1).wait_recv()
    fwd_x(1).start()
    on_y(3, 1)
    on_y(2, 0)
    on_x(3, 0)
    on_x(3, 1)
    for j in range(4):
        on_y(4, j)
    for d in range(3):
        z_kv(d).wait_send()
        z_q(d).wait()
        fwd_x(d).wait()
    own_x().wait()
    keep_kv.wait()
    keep_q.wait()
    for u in (2, 3, 4):
        finish_recv(u)
    for u in range(5):
        finish_send(u)
    for i in range(3):
        vec(i, vec_peers[i]).wait_send()
    for item in outs:
        item.wait()


def any_specs(count):
    return [pl.BlockSpec(memory_space=pl.ANY)] * count


def vmem_specs(count):
    return [pl.BlockSpec(memory_space=pltpu.VMEM)] * count


def half(*shape):
    return jax.ShapeDtypeStruct(shape, jnp.bfloat16)


def full(*shape):
    return jax.ShapeDtypeStruct(shape, jnp.float32)


def gather_project(tok, wq, wkv, wo, win, wout, vec):
    rows, width = tok.shape
    d = pltpu.SemaphoreType.DMA
    count = sum(item[1] for item in GATHER_PIECES)
    return pl.pallas_call(
        gather_project_kernel,
        out_shape=[
            half(4, rows, 256),
            half(8, rows, 384),
            half(width, width),
            half(width, 2 * width),
            half(width, width),
            half(width, win.shape[1]),
            half(4 * wout.shape[0], width),
            half(4, 16, 384),
        ],
        in_specs=vmem_specs(1) + any_specs(6),
        out_specs=any_specs(8),
        scratch_shapes=[
            pltpu.VMEM((width, width), jnp.bfloat16),
            pltpu.VMEM((width, 2 * width), jnp.bfloat16),
            pltpu.VMEM((4, 16, 384), jnp.bfloat16),
            pltpu.VMEM((4, rows, 384), jnp.bfloat16),
            pltpu.VMEM((4, rows, 256), jnp.bfloat16),
            d((5,)),
            d((5,)),
            d((5,)),
        ]
        + [d((count,))] * 8
        + [d((3,)), d((3,)), d, d((3,)), d((3,)), d((3,)), d((3,)), d((4,)), d((4,)), d((2,)), d((3,))],
        compiler_params=pltpu.CompilerParams(
            collective_id=2, has_side_effects=True, vmem_limit_bytes=40 * 2**20
        ),
        cost_estimate=pl.CostEstimate(flops=10**9, bytes_accessed=10**8, transcendentals=0),
        name="gather_project",
    )(tok, wq, wkv, wo, win, wout, vec)


def pick(parity, value_side, by_window):
    shape = (384, 256) if not by_window else (256, 384)
    spread = lax.broadcasted_iota(jnp.int32, shape, 0 if not by_window else 1)
    window = lax.broadcasted_iota(jnp.int32, shape, 1 if not by_window else 0)
    lane = spread % 128
    low = 64 if value_side else 0
    target = (spread // 128) * 64 + (lane - low) + 64 * parity
    inside = (lane >= low) & (lane < low + 64)
    return jnp.where(inside & (target == window), 1.0, 0.0)


def dot_nt(left, right):
    return lax.dot_general(
        left, right, (((1,), (1,)), ((), ())), preferred_element_type=jnp.float32
    )


def attention_kernel(deal, lengths, qg, kvg, owin, osave, lse, kvn, kvt, qt):
    c = lax.axis_index("ctx")
    z = c // 2
    x = c % 2
    scale = HEAD_DIM ** (-0.5)
    span = 1024
    for b in range(16):
        seq = deal[b] // 8
        natural = pl.multiple_of((deal[b] % 8) * BLOCK, BLOCK)
        for h in range(3):
            tile = kvg[b // 2, pl.ds((b % 2) * BLOCK, BLOCK), pl.ds(128 * h, 128)]
            kvn[h, seq, pl.ds(natural, BLOCK), :] = tile
            kvt[h, seq, :, pl.ds(natural, BLOCK)] = jnp.transpose(tile.astype(jnp.float32)).astype(
                jnp.bfloat16
            )
    spread = (pick(z % 2, False, False) * scale).astype(jnp.bfloat16)
    gather = pick(z % 2, True, False).astype(jnp.bfloat16)
    for part in range(4):
        qt[:, pl.ds(256 * part, 256)] = dot_nt(spread, qg[part]).astype(jnp.bfloat16)

    @pl.loop(0, 8)
    def _(b):
        dealt = ((b // 2) * 2 + x) * 2 + b % 2
        seq = deal[dealt] // 8
        length = lengths[seq]
        here = pl.ds(pl.multiple_of(b * BLOCK, BLOCK), BLOCK)
        rows = lax.broadcasted_iota(jnp.int32, (span, BLOCK), 0)
        made = []
        for h in range(3):
            scores = jnp.dot(
                kvn[h, seq],
                qt[pl.ds(128 * h, 128), here],
                preferred_element_type=jnp.float32,
            )
            scores = jnp.where(rows < length, scores, NEG_FILL)
            top = jnp.max(scores, axis=0, keepdims=True)
            weights = jnp.exp(scores - top)
            total = jnp.sum(weights, axis=0, keepdims=True)
            mixed = jnp.dot(
                kvt[h, seq],
                weights.astype(jnp.bfloat16),
                preferred_element_type=jnp.float32,
            )
            mixed = mixed / total
            osave[h, b] = mixed[64:]
            lse[h, b] = jnp.broadcast_to(top + jnp.log(total), (8, BLOCK))
            made.append(jnp.transpose(mixed).astype(jnp.bfloat16))
        joined = jnp.concatenate(made, axis=1)
        owin[b // 2, pl.ds(pl.multiple_of((b % 2) * BLOCK, BLOCK), BLOCK), :] = jnp.dot(
            joined, gather, preferred_element_type=jnp.float32
        ).astype(jnp.bfloat16)


def attention_forward(deal, lengths, qg, kvg):
    smem = [pl.BlockSpec(memory_space=pltpu.SMEM)] * 2
    return pl.pallas_call(
        attention_kernel,
        out_shape=[
            half(4, 256, 256),
            full(3, 8, 64, BLOCK),
            full(3, 8, 8, BLOCK),
            half(3, 2, 1024, 128),
            half(3, 2, 128, 1024),
        ],
        in_specs=smem + vmem_specs(2),
        out_specs=vmem_specs(5),
        scratch_shapes=[pltpu.VMEM((384, 1024), jnp.bfloat16)],
        compiler_params=pltpu.CompilerParams(vmem_limit_bytes=40 * 2**20),
        cost_estimate=pl.CostEstimate(flops=2 * 10**9, bytes_accessed=10**7, transcendentals=3 * 10**6),
        name="attention_forward",
    )(deal, lengths, qg, kvg)


def heads_home_kernel(win, out, got, send, recv, local):
    c, f, z, x, y, k = places()
    zt = [(z + d) % 4 for d in (1, 2, 3)]
    zp = [(item * 2 + x, f) for item in zt]
    greet(zp)
    copies = [
        remote_copy(win.at[zt[d]], got.at[z], send.at[d], recv.at[d], zp[d]) for d in range(3)
    ]
    for d in (1, 0, 2):
        copies[d].start()
    keep = pltpu.make_async_copy(win.at[z], got.at[z], local)
    keep.start()
    keep.wait()
    for item in copies:
        item.wait()
    out[...] = lane_windows([got[part] for part in range(4)])


def heads_home(win):
    d = pltpu.SemaphoreType.DMA
    return pl.pallas_call(
        heads_home_kernel,
        out_shape=half(256, 768),
        in_specs=vmem_specs(1),
        out_specs=pl.BlockSpec(memory_space=pltpu.VMEM),
        scratch_shapes=[pltpu.VMEM((4, 256, 256), jnp.bfloat16), d((3,)), d((3,)), d],
        compiler_params=pltpu.CompilerParams(collective_id=3, has_side_effects=True, vmem_limit_bytes=16 * 2**20),
        cost_estimate=pl.CostEstimate(flops=10**6, bytes_accessed=10**7, transcendentals=0),
        name="heads_home",
    )(win)


class Reducer:
    def __init__(self, chunks, ins, outs, scr):
        n = len(chunks)
        self.chunks, self.ins, self.outs, self.n = chunks, ins, outs, n
        groups = [scr[n * i : n * (i + 1)] for i in range(8)]
        self.loc, self.rc, self.ry, self.rx, self.cb, self.rz, self.re, self.res = groups
        self.sems = scr[8 * n :]
        c, f, z, x, y, k = places()
        self.side = jnp.where((z == 1) | (z == 2), 1, 0)
        self.deep = z // 2
        self.near = ((z + 1 - 2 * (z % 2)) * 2 + x, f)
        self.far = ((3 - z) * 2 + x, f)
        self.z, self.x, self.y, self.k = z, x, y, k
        self.sib = (c, y * 2 + (1 - k))
        self.yp = (c, (1 - y) * 2 + k)
        self.xp = (z * 2 + (1 - x), f)

    def slab(self, i, f):
        m, slab = self.chunks[i][:2]
        return slab(self.ins[m], f)

    def load(self, i, yy):
        sem = self.sems[0].at[i, yy]
        return pltpu.make_async_copy(self.slab(i, yy * 2 + self.k), self.loc[i].at[yy], sem)

    def core(self, i, yy):
        src = self.slab(i, yy * 2 + (1 - self.k))
        send, recv = self.sems[2].at[i, yy], self.sems[3].at[i, yy]
        return remote_copy(src, self.rc[i].at[yy], send, recv, self.sib)

    def over_y(self, i):
        send, recv = self.sems[4].at[i], self.sems[5].at[i]
        return remote_copy(self.loc[i].at[1 - self.y], self.ry[i], send, recv, self.yp)

    def lanes(self, i, xx):
        wide = self.chunks[i][5] // 2
        return pl.ds(pl.multiple_of(xx * wide, 128), wide)

    def span(self, i, side, deep=None):
        high = self.chunks[i][4]
        if deep is None:
            return pl.ds(pl.multiple_of(side * (high // 2), high // 2), high // 2)
        base = side * (high // 2) + deep * (high // 4)
        return pl.ds(pl.multiple_of(base, high // 4), high // 4)

    def over_x(self, i):
        src = self.loc[i].at[self.y, :, self.lanes(i, 1 - self.x)]
        send, recv = self.sems[6].at[i], self.sems[7].at[i]
        return remote_copy(src, self.rx[i], send, recv, self.xp)

    def to_near(self, i):
        src = self.cb[i].at[self.span(i, 1 - self.side)]
        send, recv = self.sems[8].at[i], self.sems[9].at[i]
        return remote_copy(src, self.rz[i], send, recv, self.near)

    def to_far(self, i):
        src = self.cb[i].at[self.span(i, self.side, 1 - self.deep)]
        send, recv = self.sems[10].at[i], self.sems[11].at[i]
        return remote_copy(src, self.re[i], send, recv, self.far)

    def share_far(self, i, deep):
        ref = self.res[i].at[self.x, self.span(i, self.side, deep)]
        send, recv = self.sems[14].at[i], self.sems[15].at[i]
        return remote_copy(ref, ref, send, recv, self.far)

    def share_near(self, i, side):
        ref = self.res[i].at[self.x, self.span(i, side)]
        send, recv = self.sems[16].at[i], self.sems[17].at[i]
        return remote_copy(ref, ref, send, recv, self.near)

    def share_x(self, i, xx):
        ref = self.res[i].at[xx]
        send, recv = self.sems[12].at[i], self.sems[13].at[i]
        return remote_copy(ref, ref, send, recv, self.xp)

    def out(self, i, xx):
        m, home = self.chunks[i][2:4]
        sem = self.sems[1].at[i, xx]
        return pltpu.make_async_copy(self.res[i].at[xx], home(self.outs[m], xx), sem)

    def start(self, i):
        for yy in (0, 1):
            self.core(i, yy).start()
            self.load(i, yy).start()

    def stage0(self, i):
        for yy in (0, 1):
            self.load(i, yy).wait()
            self.core(i, yy).wait()

        def add(s):
            for yy in (0, 1):
                total = self.loc[i][yy, s].astype(jnp.float32) + self.rc[i][yy, s].astype(jnp.float32)
                self.loc[i][yy, s] = total.astype(jnp.bfloat16)

        add_strips(self.chunks[i][4], add)
        self.over_y(i).start()

    def stage1(self, i):
        self.over_y(i).wait()

        def add(s):
            total = self.loc[i][self.y, s].astype(jnp.float32) + self.ry[i][s].astype(jnp.float32)
            self.loc[i][self.y, s] = total.astype(jnp.bfloat16)

        add_strips(self.chunks[i][4], add)
        self.over_x(i).start()

    def stage2(self, i):
        self.over_x(i).wait()
        mine = self.lanes(i, self.x)

        def add(s):
            total = self.loc[i][self.y, s, mine].astype(jnp.float32) + self.rx[i][s].astype(jnp.float32)
            self.cb[i][s] = total.astype(jnp.bfloat16)

        add_strips(self.chunks[i][4], add)
        self.to_near(i).start()

    def stage3(self, i):
        self.to_near(i).wait()
        high = self.chunks[i][4] // 2

        @pl.loop(0, high // 16)
        def _(j):
            own = pl.ds(pl.multiple_of(self.side * high + j * 16, 16), 16)
            s = pl.ds(pl.multiple_of(j * 16, 16), 16)
            total = self.cb[i][own].astype(jnp.float32) + self.rz[i][s].astype(jnp.float32)
            self.cb[i][own] = total.astype(jnp.bfloat16)

        self.to_far(i).start()

    def stage4(self, i):
        self.to_far(i).wait()
        high = self.chunks[i][4] // 4

        @pl.loop(0, high // 16)
        def _(j):
            base = self.side * (2 * high) + self.deep * high + j * 16
            own = pl.ds(pl.multiple_of(base, 16), 16)
            s = pl.ds(pl.multiple_of(j * 16, 16), 16)
            total = self.cb[i][own].astype(jnp.float32) + self.re[i][s].astype(jnp.float32)
            self.res[i][self.x, own] = total.astype(jnp.bfloat16)

        self.share_far(i, self.deep).start()

    def stage5(self, i):
        self.share_far(i, self.deep).wait_send()
        self.share_far(i, 1 - self.deep).wait_recv()
        self.share_near(i, self.side).start()

    def stage6(self, i):
        self.share_near(i, self.side).wait_send()
        self.share_near(i, 1 - self.side).wait_recv()
        self.share_x(i, self.x).start()
        self.out(i, self.x).start()

    def stage7(self, i):
        self.share_x(i, self.x).wait_send()
        self.share_x(i, 1 - self.x).wait_recv()
        self.out(i, 1 - self.x).start()

    def tick(self, t):
        for lag, stage in (
            (0, self.stage0),
            (8, self.stage7),
            (7, self.stage6),
            (6, self.stage5),
            (5, self.stage4),
            (4, self.stage3),
            (3, self.stage2),
            (2, self.stage1),
        ):
            if 0 <= t - lag < self.n:
                stage(t - lag)

    def finish(self):
        for i in range(self.n):
            for xx in (0, 1):
                self.out(i, xx).wait()


def reduce_plan(shapes):
    chunks = []
    for m, (rows, width) in enumerate(shapes):
        shard = rows // 4
        high = min(shard, 192)
        wide = min(width, 768)
        for i in range(shard // high):
            for j in range(width // wide):

                def slab(ref, f, i=i, j=j, shard=shard, high=high, wide=wide):
                    rows = pl.ds(pl.multiple_of(f * shard + i * high, high), high)
                    return ref.at[rows, pl.ds(j * wide, wide)]

                def home(ref, xx, i=i, j=j, high=high, wide=wide):
                    lanes = pl.ds(pl.multiple_of(j * wide + xx * (wide // 2), 128), wide // 2)
                    return ref.at[pl.ds(i * high, high), lanes]

                chunks.append((m, slab, m, home, high, wide))
    return chunks


def reduce_scratch(chunks):
    scratch = []
    for lead, divide_rows, divide_lanes in (
        ((2,), 1, 1),
        ((2,), 1, 1),
        ((), 1, 1),
        ((), 1, 2),
        ((), 1, 2),
        ((), 2, 2),
        ((), 4, 2),
        ((2,), 1, 2),
    ):
        for item in chunks:
            shape = lead + (item[4] // divide_rows, item[5] // divide_lanes)
            scratch.append(pltpu.VMEM(shape, jnp.bfloat16))
    for lanes in (2, 2, 2, 2) + (1,) * 14:
        shape = (len(chunks), lanes) if lanes > 1 else (len(chunks),)
        scratch.append(pltpu.SemaphoreType.DMA(shape))
    return scratch


def split_pairs():
    src = lax.broadcasted_iota(jnp.int32, (256, 256), 0)
    dst = lax.broadcasted_iota(jnp.int32, (256, 256), 1)
    piece = src // 64
    moved = (piece % 2) * 128 + (piece // 2) * 64 + src % 64
    return jnp.where(moved == dst, 1.0, 0.0).astype(jnp.bfloat16)


def dot_tn(left, right):
    return lax.dot_general(
        left, right, (((0,), (0,)), ((), ())), preferred_element_type=jnp.float32
    )


def backward_kernel(chunks, *refs):
    deal, lengths, seqs = refs[:3]
    refs = refs[1:]
    (gm, qg_h, os_h, lse_h, kvn_h, kvt_h, tok_h, wq_h, wkv_h, gone_h, gout, gin, gmix) = refs[2:15]
    small_h = refs[15:22]
    gtok = refs[22]
    outs = refs[23:30]
    (qg, osave, lse, kvn, kvt, tok, wq, wkv, gone) = refs[30:39]
    small = refs[39:46]
    gvec = refs[46]
    (dog, qt, dot_t, qd, acc, dqw, give, theirs, mine, got_q, got_kv, gq, gk, gv, tok_out) = refs[47:62]
    (load_sem, o_s, o_r, o_l, q_s, q_r, q_l, x_s, x_r, k_s, k_r, k_l, t_l) = refs[62:75]
    ins = (gout, gin, gmix, gq, gk, gv, gvec)
    red = Reducer(chunks, ins, outs, refs[75:])
    c, f, z, x, y, k = places()
    zt = [(z + d) % 4 for d in (1, 2, 3)]
    zp = [(item * 2 + x, f) for item in zt]
    xp = red.xp
    loads = [
        pltpu.make_async_copy(src, dst, load_sem.at[i])
        for i, (src, dst) in enumerate(
            (
                (qg_h, qg),
                (kvn_h, kvn),
                (kvt_h, kvt),
                (os_h, osave),
                (lse_h, lse),
                (tok_h, tok),
                (wq_h, wq),
                (wkv_h, wkv),
                (gone_h, gone),
            )
            + tuple(zip(small_h, small))
        )
    ]
    for item in loads[:5]:
        item.start()
    greet([red.sib, red.yp, xp] + zp)

    def window(part):
        return pl.ds(pl.multiple_of(window_start(part), 128), 256)

    def o_copy(d):
        return remote_copy(gm.at[:, window(zt[d])], dog.at[z], o_s.at[d], o_r.at[d], zp[d])

    for d in (1, 0, 2):
        o_copy(d).start()
    keep_o = pltpu.make_async_copy(gm.at[:, window(z)], dog.at[z], o_l)
    keep_o.start()
    for i in range(3):
        red.start(i)
    red.tick(0)
    red.start(3)
    red.tick(1)
    red.start(4)
    for item in loads[5:]:
        item.start()

    scale = HEAD_DIM ** (-0.5)
    span = 1024
    spread_q = (pick(z % 2, False, False) * scale).astype(jnp.bfloat16)
    spread_o = pick(z % 2, True, False).astype(jnp.bfloat16)
    gather_q = pick(z % 2, False, False).astype(jnp.bfloat16)

    def place(b):
        return seqs[((b // 2) * 2 + x) * 2 + b % 2]

    def masked(rows, b, base):
        later = place(b).astype(jnp.float32)
        for s in range(2):
            keep = later if s == 1 else 1.0 - later
            kept = (rows * keep).astype(jnp.bfloat16)
            for h in range(3):
                qd[b, pl.ds(base, BLOCK), pl.ds(256 * h + 128 * s, 128)] = kept[
                    :, 128 * h : 128 * (h + 1)
                ]

    loads[0].wait()
    for part in range(4):
        qt[:, pl.ds(256 * part, 256)] = dot_nt(spread_q, qg[part]).astype(jnp.bfloat16)
        rows = dot_nt(qg[part], spread_q)
        for i in range(2):
            masked(rows[i * BLOCK : (i + 1) * BLOCK], 2 * part + i, 0)
    for h in range(3):
        acc[h] = jnp.zeros(acc.shape[1:], jnp.float32)
    red.tick(2)
    red.start(5)
    keep_o.wait()
    for d in range(3):
        o_copy(d).wait()
    for part in range(4):
        dot_t[:, pl.ds(256 * part, 256)] = dot_nt(spread_o, dog[part]).astype(jnp.bfloat16)
        rows = dot_nt(dog[part], spread_o)
        for i in range(2):
            masked(rows[i * BLOCK : (i + 1) * BLOCK], 2 * part + i, BLOCK)
    for item in loads[1:5]:
        item.wait()
    red.tick(3)
    red.start(6)

    def pair(p):
        key_rows = lax.broadcasted_iota(jnp.int32, (span, BLOCK), 0)
        made = ([], [])
        for h in range(3):
            lanes = pl.ds(128 * h, 128)
            both = []
            for i in range(2):
                b = 2 * p + i
                seq = place(b)
                length = lengths[seq]
                here = pl.ds(pl.multiple_of(b * BLOCK, BLOCK), BLOCK)
                part = kvn[h, seq]
                scores = jnp.dot(part, qt[lanes, here], preferred_element_type=jnp.float32)
                scores = jnp.where(key_rows < length, scores, NEG_FILL)
                probs = jnp.exp(scores - lse[h, b, 0:1, :])
                upstream = dot_t[lanes, here]
                grad_probs = jnp.dot(part, upstream, preferred_element_type=jnp.float32)
                delta = jnp.sum(
                    osave[h, b] * upstream[64:].astype(jnp.float32), axis=0, keepdims=True
                )
                grad_scores = (probs * (grad_probs - delta)).astype(jnp.bfloat16)
                grad_query = jnp.dot(
                    kvt[h, seq], grad_scores, preferred_element_type=jnp.float32
                )
                made[i].append((jnp.transpose(grad_query) * scale).astype(jnp.bfloat16))
                both += [grad_scores, probs.astype(jnp.bfloat16)]
            right = jnp.concatenate(
                [qd[2 * p, :, pl.ds(256 * h, 256)], qd[2 * p + 1, :, pl.ds(256 * h, 256)]], axis=0
            )
            found = jnp.dot(
                jnp.concatenate(both, axis=1), right, preferred_element_type=jnp.float32
            )
            acc[h, pl.ds(0, 8)] += found[:, :128].reshape(8, BLOCK, 128)
            acc[h, pl.ds(8, 8)] += found[:, 128:].reshape(8, BLOCK, 128)
        for i in range(2):
            dqw[p, pl.ds(i * BLOCK, BLOCK), :] = jnp.dot(
                jnp.concatenate(made[i], axis=1), gather_q, preferred_element_type=jnp.float32
            ).astype(jnp.bfloat16)

    pl.loop(0, 3)(pair)
    red.tick(4)
    red.start(7)
    pl.loop(3, 4)(pair)

    def q_copy(d):
        return remote_copy(dqw.at[zt[d]], got_q.at[z], q_s.at[d], q_r.at[d], zp[d])

    for d in (1, 0, 2):
        q_copy(d).start()
    keep_q = pltpu.make_async_copy(dqw.at[z], got_q.at[z], q_l)
    keep_q.start()
    order = [zt[1], zt[0], zt[2], z]
    where = [1, 0, 2]

    def over_x(i):
        return remote_copy(give.at[i], theirs.at[i], x_s.at[i], x_r.at[i], xp)

    def collect(out, i, part, xx):
        for j in range(2):
            natural = deal[(part * 2 + xx) * 2 + j]
            for h in range(3):
                out[i, pl.ds(j * BLOCK, BLOCK), pl.ds(128 * h, 128)] = acc[
                    h, natural
                ].astype(jnp.bfloat16)

    for i in range(4):
        collect(give, i, order[i], 1 - x)
        over_x(i).start()
    red.tick(5)
    red.start(8)
    for i in range(4):
        collect(mine, i, order[i], x)

    def kv_copy(i):
        d = where[i]
        return remote_copy(mine.at[i], got_kv.at[z], k_s.at[d], k_r.at[d], zp[d])

    for i in range(4):
        over_x(i).wait_recv()

        @pl.loop(0, 16)
        def _(j, i=i):
            rows = pl.ds(pl.multiple_of(j * 16, 16), 16)
            mine[i, rows] = (
                mine[i, rows].astype(jnp.float32) + theirs[i, rows].astype(jnp.float32)
            ).astype(jnp.bfloat16)

        if i < 3:
            kv_copy(i).start()
        if i == 1:
            red.tick(6)
    keep_kv = pltpu.make_async_copy(mine.at[3], got_kv.at[z], k_l)
    keep_kv.start()
    keep_q.wait()
    for d in range(3):
        q_copy(d).wait()
    for item in loads[5:]:
        item.wait()
    dq = lane_windows([got_q[part] for part in range(4)])
    tokens = tok[...]
    gq[...] = dot_tn(tokens, dq).astype(jnp.bfloat16)
    red.start(9)
    total = gone[...] + dot_nt(dq, wq[...])
    red.tick(7)
    keep_kv.wait()
    for i in range(3):
        kv_copy(i).wait()
    split = split_pairs()
    keys, values = [], []
    for part in range(4):
        block = got_kv[part]
        total = total + dot_nt(block, wkv[:, pl.ds(384 * part, 384)])
    joined = jnp.concatenate([got_kv[part] for part in range(4)], axis=1)
    for i in range(6):
        apart = jnp.dot(
            joined[:, 256 * i : 256 * (i + 1)], split, preferred_element_type=jnp.float32
        ).astype(jnp.bfloat16)
        keys.append(apart[:, :128])
        values.append(apart[:, 128:])
    dk = jnp.concatenate(keys, axis=1)
    dv = jnp.concatenate(values, axis=1)
    gk[...] = dot_tn(tokens, dk).astype(jnp.bfloat16)
    red.start(10)
    gv[...] = dot_tn(tokens, dv).astype(jnp.bfloat16)
    red.start(11)
    q_bias = jnp.sum(dq.astype(jnp.float32), axis=0, keepdims=True)
    v_bias = jnp.sum(dv.astype(jnp.float32), axis=0, keepdims=True)
    line = lax.broadcasted_iota(jnp.int32, (16, 256), 0)
    lines = [q_bias, v_bias] + [item[...] for item in small[:6]]
    for part in range(4):
        lanes = slice(window_start(part), window_start(part) + 256)
        top = jnp.zeros((16, 256), jnp.float32)
        for i, item in enumerate(lines):
            top = jnp.where(line == i, item[:, lanes], top)
        for i in range(3):
            base = 768 * part + 256 * i
            top = jnp.where(line == 8 + i, small[6][:, base : base + 256], top)
        gvec[pl.ds(64 * part, 16), :] = top.astype(jnp.bfloat16)
        gvec[pl.ds(64 * part + 16, 48), :] = jnp.zeros((48, 256), jnp.bfloat16)
    red.start(12)
    tok_out[...] = total
    keep_tok = pltpu.make_async_copy(tok_out, gtok, t_l)
    keep_tok.start()
    for t in range(8, red.n + 8):
        red.tick(t)
    red.finish()
    keep_tok.wait()
    for i in range(4):
        over_x(i).wait_send()


def backward(deal, lengths, seqs, gm, qg, osave, lse, kvn, kvt, tok, wq, wkv, gone, gout, gin, gmix, small):
    chunks = reduce_plan(
        [gout.shape, gin.shape, gmix.shape, (768, 768), (768, 768), (768, 768), (256, 256)]
    )
    bf, f32, d = jnp.bfloat16, jnp.float32, pltpu.SemaphoreType.DMA
    v = pltpu.VMEM
    scratch = [
        v((4, 256, 256), bf),
        v((3, 8, 64, BLOCK), f32),
        v((3, 8, 8, BLOCK), f32),
        v((3, 2, 1024, 128), bf),
        v((3, 2, 128, 1024), bf),
        v((256, 768), bf),
        v((768, 768), bf),
        v((768, 1536), bf),
        v((256, 768), f32),
    ]
    scratch += [v(item.shape, f32) for item in small]
    scratch += [
        v((256, 256), bf),
        v((4, 256, 256), bf),
        v((384, 1024), bf),
        v((384, 1024), bf),
        v((8, 256, 768), bf),
        v((3, 16, BLOCK, 128), f32),
        v((4, 256, 256), bf),
        v((4, 256, 384), bf),
        v((4, 256, 384), bf),
        v((4, 256, 384), bf),
        v((4, 256, 256), bf),
        v((4, 256, 384), bf),
        v((768, 768), bf),
        v((768, 768), bf),
        v((768, 768), bf),
        v((256, 768), f32),
        d((16,)),
        d((3,)),
        d((3,)),
        d,
        d((3,)),
        d((3,)),
        d,
        d((4,)),
        d((4,)),
        d((3,)),
        d((3,)),
        d,
        d,
    ]
    return pl.pallas_call(
        functools.partial(backward_kernel, chunks),
        out_shape=[
            full(256, 768),
            half(768, 768),
            half(192, 3072),
            half(192, 768),
            half(192, 768),
            half(192, 768),
            half(192, 768),
            half(64, 256),
        ],
        in_specs=[pl.BlockSpec(memory_space=pltpu.SMEM)] * 3 + any_specs(20),
        out_specs=any_specs(8),
        scratch_shapes=scratch + reduce_scratch(chunks),
        compiler_params=pltpu.CompilerParams(
            collective_id=6, has_side_effects=True, vmem_limit_bytes=60 * 2**20
        ),
        cost_estimate=pl.CostEstimate(flops=10**10, bytes_accessed=10**8, transcendentals=3 * 10**6),
        name="backward",
    )(deal, lengths, seqs, gm, qg, osave, lse, kvn, kvt, tok, wq, wkv, gone, gout, gin, gmix, *small)


def body_fast(
    tokens,
    seq_lengths,
    deal,
    w_query,
    w_key,
    w_value,
    w_attn_out,
    b_query,
    b_value,
    b_attn_out,
    norm1_gain,
    norm1_bias,
    w_in,
    b_in,
    w_out,
    b_out,
    norm2_gain,
    norm2_bias,
    cotangent,
):
    inputs = tokens[0]
    width = inputs.shape[1]
    part = width // 4
    odd = lax.axis_index("fsdp") % 2 == 1
    pair_shape = (part, HEADS, HEAD_DIM)
    pair_weight = jnp.stack(
        [to_half(w_key).reshape(pair_shape), to_half(w_value).reshape(pair_shape)], axis=2
    ).reshape(part, 2 * width)
    query_row = jnp.where(
        odd, jnp.pad(b_query, (HEAD_DIM, 384 - 256)), jnp.pad(b_query, (0, 384 - 192))
    )
    value_heads = b_value.reshape(3, HEAD_DIM)
    pair_row = jnp.stack([jnp.zeros_like(value_heads), value_heads], axis=1).reshape(384)
    small = [query_row, pair_row]
    for item in (b_attn_out, norm1_gain, norm1_bias, b_out, norm2_gain, norm2_bias):
        small.append(jnp.pad(item, (0, 384 - part)))
    packed = jnp.concatenate(
        [jnp.stack(small), b_in.reshape(2, 384), jnp.zeros((6, 384), jnp.float32)], axis=0
    )
    (
        query_groups,
        pair_groups,
        query_weight,
        pair_weights,
        mix_weight,
        inner_weight,
        outer_weight,
        vectors,
    ) = gather_project(
        inputs,
        to_half(w_query),
        pair_weight,
        to_half(w_attn_out),
        to_half(w_in),
        to_half(w_out),
        to_half(packed),
    )
    vectors = vectors.astype(jnp.float32)
    mix_bias, gain_one, shift_one, outer_bias, gain_two, shift_two = (
        vectors[:, 2 + i, :part].reshape(width) for i in range(6)
    )
    inner_bias = vectors[:, 8:10, :].reshape(4 * width)
    deal_row = deal[0]
    lengths = seq_lengths[0]
    out_windows, out_heads, log_totals, pairs, pairs_turned = attention_forward(
        deal_row, lengths, query_groups, pair_groups
    )
    attn_in = heads_home(out_windows)
    residual_one = (
        inputs.astype(jnp.float32)
        + jnp.dot(attn_in, mix_weight, preferred_element_type=jnp.float32)
        + mix_bias
    )
    normal_one, normed_one, inverse_one = norm_forward(residual_one, gain_one, shift_one)
    normal_half = normal_one.astype(jnp.bfloat16)
    pre_act = jnp.dot(normal_half, inner_weight, preferred_element_type=jnp.float32) + inner_bias
    activated, gelu_pull = jax.vjp(exact_gelu, pre_act)
    hidden = activated.astype(jnp.bfloat16)
    residual_two = (
        normal_one
        + jnp.dot(hidden, outer_weight, preferred_element_type=jnp.float32)
        + outer_bias
    )
    layer_out, normed_two, inverse_two = norm_forward(residual_two, gain_two, shift_two)
    upstream = cotangent[0].astype(jnp.float32)
    grad_two, grad_gain_two, grad_shift_two = norm_backward(
        upstream, gain_two, normed_two, inverse_two
    )
    grad_branch = grad_two.astype(jnp.bfloat16)
    grad_outer_bias = jnp.sum(grad_branch.astype(jnp.float32), axis=0)
    grad_outer = jnp.einsum("tf,td->fd", hidden, grad_branch, preferred_element_type=jnp.float32)
    grad_hidden = jnp.einsum(
        "td,fd->tf", grad_branch, outer_weight, preferred_element_type=jnp.float32
    )
    grad_pre = gelu_pull(grad_hidden)[0].astype(jnp.bfloat16)
    grad_inner_bias = jnp.sum(grad_pre.astype(jnp.float32), axis=0)
    grad_inner = jnp.einsum("td,tf->df", normal_half, grad_pre, preferred_element_type=jnp.float32)
    grad_normal = grad_two + jnp.einsum(
        "tf,df->td", grad_pre, inner_weight, preferred_element_type=jnp.float32
    )
    grad_one, grad_gain_one, grad_shift_one = norm_backward(
        grad_normal, gain_one, normed_one, inverse_one
    )
    grad_attn = grad_one.astype(jnp.bfloat16)
    grad_mix_bias = jnp.sum(grad_attn.astype(jnp.float32), axis=0)
    grad_mix = jnp.einsum("td,te->de", attn_in, grad_attn, preferred_element_type=jnp.float32)
    grad_mixed = jnp.einsum(
        "te,de->td", grad_attn, mix_weight, preferred_element_type=jnp.float32
    ).astype(jnp.bfloat16)
    (
        grad_inputs,
        sum_outer,
        sum_inner,
        sum_mix,
        sum_query,
        sum_key,
        sum_value,
        sum_small,
    ) = backward(
        deal_row,
        lengths,
        deal_row // 8,
        grad_mixed,
        query_groups,
        out_heads,
        log_totals,
        pairs,
        pairs_turned,
        inputs,
        query_weight,
        pair_weights,
        grad_one,
        to_half(grad_outer),
        to_half(grad_inner),
        to_half(grad_mix),
        [
            item.reshape(1, -1)
            for item in (
                grad_mix_bias,
                grad_gain_one,
                grad_shift_one,
                grad_outer_bias,
                grad_gain_two,
                grad_shift_two,
                grad_inner_bias,
            )
        ],
    )
    sum_small = sum_small.astype(jnp.float32)
    small = jnp.where(odd, sum_small[:8, HEAD_DIM:], sum_small[:8, :part])
    others = small[2:]
    return (
        layer_out.astype(jnp.bfloat16)[None],
        grad_inputs[None],
        sum_query.astype(jnp.float32),
        sum_key.astype(jnp.float32),
        sum_value.astype(jnp.float32),
        sum_mix.astype(jnp.float32),
        small[0],
        small[1],
        others[0],
        others[1],
        others[2],
        sum_inner.astype(jnp.float32),
        sum_small[8:11].reshape(width),
        sum_outer.astype(jnp.float32),
        others[3],
        others[4],
        others[5],
    )


def solution(mesh):
    placed = (
        P("fsdp", "ctx", None),
        P("fsdp", None),
        P("fsdp", None),
        P("fsdp", None),
        P("fsdp", None),
        P("fsdp", None),
        P("fsdp", None),
        P("fsdp"),
        P("fsdp"),
        P("fsdp"),
        P("fsdp"),
        P("fsdp"),
        P("fsdp", None),
        P("fsdp"),
        P("fsdp", None),
        P("fsdp"),
        P("fsdp"),
        P("fsdp"),
        P("fsdp", "ctx", None),
    )
    fast = dict(mesh.shape) == {"ctx": 8, "fsdp": 4}
    return jax.shard_map(
        body_fast if fast else body,
        mesh=mesh,
        in_specs=placed,
        out_specs=(
            P("fsdp", "ctx", None),
            P("fsdp", "ctx", None),
            P("fsdp", None),
            P("fsdp", None),
            P("fsdp", None),
            P("fsdp", None),
            P("fsdp"),
            P("fsdp"),
            P("fsdp"),
            P("fsdp"),
            P("fsdp"),
            P("fsdp", None),
            P("fsdp"),
            P("fsdp", None),
            P("fsdp"),
            P("fsdp"),
            P("fsdp"),
        ),
        check_vma=False,
    )
```

```python
import functools

import jax
import jax.numpy as jnp
from jax import lax
from jax.experimental import pallas as pl
from jax.experimental.pallas import tpu as pltpu
from jax.sharding import PartitionSpec as P

HEADS = 12
HEAD_DIM = 64
BLOCK = 128


EPSILON = 1e-12
NEG_FILL = -1e30


def block_codes(lengths, deal_row):
    padded = (lengths + BLOCK - 1) // BLOCK * BLOCK
    seq_ends = jnp.cumsum(padded)
    offsets = jnp.tile(jnp.arange(BLOCK, dtype=jnp.int32), deal_row.shape[0])
    natural = jnp.repeat(deal_row * BLOCK, BLOCK) + offsets
    passed = (natural[:, None] >= seq_ends[None, :]).astype(jnp.int32)
    seq_ids = jnp.sum(passed, axis=1)
    begins = jnp.sum(passed * padded[None, :], axis=1)
    owners = (seq_ids[:, None] == jnp.arange(lengths.shape[0], dtype=jnp.int32)[None, :]).astype(
        jnp.int32
    )
    own_length = jnp.sum(owners * lengths[None, :], axis=1)
    key_codes = jnp.where(natural - begins < own_length, seq_ids, -1)
    return (seq_ids, key_codes)


def to_half(value):
    return value.astype(jnp.bfloat16)


def exact_gelu(value):
    return jax.nn.gelu(value, approximate=False)


def split_heads(matrix):
    return matrix.reshape(matrix.shape[0], HEADS, HEAD_DIM)


def sub_width(rows):
    width = rows
    while width > 1024 and width % 2 == 0:
        width = width // 2
    return width


def add_rows(total, term, at_row):
    current = lax.dynamic_slice_in_dim(total, at_row, term.shape[0])
    return lax.dynamic_update_slice_in_dim(total, current + term, at_row, 0)


def norm_forward(residual, gain, shift):
    centre = residual - jnp.mean(residual, axis=-1, keepdims=True)
    spread = jnp.mean(centre * centre, axis=-1, keepdims=True)
    inverse = lax.rsqrt(spread + EPSILON)
    normed = centre * inverse
    return (normed * gain + shift, normed, inverse)


def norm_backward(upstream, gain, normed, inverse):
    scaled = upstream * gain
    across = jnp.mean(scaled, axis=-1, keepdims=True)
    along = jnp.mean(scaled * normed, axis=-1, keepdims=True)
    grad_residual = inverse * (scaled - across - normed * along)
    return (grad_residual, jnp.sum(upstream * normed, axis=0), jnp.sum(upstream, axis=0))


def score_grads(
    query_heads, grad_heads, key_part, value_part, query_ids, code_part, log_totals, delta, scale
):
    scores = (
        jnp.einsum("qhd,khd->hqk", query_heads, key_part, preferred_element_type=jnp.float32)
        * scale
    )
    scores = jnp.where((query_ids[:, None] == code_part[None, :])[None], scores, NEG_FILL)
    probs = jnp.exp(scores - log_totals[:, :, None])
    grad_probs = jnp.einsum(
        "qhd,khd->hqk", grad_heads, value_part, preferred_element_type=jnp.float32
    )
    grad_scores = (probs * (grad_probs - delta[:, :, None])).astype(jnp.bfloat16)
    return (probs, grad_scores)


def attend_forward(query_heads, query_ids, key_codes_all, scale, carry, piece):
    keys, values = piece
    rows = keys.shape[0]
    width = sub_width(rows)

    def one_block(state, offset):
        running, totals, accum = state
        key_part = split_heads(lax.dynamic_slice_in_dim(keys, offset, width))
        value_part = split_heads(lax.dynamic_slice_in_dim(values, offset, width))
        code_part = lax.dynamic_slice_in_dim(key_codes_all, offset, width)
        scores = (
            jnp.einsum("qhd,khd->hqk", query_heads, key_part, preferred_element_type=jnp.float32)
            * scale
        )
        scores = jnp.where((query_ids[:, None] == code_part[None, :])[None], scores, NEG_FILL)
        newest = jnp.maximum(running, jnp.max(scores, axis=-1))
        factor = jnp.exp(running - newest)
        weights = jnp.exp(scores - newest[:, :, None])
        totals = totals * factor + jnp.sum(weights, axis=-1)
        mixed = jnp.einsum(
            "hqk,khd->qhd",
            weights.astype(jnp.bfloat16),
            value_part,
            preferred_element_type=jnp.float32,
        )
        accum = accum * jnp.transpose(factor)[:, :, None] + mixed
        return ((newest, totals, accum), None)

    carry, unused = lax.scan(one_block, carry, jnp.arange(rows // width, dtype=jnp.int32) * width)
    return carry


def attend_back(
    query_heads, grad_heads, query_ids, key_codes_all, log_totals, delta, scale, carry, piece
):
    keys, values = piece
    rows = keys.shape[0]
    width = sub_width(rows)

    def one_block(state, offset):
        grad_query, grad_keys_all, grad_values_all = state
        key_part = split_heads(lax.dynamic_slice_in_dim(keys, offset, width))
        value_part = split_heads(lax.dynamic_slice_in_dim(values, offset, width))
        code_part = lax.dynamic_slice_in_dim(key_codes_all, offset, width)
        probs, grad_scores = score_grads(
            query_heads,
            grad_heads,
            key_part,
            value_part,
            query_ids,
            code_part,
            log_totals,
            delta,
            scale,
        )
        grad_query = (
            grad_query
            + jnp.einsum("hqk,khd->qhd", grad_scores, key_part, preferred_element_type=jnp.float32)
            * scale
        )
        key_term = (
            jnp.einsum("hqk,qhd->khd", grad_scores, query_heads, preferred_element_type=jnp.float32)
            * scale
        )
        value_term = jnp.einsum(
            "hqk,qhd->khd",
            probs.astype(jnp.bfloat16),
            grad_heads,
            preferred_element_type=jnp.float32,
        )
        grad_keys_all = add_rows(grad_keys_all, key_term.reshape(width, HEADS * HEAD_DIM), offset)
        grad_values_all = add_rows(
            grad_values_all, value_term.reshape(width, HEADS * HEAD_DIM), offset
        )
        return ((grad_query, grad_keys_all, grad_values_all), None)

    carry, unused = lax.scan(one_block, carry, jnp.arange(rows // width, dtype=jnp.int32) * width)
    return carry


def body(
    tokens,
    seq_lengths,
    deal,
    w_query,
    w_key,
    w_value,
    w_attn_out,
    b_query,
    b_value,
    b_attn_out,
    norm1_gain,
    norm1_bias,
    w_in,
    b_in,
    w_out,
    b_out,
    norm2_gain,
    norm2_bias,
    cotangent,
):
    gathered = (
        lax.all_gather(to_half(w_query), "fsdp", axis=0, tiled=True),
        lax.all_gather(to_half(w_key), "fsdp", axis=0, tiled=True),
        lax.all_gather(to_half(w_value), "fsdp", axis=0, tiled=True),
        lax.all_gather(to_half(w_attn_out), "fsdp", axis=0, tiled=True),
        lax.all_gather(to_half(b_query), "fsdp", axis=0, tiled=True),
        lax.all_gather(to_half(b_value), "fsdp", axis=0, tiled=True),
        lax.all_gather(to_half(b_attn_out), "fsdp", axis=0, tiled=True),
        lax.all_gather(to_half(norm1_gain), "fsdp", axis=0, tiled=True),
        lax.all_gather(to_half(norm1_bias), "fsdp", axis=0, tiled=True),
        lax.all_gather(to_half(w_in), "fsdp", axis=0, tiled=True),
        lax.all_gather(to_half(b_in), "fsdp", axis=0, tiled=True),
        lax.all_gather(to_half(w_out), "fsdp", axis=0, tiled=True),
        lax.all_gather(to_half(b_out), "fsdp", axis=0, tiled=True),
        lax.all_gather(to_half(norm2_gain), "fsdp", axis=0, tiled=True),
        lax.all_gather(to_half(norm2_bias), "fsdp", axis=0, tiled=True),
    )
    (
        query_weight,
        key_weight,
        value_weight,
        mix_weight,
        query_bias,
        value_bias,
        mix_bias,
        gain_one,
        shift_one,
        inner_weight,
        inner_bias,
        outer_weight,
        outer_bias,
        gain_two,
        shift_two,
    ) = gathered
    scale = HEAD_DIM ** (-0.5)
    inputs = tokens[0]
    rows = inputs.shape[0]
    query_ids_all, key_codes_all = block_codes(seq_lengths[0], deal[0])
    first_row = lax.axis_index("ctx") * rows
    query_ids = lax.dynamic_slice_in_dim(query_ids_all, first_row, rows)
    query = (
        jnp.dot(inputs, query_weight, preferred_element_type=jnp.float32)
        + query_bias.astype(jnp.float32)
    ).astype(jnp.bfloat16)
    keys = jnp.dot(inputs, key_weight, preferred_element_type=jnp.float32).astype(jnp.bfloat16)
    values = (
        jnp.dot(inputs, value_weight, preferred_element_type=jnp.float32)
        + value_bias.astype(jnp.float32)
    ).astype(jnp.bfloat16)
    query_heads = split_heads(query)
    start_state = (
        jnp.full((HEADS, rows), NEG_FILL, jnp.float32),
        jnp.zeros((HEADS, rows), jnp.float32),
        jnp.zeros((rows, HEADS, HEAD_DIM), jnp.float32),
    )
    running, totals, accum = attend_forward(
        query_heads,
        query_ids,
        key_codes_all,
        scale,
        start_state,
        (
            lax.all_gather(keys, "ctx", axis=0, tiled=True),
            lax.all_gather(values, "ctx", axis=0, tiled=True),
        ),
    )
    out_heads = accum / jnp.transpose(totals)[:, :, None]
    log_totals = running + jnp.log(totals)
    attn_in = out_heads.reshape(rows, HEADS * HEAD_DIM).astype(jnp.bfloat16)
    residual_one = (
        inputs.astype(jnp.float32)
        + jnp.dot(attn_in, mix_weight, preferred_element_type=jnp.float32)
        + mix_bias.astype(jnp.float32)
    )
    normal_one, normed_one, inverse_one = norm_forward(
        residual_one, gain_one.astype(jnp.float32), shift_one.astype(jnp.float32)
    )
    normal_half = normal_one.astype(jnp.bfloat16)
    pre_act = jnp.dot(
        normal_half, inner_weight, preferred_element_type=jnp.float32
    ) + inner_bias.astype(jnp.float32)
    activated, gelu_pull = jax.vjp(exact_gelu, pre_act)
    hidden = activated.astype(jnp.bfloat16)
    residual_two = (
        normal_one
        + jnp.dot(hidden, outer_weight, preferred_element_type=jnp.float32)
        + outer_bias.astype(jnp.float32)
    )
    layer_out, normed_two, inverse_two = norm_forward(
        residual_two, gain_two.astype(jnp.float32), shift_two.astype(jnp.float32)
    )
    upstream = cotangent[0].astype(jnp.float32)
    grad_two, grad_gain_two, grad_shift_two = norm_backward(
        upstream, gain_two.astype(jnp.float32), normed_two, inverse_two
    )
    grad_branch = grad_two.astype(jnp.bfloat16)
    grad_outer_bias = jnp.sum(grad_branch.astype(jnp.float32), axis=0)
    grad_outer = jnp.einsum("tf,td->fd", hidden, grad_branch, preferred_element_type=jnp.float32)
    grad_hidden = jnp.einsum(
        "td,fd->tf", grad_branch, outer_weight, preferred_element_type=jnp.float32
    )
    grad_pre = gelu_pull(grad_hidden)[0].astype(jnp.bfloat16)
    grad_inner_bias = jnp.sum(grad_pre.astype(jnp.float32), axis=0)
    grad_inner = jnp.einsum("td,tf->df", normal_half, grad_pre, preferred_element_type=jnp.float32)
    grad_normal = grad_two + jnp.einsum(
        "tf,df->td", grad_pre, inner_weight, preferred_element_type=jnp.float32
    )
    grad_one, grad_gain_one, grad_shift_one = norm_backward(
        grad_normal, gain_one.astype(jnp.float32), normed_one, inverse_one
    )
    grad_attn = grad_one.astype(jnp.bfloat16)
    grad_mix_bias = jnp.sum(grad_attn.astype(jnp.float32), axis=0)
    grad_mix = jnp.einsum("td,te->de", attn_in, grad_attn, preferred_element_type=jnp.float32)
    grad_mixed = jnp.einsum(
        "te,de->td", grad_attn, mix_weight, preferred_element_type=jnp.float32
    ).astype(jnp.bfloat16)
    grad_heads = split_heads(grad_mixed)
    delta = jnp.einsum("qhd,qhd->hq", grad_heads.astype(jnp.float32), out_heads)
    group_rows = key_codes_all.shape[0]
    start_back = (
        jnp.zeros((rows, HEADS, HEAD_DIM), jnp.float32),
        jnp.zeros((group_rows, HEADS * HEAD_DIM), jnp.float32),
        jnp.zeros((group_rows, HEADS * HEAD_DIM), jnp.float32),
    )
    grad_query_heads, grad_keys_all, grad_values_all = attend_back(
        query_heads,
        grad_heads,
        query_ids,
        key_codes_all,
        log_totals,
        delta,
        scale,
        start_back,
        (
            lax.all_gather(keys, "ctx", axis=0, tiled=True),
            lax.all_gather(values, "ctx", axis=0, tiled=True),
        ),
    )
    grad_keys_flat, grad_values_flat = (
        lax.psum_scatter(
            grad_keys_all.astype(jnp.bfloat16), "ctx", scatter_dimension=0, tiled=True
        ).astype(jnp.float32),
        lax.psum_scatter(
            grad_values_all.astype(jnp.bfloat16), "ctx", scatter_dimension=0, tiled=True
        ).astype(jnp.float32),
    )
    grad_query_half = grad_query_heads.reshape(rows, HEADS * HEAD_DIM).astype(jnp.bfloat16)
    grad_keys_half = grad_keys_flat.astype(jnp.bfloat16)
    grad_values_half = grad_values_flat.astype(jnp.bfloat16)
    grad_query_weight = jnp.einsum(
        "td,te->de", inputs, grad_query_half, preferred_element_type=jnp.float32
    )
    grad_key_weight = jnp.einsum(
        "td,te->de", inputs, grad_keys_half, preferred_element_type=jnp.float32
    )
    grad_value_weight = jnp.einsum(
        "td,te->de", inputs, grad_values_half, preferred_element_type=jnp.float32
    )
    grad_query_bias = jnp.sum(grad_query_half.astype(jnp.float32), axis=0)
    grad_value_bias = jnp.sum(grad_values_half.astype(jnp.float32), axis=0)
    grad_inputs = (
        grad_one
        + jnp.einsum("te,de->td", grad_query_half, query_weight, preferred_element_type=jnp.float32)
        + jnp.einsum("te,de->td", grad_keys_half, key_weight, preferred_element_type=jnp.float32)
        + jnp.einsum(
            "te,de->td", grad_values_half, value_weight, preferred_element_type=jnp.float32
        )
    )
    shares = (
        lax.psum_scatter(
            grad_query_weight.astype(jnp.bfloat16), "fsdp", scatter_dimension=0, tiled=True
        ).astype(jnp.float32),
        lax.psum_scatter(
            grad_key_weight.astype(jnp.bfloat16), "fsdp", scatter_dimension=0, tiled=True
        ).astype(jnp.float32),
        lax.psum_scatter(
            grad_value_weight.astype(jnp.bfloat16), "fsdp", scatter_dimension=0, tiled=True
        ).astype(jnp.float32),
        lax.psum_scatter(
            grad_mix.astype(jnp.bfloat16), "fsdp", scatter_dimension=0, tiled=True
        ).astype(jnp.float32),
        lax.psum_scatter(
            grad_query_bias.astype(jnp.bfloat16), "fsdp", scatter_dimension=0, tiled=True
        ).astype(jnp.float32),
        lax.psum_scatter(
            grad_value_bias.astype(jnp.bfloat16), "fsdp", scatter_dimension=0, tiled=True
        ).astype(jnp.float32),
        lax.psum_scatter(
            grad_mix_bias.astype(jnp.bfloat16), "fsdp", scatter_dimension=0, tiled=True
        ).astype(jnp.float32),
        lax.psum_scatter(
            grad_gain_one.astype(jnp.bfloat16), "fsdp", scatter_dimension=0, tiled=True
        ).astype(jnp.float32),
        lax.psum_scatter(
            grad_shift_one.astype(jnp.bfloat16), "fsdp", scatter_dimension=0, tiled=True
        ).astype(jnp.float32),
        lax.psum_scatter(
            grad_inner.astype(jnp.bfloat16), "fsdp", scatter_dimension=0, tiled=True
        ).astype(jnp.float32),
        lax.psum_scatter(
            grad_inner_bias.astype(jnp.bfloat16), "fsdp", scatter_dimension=0, tiled=True
        ).astype(jnp.float32),
        lax.psum_scatter(
            grad_outer.astype(jnp.bfloat16), "fsdp", scatter_dimension=0, tiled=True
        ).astype(jnp.float32),
        lax.psum_scatter(
            grad_outer_bias.astype(jnp.bfloat16), "fsdp", scatter_dimension=0, tiled=True
        ).astype(jnp.float32),
        lax.psum_scatter(
            grad_gain_two.astype(jnp.bfloat16), "fsdp", scatter_dimension=0, tiled=True
        ).astype(jnp.float32),
        lax.psum_scatter(
            grad_shift_two.astype(jnp.bfloat16), "fsdp", scatter_dimension=0, tiled=True
        ).astype(jnp.float32),
    )
    summed = (
        lax.psum(shares[0].astype(jnp.bfloat16), "ctx").astype(jnp.float32),
        lax.psum(shares[1].astype(jnp.bfloat16), "ctx").astype(jnp.float32),
        lax.psum(shares[2].astype(jnp.bfloat16), "ctx").astype(jnp.float32),
        lax.psum(shares[3].astype(jnp.bfloat16), "ctx").astype(jnp.float32),
        lax.psum(shares[4].astype(jnp.bfloat16), "ctx").astype(jnp.float32),
        lax.psum(shares[5].astype(jnp.bfloat16), "ctx").astype(jnp.float32),
        lax.psum(shares[6].astype(jnp.bfloat16), "ctx").astype(jnp.float32),
        lax.psum(shares[7].astype(jnp.bfloat16), "ctx").astype(jnp.float32),
        lax.psum(shares[8].astype(jnp.bfloat16), "ctx").astype(jnp.float32),
        lax.psum(shares[9].astype(jnp.bfloat16), "ctx").astype(jnp.float32),
        lax.psum(shares[10].astype(jnp.bfloat16), "ctx").astype(jnp.float32),
        lax.psum(shares[11].astype(jnp.bfloat16), "ctx").astype(jnp.float32),
        lax.psum(shares[12].astype(jnp.bfloat16), "ctx").astype(jnp.float32),
        lax.psum(shares[13].astype(jnp.bfloat16), "ctx").astype(jnp.float32),
        lax.psum(shares[14].astype(jnp.bfloat16), "ctx").astype(jnp.float32),
    )
    return (
        layer_out.astype(jnp.bfloat16)[None],
        grad_inputs[None],
        summed[0],
        summed[1],
        summed[2],
        summed[3],
        summed[4],
        summed[5],
        summed[6],
        summed[7],
        summed[8],
        summed[9],
        summed[10],
        summed[11],
        summed[12],
        summed[13],
        summed[14],
    )


MESH=pl.DeviceIdType.MESH
F32=jnp.float32; BF=jnp.bfloat16

def places():
    c=lax.axis_index("ctx"); f=lax.axis_index("fsdp")
    z=c//2; x=c%2; y=f//2; k=f%2
    return c,f,z,x,y,k

def add_strips(rows, fn, step=16):
    @pl.loop(0, rows//step)
    def _(i):
        fn(pl.ds(pl.multiple_of(i*step,step),step))

def remote_copy(src, dst, send, recv, device):
    return pltpu.make_async_remote_copy(
        src_ref=src,
        dst_ref=dst,
        send_sem=send,
        recv_sem=recv,
        device_id=device,
        device_id_type=MESH,
    )


def greet(peers):
    barrier = pltpu.get_barrier_semaphore()
    for peer in peers:
        pl.semaphore_signal(barrier, inc=1, device_id=peer, device_id_type=MESH)
    pl.semaphore_wait(barrier, len(peers))


def at_row(value, size):
    return pl.ds(pl.multiple_of(value, 16), size)


def window_start(part):
    return 192 * part - 64 * (part % 2)


def lane_windows(parts):
    first, second, third, fourth = parts
    return jnp.concatenate(
        [
            first[:, :128],
            first[:, 128:] + second[:, :128],
            second[:, 128:],
            third[:, :128],
            third[:, 128:] + fourth[:, :128],
            fourth[:, 128:],
        ],
        axis=1,
    )


def any_specs(count):
    return [pl.BlockSpec(memory_space=pl.ANY)] * count


def vmem_specs(count):
    return [pl.BlockSpec(memory_space=pltpu.VMEM)] * count


def half(*shape):
    return jax.ShapeDtypeStruct(shape, jnp.bfloat16)


def full(*shape):
    return jax.ShapeDtypeStruct(shape, jnp.float32)


def pick(parity, value_side, by_window):
    shape = (384, 256) if not by_window else (256, 384)
    spread = lax.broadcasted_iota(jnp.int32, shape, 0 if not by_window else 1)
    window = lax.broadcasted_iota(jnp.int32, shape, 1 if not by_window else 0)
    lane = spread % 128
    low = 64 if value_side else 0
    target = (spread // 128) * 64 + (lane - low) + 64 * parity
    inside = (lane >= low) & (lane < low + 64)
    return jnp.where(inside & (target == window), 1.0, 0.0)


def dot_nt(left, right):
    return lax.dot_general(
        left, right, (((1,), (1,)), ((), ())), preferred_element_type=jnp.float32
    )


class Reducer:
    def __init__(self, chunks, ins, outs, scr):
        n = len(chunks)
        self.chunks, self.ins, self.outs, self.n = chunks, ins, outs, n
        groups = [scr[n * i : n * (i + 1)] for i in range(8)]
        self.loc, self.rc, self.ry, self.rx, self.cb, self.rz, self.re, self.res = groups
        self.sems = scr[8 * n :]
        c, f, z, x, y, k = places()
        self.side = jnp.where((z == 1) | (z == 2), 1, 0)
        self.deep = z // 2
        self.near = ((z + 1 - 2 * (z % 2)) * 2 + x, f)
        self.far = ((3 - z) * 2 + x, f)
        self.z, self.x, self.y, self.k = z, x, y, k
        self.sib = (c, y * 2 + (1 - k))
        self.yp = (c, (1 - y) * 2 + k)
        self.xp = (z * 2 + (1 - x), f)

    def slab(self, i, f):
        m, slab = self.chunks[i][:2]
        return slab(self.ins[m], f)

    def load(self, i, yy):
        sem = self.sems[0].at[i, yy]
        return pltpu.make_async_copy(self.slab(i, yy * 2 + self.k), self.loc[i].at[yy], sem)

    def core(self, i, yy):
        src = self.slab(i, yy * 2 + (1 - self.k))
        send, recv = self.sems[2].at[i, yy], self.sems[3].at[i, yy]
        return remote_copy(src, self.rc[i].at[yy], send, recv, self.sib)

    def over_y(self, i):
        send, recv = self.sems[4].at[i], self.sems[5].at[i]
        return remote_copy(self.loc[i].at[1 - self.y], self.ry[i], send, recv, self.yp)

    def lanes(self, i, xx):
        wide = self.chunks[i][5] // 2
        return pl.ds(pl.multiple_of(xx * wide, 128), wide)

    def span(self, i, side, deep=None):
        high = self.chunks[i][4]
        if deep is None:
            return pl.ds(pl.multiple_of(side * (high // 2), high // 2), high // 2)
        base = side * (high // 2) + deep * (high // 4)
        return pl.ds(pl.multiple_of(base, high // 4), high // 4)

    def over_x(self, i):
        src = self.loc[i].at[self.y, :, self.lanes(i, 1 - self.x)]
        send, recv = self.sems[6].at[i], self.sems[7].at[i]
        return remote_copy(src, self.rx[i], send, recv, self.xp)

    def to_near(self, i):
        src = self.cb[i].at[self.span(i, 1 - self.side)]
        send, recv = self.sems[8].at[i], self.sems[9].at[i]
        return remote_copy(src, self.rz[i], send, recv, self.near)

    def to_far(self, i):
        src = self.cb[i].at[self.span(i, self.side, 1 - self.deep)]
        send, recv = self.sems[10].at[i], self.sems[11].at[i]
        return remote_copy(src, self.re[i], send, recv, self.far)

    def share_far(self, i, deep):
        ref = self.res[i].at[self.x, self.span(i, self.side, deep)]
        send, recv = self.sems[14].at[i], self.sems[15].at[i]
        return remote_copy(ref, ref, send, recv, self.far)

    def share_near(self, i, side):
        ref = self.res[i].at[self.x, self.span(i, side)]
        send, recv = self.sems[16].at[i], self.sems[17].at[i]
        return remote_copy(ref, ref, send, recv, self.near)

    def share_x(self, i, xx):
        ref = self.res[i].at[xx]
        send, recv = self.sems[12].at[i], self.sems[13].at[i]
        return remote_copy(ref, ref, send, recv, self.xp)

    def out(self, i, xx):
        m, home = self.chunks[i][2:4]
        sem = self.sems[1].at[i, xx]
        return pltpu.make_async_copy(self.res[i].at[xx], home(self.outs[m], xx), sem)

    def start(self, i):
        for yy in (0, 1):
            self.core(i, yy).start()
            self.load(i, yy).start()

    def stage0(self, i):
        for yy in (0, 1):
            self.load(i, yy).wait()
            self.core(i, yy).wait()

        def add(s):
            for yy in (0, 1):
                total = self.loc[i][yy, s].astype(jnp.float32) + self.rc[i][yy, s].astype(jnp.float32)
                self.loc[i][yy, s] = total.astype(jnp.bfloat16)

        add_strips(self.chunks[i][4], add)
        self.over_y(i).start()

    def stage1(self, i):
        self.over_y(i).wait()

        def add(s):
            total = self.loc[i][self.y, s].astype(jnp.float32) + self.ry[i][s].astype(jnp.float32)
            self.loc[i][self.y, s] = total.astype(jnp.bfloat16)

        add_strips(self.chunks[i][4], add)
        self.over_x(i).start()

    def stage2(self, i):
        self.over_x(i).wait()
        mine = self.lanes(i, self.x)

        def add(s):
            total = self.loc[i][self.y, s, mine].astype(jnp.float32) + self.rx[i][s].astype(jnp.float32)
            self.cb[i][s] = total.astype(jnp.bfloat16)

        add_strips(self.chunks[i][4], add)
        self.to_near(i).start()

    def stage3(self, i):
        self.to_near(i).wait()
        high = self.chunks[i][4] // 2

        @pl.loop(0, high // 16)
        def _(j):
            own = pl.ds(pl.multiple_of(self.side * high + j * 16, 16), 16)
            s = pl.ds(pl.multiple_of(j * 16, 16), 16)
            total = self.cb[i][own].astype(jnp.float32) + self.rz[i][s].astype(jnp.float32)
            self.cb[i][own] = total.astype(jnp.bfloat16)

        self.to_far(i).start()

    def stage4(self, i):
        self.to_far(i).wait()
        high = self.chunks[i][4] // 4

        @pl.loop(0, high // 16)
        def _(j):
            base = self.side * (2 * high) + self.deep * high + j * 16
            own = pl.ds(pl.multiple_of(base, 16), 16)
            s = pl.ds(pl.multiple_of(j * 16, 16), 16)
            total = self.cb[i][own].astype(jnp.float32) + self.re[i][s].astype(jnp.float32)
            self.res[i][self.x, own] = total.astype(jnp.bfloat16)

        self.share_far(i, self.deep).start()

    def stage5(self, i):
        self.share_far(i, self.deep).wait_send()
        self.share_far(i, 1 - self.deep).wait_recv()
        self.share_near(i, self.side).start()

    def stage6(self, i):
        self.share_near(i, self.side).wait_send()
        self.share_near(i, 1 - self.side).wait_recv()
        self.share_x(i, self.x).start()
        self.out(i, self.x).start()

    def stage7(self, i):
        self.share_x(i, self.x).wait_send()
        self.share_x(i, 1 - self.x).wait_recv()
        self.out(i, 1 - self.x).start()

    def tick(self, t):
        for lag, stage in (
            (0, self.stage0),
            (8, self.stage7),
            (7, self.stage6),
            (6, self.stage5),
            (5, self.stage4),
            (4, self.stage3),
            (3, self.stage2),
            (2, self.stage1),
        ):
            if 0 <= t - lag < self.n:
                stage(t - lag)

    def finish(self):
        for i in range(self.n):
            for xx in (0, 1):
                self.out(i, xx).wait()


def reduce_plan(shapes):
    chunks = []
    for m, (rows, width) in enumerate(shapes):
        shard = rows // 4
        high = min(shard, 192)
        wide = min(width, 768)
        for i in range(shard // high):
            for j in range(width // wide):

                def slab(ref, f, i=i, j=j, shard=shard, high=high, wide=wide):
                    rows = pl.ds(pl.multiple_of(f * shard + i * high, high), high)
                    return ref.at[rows, pl.ds(j * wide, wide)]

                def home(ref, xx, i=i, j=j, high=high, wide=wide):
                    lanes = pl.ds(pl.multiple_of(j * wide + xx * (wide // 2), 128), wide // 2)
                    return ref.at[pl.ds(i * high, high), lanes]

                chunks.append((m, slab, m, home, high, wide))
    return chunks


def reduce_scratch(chunks):
    scratch = []
    for lead, divide_rows, divide_lanes in (
        ((2,), 1, 1),
        ((2,), 1, 1),
        ((), 1, 1),
        ((), 1, 2),
        ((), 1, 2),
        ((), 2, 2),
        ((), 4, 2),
        ((2,), 1, 2),
    ):
        for item in chunks:
            shape = lead + (item[4] // divide_rows, item[5] // divide_lanes)
            scratch.append(pltpu.VMEM(shape, jnp.bfloat16))
    for lanes in (2, 2, 2, 2) + (1,) * 14:
        shape = (len(chunks), lanes) if lanes > 1 else (len(chunks),)
        scratch.append(pltpu.SemaphoreType.DMA(shape))
    return scratch


def split_pairs():
    src = lax.broadcasted_iota(jnp.int32, (256, 256), 0)
    dst = lax.broadcasted_iota(jnp.int32, (256, 256), 1)
    piece = src // 64
    moved = (piece % 2) * 128 + (piece // 2) * 64 + src % 64
    return jnp.where(moved == dst, 1.0, 0.0).astype(jnp.bfloat16)


def dot_tn(left, right):
    return lax.dot_general(
        left, right, (((0,), (0,)), ((), ())), preferred_element_type=jnp.float32
    )


def backward_kernel(chunks, *refs):
    deal, lengths, seqs = refs[:3]
    refs = refs[1:]
    (gm, qg_h, os_h, lse_h, kvn_h, kvt_h, tok_h, wq_h, wk_h, wv_h, gone_h, gout, gin, gmix) = refs[2:16]
    small_h = refs[16:23]
    gtok = refs[23]
    outs = refs[24:31]
    (qg, osave, lse, kvn, kvt, tok, wq, wk, wv, gone) = refs[31:41]
    small = refs[41:48]
    gvec = refs[48]
    (dog, qt, dot_t, qd, acc, dqw, give, theirs, mine, got_q, got_kv, gq, gk, gv, tok_out) = refs[49:64]
    (load_sem, o_s, o_r, o_l, q_s, q_r, q_l, x_s, x_r, k_s, k_r, k_l, t_l) = refs[64:77]
    ins = (gout, gin, gmix, gq, gk, gv, gvec)
    red = Reducer(chunks, ins, outs, refs[77:])
    c, f, z, x, y, k = places()
    zt = [(z + d) % 4 for d in (1, 2, 3)]
    zp = [(item * 2 + x, f) for item in zt]
    xp = red.xp
    loads = [
        pltpu.make_async_copy(src, dst, load_sem.at[i])
        for i, (src, dst) in enumerate(
            (
                (qg_h, qg),
                (kvn_h, kvn),
                (kvt_h, kvt),
                (os_h, osave),
                (lse_h, lse),
                (tok_h, tok),
                (wq_h, wq),
                (wk_h, wk),
                (wv_h, wv),
                (gone_h, gone),
            )
            + tuple(zip(small_h, small))
        )
    ]
    for item in loads[:5]:
        item.start()
    greet([red.sib, red.yp, xp] + zp)

    def window(part):
        return pl.ds(pl.multiple_of(window_start(part), 128), 256)

    def o_copy(d):
        return remote_copy(gm.at[:, window(zt[d])], dog.at[z], o_s.at[d], o_r.at[d], zp[d])

    for d in (1, 0, 2):
        o_copy(d).start()
    keep_o = pltpu.make_async_copy(gm.at[:, window(z)], dog.at[z], o_l)
    keep_o.start()
    for i in range(3):
        red.start(i)
    red.tick(0)
    red.start(3)
    red.tick(1)
    red.start(4)
    for item in loads[5:]:
        item.start()

    scale = HEAD_DIM ** (-0.5)
    span = 1024
    spread_q = (pick(z % 2, False, False) * scale).astype(jnp.bfloat16)
    spread_o = pick(z % 2, True, False).astype(jnp.bfloat16)
    gather_q = pick(z % 2, False, False).astype(jnp.bfloat16)

    def place(b):
        return seqs[((b // 2) * 2 + x) * 2 + b % 2]

    def masked(rows, b, base):
        later = place(b).astype(jnp.float32)
        for s in range(2):
            keep = later if s == 1 else 1.0 - later
            kept = (rows * keep).astype(jnp.bfloat16)
            for h in range(3):
                qd[b, pl.ds(base, BLOCK), pl.ds(256 * h + 128 * s, 128)] = kept[
                    :, 128 * h : 128 * (h + 1)
                ]

    loads[0].wait()
    for part in range(4):
        qt[:, pl.ds(256 * part, 256)] = dot_nt(spread_q, qg[part]).astype(jnp.bfloat16)
        rows = dot_nt(qg[part], spread_q)
        for i in range(2):
            masked(rows[i * BLOCK : (i + 1) * BLOCK], 2 * part + i, 0)
    for h in range(3):
        acc[h] = jnp.zeros(acc.shape[1:], jnp.float32)
    red.tick(2)
    red.start(5)
    keep_o.wait()
    for d in range(3):
        o_copy(d).wait()
    for part in range(4):
        dot_t[:, pl.ds(256 * part, 256)] = dot_nt(spread_o, dog[part]).astype(jnp.bfloat16)
        rows = dot_nt(dog[part], spread_o)
        for i in range(2):
            masked(rows[i * BLOCK : (i + 1) * BLOCK], 2 * part + i, BLOCK)
    for item in loads[1:5]:
        item.wait()
    red.tick(3)
    red.start(6)

    def pair(p):
        key_rows = lax.broadcasted_iota(jnp.int32, (span, BLOCK), 0)
        made = ([], [])
        for h in range(3):
            lanes = pl.ds(128 * h, 128)
            both = []
            for i in range(2):
                b = 2 * p + i
                seq = place(b)
                length = lengths[seq]
                here = pl.ds(pl.multiple_of(b * BLOCK, BLOCK), BLOCK)
                part = kvn[h, seq]
                scores = jnp.dot(part, qt[lanes, here], preferred_element_type=jnp.float32)
                scores = jnp.where(key_rows < length, scores, NEG_FILL)
                probs = jnp.exp(scores - lse[h, b, 0:1, :])
                upstream = dot_t[lanes, here]
                grad_probs = jnp.dot(part, upstream, preferred_element_type=jnp.float32)
                delta = jnp.sum(
                    osave[h, b] * upstream[64:].astype(jnp.float32), axis=0, keepdims=True
                )
                grad_scores = (probs * (grad_probs - delta)).astype(jnp.bfloat16)
                grad_query = jnp.dot(
                    kvt[h, seq], grad_scores, preferred_element_type=jnp.float32
                )
                made[i].append((jnp.transpose(grad_query) * scale).astype(jnp.bfloat16))
                both += [grad_scores, probs.astype(jnp.bfloat16)]
            right = jnp.concatenate(
                [qd[2 * p, :, pl.ds(256 * h, 256)], qd[2 * p + 1, :, pl.ds(256 * h, 256)]], axis=0
            )
            found = jnp.dot(
                jnp.concatenate(both, axis=1), right, preferred_element_type=jnp.float32
            )
            acc[h, pl.ds(0, 8)] += found[:, :128].reshape(8, BLOCK, 128)
            acc[h, pl.ds(8, 8)] += found[:, 128:].reshape(8, BLOCK, 128)
        for i in range(2):
            dqw[p, pl.ds(i * BLOCK, BLOCK), :] = jnp.dot(
                jnp.concatenate(made[i], axis=1), gather_q, preferred_element_type=jnp.float32
            ).astype(jnp.bfloat16)

    pl.loop(0, 3)(pair)
    red.tick(4)
    red.start(7)
    pl.loop(3, 4)(pair)

    def q_copy(d):
        return remote_copy(dqw.at[zt[d]], got_q.at[z], q_s.at[d], q_r.at[d], zp[d])

    for d in (1, 0, 2):
        q_copy(d).start()
    keep_q = pltpu.make_async_copy(dqw.at[z], got_q.at[z], q_l)
    keep_q.start()
    order = [zt[1], zt[0], zt[2], z]
    where = [1, 0, 2]

    def over_x(i):
        return remote_copy(give.at[i], theirs.at[i], x_s.at[i], x_r.at[i], xp)

    def collect(out, i, part, xx):
        for j in range(2):
            natural = deal[(part * 2 + xx) * 2 + j]
            for h in range(3):
                out[i, pl.ds(j * BLOCK, BLOCK), pl.ds(128 * h, 128)] = acc[
                    h, natural
                ].astype(jnp.bfloat16)

    for i in range(4):
        collect(give, i, order[i], 1 - x)
        over_x(i).start()
    red.tick(5)
    red.start(8)
    for i in range(4):
        collect(mine, i, order[i], x)

    def kv_copy(i):
        d = where[i]
        return remote_copy(mine.at[i], got_kv.at[z], k_s.at[d], k_r.at[d], zp[d])

    for i in range(4):
        over_x(i).wait_recv()

        @pl.loop(0, 16)
        def _(j, i=i):
            rows = pl.ds(pl.multiple_of(j * 16, 16), 16)
            mine[i, rows] = (
                mine[i, rows].astype(jnp.float32) + theirs[i, rows].astype(jnp.float32)
            ).astype(jnp.bfloat16)

        if i < 3:
            kv_copy(i).start()
        if i == 1:
            red.tick(6)
    keep_kv = pltpu.make_async_copy(mine.at[3], got_kv.at[z], k_l)
    keep_kv.start()
    keep_q.wait()
    for d in range(3):
        q_copy(d).wait()
    for item in loads[5:]:
        item.wait()
    dq = lane_windows([got_q[part] for part in range(4)])
    tokens = tok[...]
    gq[...] = dot_tn(tokens, dq).astype(jnp.bfloat16)
    red.start(9)
    total = gone[...] + dot_nt(dq, wq[...])
    red.tick(7)
    keep_kv.wait()
    for i in range(3):
        kv_copy(i).wait()
    split = split_pairs()
    keys, values = [], []
    joined = jnp.concatenate([got_kv[part] for part in range(4)], axis=1)
    for i in range(6):
        apart = jnp.dot(
            joined[:, 256 * i : 256 * (i + 1)], split, preferred_element_type=jnp.float32
        ).astype(jnp.bfloat16)
        keys.append(apart[:, :128])
        values.append(apart[:, 128:])
    dk = jnp.concatenate(keys, axis=1)
    dv = jnp.concatenate(values, axis=1)
    gk[...] = dot_tn(tokens, dk).astype(jnp.bfloat16)
    red.start(10)
    gv[...] = dot_tn(tokens, dv).astype(jnp.bfloat16)
    red.start(11)
    q_bias = jnp.sum(dq.astype(jnp.float32), axis=0, keepdims=True)
    v_bias = jnp.sum(dv.astype(jnp.float32), axis=0, keepdims=True)
    line = lax.broadcasted_iota(jnp.int32, (16, 256), 0)
    lines = [q_bias, v_bias] + [item[...] for item in small[:6]]
    for part in range(4):
        lanes = slice(window_start(part), window_start(part) + 256)
        top = jnp.zeros((16, 256), jnp.float32)
        for i, item in enumerate(lines):
            top = jnp.where(line == i, item[:, lanes], top)
        for i in range(3):
            base = 768 * part + 256 * i
            top = jnp.where(line == 8 + i, small[6][:, base : base + 256], top)
        gvec[pl.ds(64 * part, 16), :] = top.astype(jnp.bfloat16)
        gvec[pl.ds(64 * part + 16, 48), :] = jnp.zeros((48, 256), jnp.bfloat16)
    red.start(12)
    tok_out[...] = total + dot_nt(dk, wk[...]) + dot_nt(dv, wv[...])
    keep_tok = pltpu.make_async_copy(tok_out, gtok, t_l)
    keep_tok.start()
    for t in range(8, red.n + 8):
        red.tick(t)
    red.finish()
    keep_tok.wait()
    for i in range(4):
        over_x(i).wait_send()


def backward(deal, lengths, seqs, gm, qg, osave, lse, kvn, kvt, tok, wq, wk, wv, gone, gout, gin, gmix, small):
    chunks = reduce_plan(
        [gout.shape, gin.shape, gmix.shape, (768, 768), (768, 768), (768, 768), (256, 256)]
    )
    bf, f32, d = jnp.bfloat16, jnp.float32, pltpu.SemaphoreType.DMA
    v = pltpu.VMEM
    scratch = [
        v((4, 256, 256), bf),
        v((3, 8, 64, BLOCK), f32),
        v((3, 8, 8, BLOCK), f32),
        v((3, 2, 1024, 128), bf),
        v((3, 2, 128, 1024), bf),
        v((256, 768), bf),
        v((768, 768), bf),
        v((768, 768), bf),
        v((768, 768), bf),
        v((256, 768), f32),
    ]
    scratch += [v(item.shape, f32) for item in small]
    scratch += [
        v((256, 256), bf),
        v((4, 256, 256), bf),
        v((384, 1024), bf),
        v((384, 1024), bf),
        v((8, 256, 768), bf),
        v((3, 16, BLOCK, 128), f32),
        v((4, 256, 256), bf),
        v((4, 256, 384), bf),
        v((4, 256, 384), bf),
        v((4, 256, 384), bf),
        v((4, 256, 256), bf),
        v((4, 256, 384), bf),
        v((768, 768), bf),
        v((768, 768), bf),
        v((768, 768), bf),
        v((256, 768), f32),
        d((17,)),
        d((3,)),
        d((3,)),
        d,
        d((3,)),
        d((3,)),
        d,
        d((4,)),
        d((4,)),
        d((3,)),
        d((3,)),
        d,
        d,
    ]
    return pl.pallas_call(
        functools.partial(backward_kernel, chunks),
        out_shape=[
            full(256, 768),
            half(768, 768),
            half(192, 3072),
            half(192, 768),
            half(192, 768),
            half(192, 768),
            half(192, 768),
            half(64, 256),
        ],
        in_specs=[pl.BlockSpec(memory_space=pltpu.SMEM)] * 3 + any_specs(21),
        out_specs=any_specs(8),
        scratch_shapes=scratch + reduce_scratch(chunks),
        compiler_params=pltpu.CompilerParams(
            collective_id=6, has_side_effects=True, vmem_limit_bytes=60 * 2**20
        ),
        cost_estimate=pl.CostEstimate(flops=10**10, bytes_accessed=10**8, transcendentals=3 * 10**6),
        name="backward",
    )(deal, lengths, seqs, gm, qg, osave, lse, kvn, kvt, tok, wq, wk, wv, gone, gout, gin, gmix, *small)


GATHER_PIECES = ((True, 3), (True, 3), (True, 3), (True, 2), (False, 1), (False, 4))


def forward_kernel(*refs):
    deal, lengths = refs[:2]
    tok_h = refs[2]
    shard_h = refs[3:9]
    small_h = refs[9:18]
    (attn_o, qg_o, kvn_o, kvt_o, os_o, lse_o, wq_o, wk_o, wv_o, wo_o, win_o, wout_o, vec_o, bin_o) = refs[18:32]
    tok = refs[32]
    stage = refs[33:39]
    small = refs[39:48]
    (wk_v, wv_v, wq_v, sh_in, sh_mix, sh_out, vec_v, vec_all, bin_all) = refs[48:57]
    (send_kv, send_q, kvg, qg, kvn, kvt, qt, owin, got, osave, lse, attn) = refs[57:69]
    (load_sem, own_s, own_r, own_l, y_s, y_r, cy_s, cy_r, x_s, x_r, cx_s, cx_r) = refs[69:81]
    (v_s, v_r, zk_s, zk_r, zq_s, zq_r, f_s, f_r, l_sem, o_s, o_r, out_sem) = refs[81:]
    c, f, z, x, y, k = places()
    sib = (c, y * 2 + (1 - k))
    yp = (c, (1 - y) * 2 + k)
    diag = (c, (1 - y) * 2 + (1 - k))
    xp = (z * 2 + (1 - x), f)
    zt = [(z + d) % 4 for d in (1, 2, 3)]
    zp = [(item * 2 + x, f) for item in zt]
    loads = [
        pltpu.make_async_copy(src, dst, load_sem.at[i])
        for i, (src, dst) in enumerate(
            tuple(zip(shard_h[:3], stage[:3]))
            + ((tok_h, tok),)
            + tuple(zip(small_h, small))
            + tuple(zip(shard_h[3:], stage[3:]))
        )
    ]
    for item in loads:
        item.start()
    greet([sib, yp, diag, xp] + zp)
    wholes = (wk_v, wv_v, wq_v, win_o, wo_o, wout_o)
    fy = (1 - y) * 2 + k
    first = [0]
    for split, count in GATHER_PIECES:
        first.append(first[-1] + count)
    heights = [item.shape[0] for item in stage]
    shards = [wholes[u].at[at_row(f * heights[u], heights[u])] for u in range(3)]
    shards += [sh_in, sh_mix, sh_out]

    def piece_rows(u, j, xx):
        rows = heights[u]
        split, count = GATHER_PIECES[u]
        if split:
            size = rows // 2 // count
            return xx * (rows // 2) + j * size, size
        size = rows // count
        return j * size, size

    def home(u):
        return wholes[u].at[at_row(f * heights[u], heights[u])]

    def own(u):
        return remote_copy(shards[u], home(u), own_s.at[u], own_r.at[u], sib)

    def keep(u):
        return pltpu.make_async_copy(shards[u], home(u), own_l.at[u])

    def over_y(u, j):
        start, size = piece_rows(u, j, x)
        i = first[u] + j
        if u < 3:
            src = wholes[u].at[at_row(f * heights[u] + start, size)]
        else:
            src = shards[u].at[at_row(start, size)]
        dst = wholes[u].at[at_row(f * heights[u] + start, size)]
        return remote_copy(src, dst, y_s.at[i], y_r.at[i], yp)

    def landed(u, j, xx):
        start, size = piece_rows(u, j, xx)
        return wholes[u].at[at_row(fy * heights[u] + start, size)]

    def relay_core(u, j):
        i = first[u] + j
        ref = landed(u, j, x)
        return remote_copy(ref, ref, cy_s.at[i], cy_r.at[i], sib)

    def relay_x(u, j):
        i = first[u] + j
        ref = landed(u, j, x)
        return remote_copy(ref, ref, x_s.at[i], x_r.at[i], xp)

    def relay_core_x(u, j):
        i = first[u] + j
        ref = landed(u, j, 1 - x)
        return remote_copy(ref, ref, cx_s.at[i], cx_r.at[i], sib)

    def pieces(u):
        return range(GATHER_PIECES[u][1])

    def on_y(u, j):
        over_y(u, j).wait_recv()
        if GATHER_PIECES[u][0]:
            relay_x(u, j).start()
        relay_core(u, j).start()

    def on_x(u, j):
        if GATHER_PIECES[u][0]:
            relay_x(u, j).wait_recv()
            relay_core_x(u, j).start()

    def finish_recv(u):
        own(u).wait_recv()
        if u >= 3:
            keep(u).wait()
        for j in pieces(u):
            relay_core(u, j).wait_recv()
            if GATHER_PIECES[u][0]:
                relay_core_x(u, j).wait_recv()

    def finish_send(u):
        own(u).wait_send()
        for j in pieces(u):
            over_y(u, j).wait_send()
            relay_core(u, j).wait_send()
            if GATHER_PIECES[u][0]:
                relay_x(u, j).wait_send()
                relay_core_x(u, j).wait_send()

    def cast(u):
        rows = heights[u]

        @pl.loop(0, rows // 32)
        def _(i):
            here = pl.ds(pl.multiple_of(i * 32, 32), 32)
            value = stage[u][here, :].astype(jnp.bfloat16)
            if u < 3:
                wholes[u][at_row(f * rows + i * 32, 32), :] = value
            else:
                shards[u][here, :] = value

    for u in range(3):
        loads[u].wait()
        cast(u)
        for j in pieces(u):
            over_y(u, j).start()
        own(u).start()
    for item in loads[4:13]:
        item.wait()
    line = lax.broadcasted_iota(jnp.int32, (16, 192), 0)
    rows = jnp.zeros((16, 192), jnp.float32)
    for i in range(8):
        rows = jnp.where(line == i, small[i][...], rows)
    widen = jnp.where(
        lax.broadcasted_iota(jnp.int32, (192, 256), 0)
        == lax.broadcasted_iota(jnp.int32, (192, 256), 1),
        1.0,
        0.0,
    ).astype(jnp.bfloat16)
    rows = jnp.dot(rows.astype(jnp.bfloat16), widen, preferred_element_type=jnp.float32)
    line = lax.broadcasted_iota(jnp.int32, (16, 256), 0)
    for i in range(3):
        rows = jnp.where(line == 8 + i, small[8][:, 256 * i : 256 * (i + 1)], rows)
    vec_v[f] = rows.astype(jnp.bfloat16)

    def vec(i, device):
        return remote_copy(vec_v.at[f], vec_v.at[f], v_s.at[i], v_r.at[i], device)

    vec_peers = (sib, yp, diag)
    vec_from = (y * 2 + (1 - k), fy, (1 - y) * 2 + (1 - k))

    def vec_in(i):
        slot = vec_v.at[vec_from[i]]
        return remote_copy(slot, slot, v_s.at[i], v_r.at[i], vec_peers[i])

    for i in range(3):
        vec(i, vec_peers[i]).start()
    for n, u in enumerate((3, 4, 5)):
        loads[13 + n].wait()
        cast(u)
        own(u).start()
        keep(u).start()
    for i in range(3):
        vec_in(i).wait_recv()
    from_lane = lax.broadcasted_iota(jnp.int32, (256, 768), 0)
    to_lane = lax.broadcasted_iota(jnp.int32, (256, 768), 1)
    spread = jnp.zeros((16, 768), jnp.float32)
    for p in range(4):
        place = jnp.where((from_lane < 192) & (to_lane == from_lane + 192 * p), 1.0, 0.0)
        spread = spread + jnp.dot(
            vec_v[p], place.astype(jnp.bfloat16), preferred_element_type=jnp.float32
        )
        for i in range(3):
            base = 768 * p + 256 * i
            bin_all[:, base : base + 256] = vec_v[p].astype(jnp.float32)[8 + i : 9 + i, :]
    vec_all[...] = spread
    for u in range(3):
        for j in pieces(u):
            on_y(u, j)
    for u in (3, 4, 5):
        for j in pieces(u):
            over_y(u, j).start()
    loads[3].wait()
    inputs = tok[...]

    def z_kv(d):
        return remote_copy(
            send_kv.at[zt[d]], kvg.at[pl.ds(2 * c, 2)], zk_s.at[d], zk_r.at[d], zp[d]
        )

    def arrived(d):
        return kvg.at[pl.ds((((z + 3 - d) % 4) * 2 + x) * 2, 2)]

    def z_kv_in(d):
        return remote_copy(arrived(d), arrived(d), zk_s.at[d], zk_r.at[d], zp[d])

    def own_x():
        return remote_copy(send_kv.at[z], kvg.at[pl.ds(2 * c, 2)], f_s.at[3], f_r.at[3], xp)

    def fwd_x(d):
        return remote_copy(arrived(d), arrived(d), f_s.at[d], f_r.at[d], xp)

    def z_q(d):
        return remote_copy(send_q.at[zt[d]], qg.at[z], zq_s.at[d], zq_r.at[d], zp[d])

    for u in (0, 1):
        for j in pieces(u):
            on_x(u, j)
        finish_recv(u)
    keys = jnp.dot(inputs, wk_v[...], preferred_element_type=jnp.float32).astype(jnp.bfloat16)
    values = jnp.dot(inputs, wv_v[...], preferred_element_type=jnp.float32) + vec_all[1:2, :]
    values = values.astype(jnp.bfloat16)
    join = split_pairs()
    for i in range(6):
        lanes = slice(128 * i, 128 * (i + 1))
        pair = jnp.concatenate([keys[:, lanes], values[:, lanes]], axis=1)
        pair = dot_nt(pair, join).astype(jnp.bfloat16)
        for t in (2 * i, 2 * i + 1):
            tile = pair[:, 128 * (t % 2) : 128 * (t % 2) + 128]
            send_kv[t // 3, :, :, pl.ds(128 * (t % 3), 128)] = tile.reshape(2, BLOCK, 128)
    own_x().start()
    for d in (1, 0, 2):
        z_kv(d).start()
    keep_kv = pltpu.make_async_copy(send_kv.at[z], kvg.at[pl.ds(2 * c, 2)], l_sem.at[0])
    keep_kv.start()
    for j in pieces(2):
        on_x(2, j)
    finish_recv(2)
    query = jnp.dot(inputs, wq_v[...], preferred_element_type=jnp.float32) + vec_all[0:1, :]
    query = query.astype(jnp.bfloat16)
    for part in range(4):
        send_q[part] = query[:, window_start(part) : window_start(part) + 256]
    for d in (1, 0, 2):
        z_q(d).start()
    keep_q = pltpu.make_async_copy(send_q.at[z], qg.at[z], l_sem.at[1])
    keep_q.start()
    outs = [
        pltpu.make_async_copy(src, dst, out_sem.at[i])
        for i, (src, dst) in enumerate(
            (
                (wq_v, wq_o),
                (wk_v, wk_o),
                (wv_v, wv_o),
                (vec_all, vec_o),
                (bin_all, bin_o),
                (qg, qg_o),
                (kvn, kvn_o),
                (kvt, kvt_o),
                (osave, os_o),
                (lse, lse_o),
                (attn, attn_o),
            )
        )
    ]
    for item in outs[:5]:
        item.start()
    natural = []
    for n in range(16):
        slot = jnp.int32(0)
        for b in range(1, 16):
            slot = jnp.where(deal[b] == n, b, slot)
        natural.append(slot)
    z_kv_in(0).wait_recv()
    fwd_x(0).start()
    z_kv_in(2).wait_recv()
    fwd_x(2).start()
    on_y(3, 0)
    z_kv_in(1).wait_recv()
    fwd_x(1).start()
    on_y(3, 1)
    keep_q.wait()
    for d in range(3):
        z_q(d).wait_recv()
    outs[5].start()
    scale = HEAD_DIM ** (-0.5)
    lift = (pick(z % 2, False, False) * scale).astype(jnp.bfloat16)
    gather = pick(z % 2, True, False).astype(jnp.bfloat16)
    for part in range(4):
        qt[:, pl.ds(256 * part, 256)] = dot_nt(lift, qg[part]).astype(jnp.bfloat16)
    keep_kv.wait()
    for d in range(3):
        fwd_x(d).wait_recv()
    own_x().wait_recv()
    on_y(4, 0)
    for j in pieces(3):
        on_x(3, j)
    for n in range(16):
        for h in range(3):
            tile = kvg[natural[n], :, pl.ds(128 * h, 128)]
            here = pl.ds((n % 8) * BLOCK, BLOCK)
            kvn[h, n // 8, here, :] = tile
            kvt[h, n // 8, :, here] = jnp.transpose(tile.astype(jnp.float32)).astype(jnp.bfloat16)
    outs[6].start()
    outs[7].start()
    span = 1024

    def o_copy(d):
        return remote_copy(owin.at[zt[d]], got.at[z], o_s.at[d], o_r.at[d], zp[d])

    def attend(part, i):
        b = part * 2 + i
        seq = jnp.where(deal[(part * 2 + x) * 2 + i] >= 8, 1, 0)
        length = lengths[seq]
        here = pl.ds(pl.multiple_of(b * BLOCK, BLOCK), BLOCK)
        key_rows = lax.broadcasted_iota(jnp.int32, (span, BLOCK), 0)
        made = []
        for h in range(3):
            scores = jnp.dot(
                kvn[h, seq], qt[pl.ds(128 * h, 128), here], preferred_element_type=jnp.float32
            )
            scores = jnp.where(key_rows < length, scores, NEG_FILL)
            top = jnp.max(scores, axis=0, keepdims=True)
            weights = jnp.exp(scores - top)
            total = jnp.sum(weights, axis=0, keepdims=True)
            mixed = jnp.dot(
                kvt[h, seq], weights.astype(jnp.bfloat16), preferred_element_type=jnp.float32
            )
            mixed = mixed / total
            osave[h, b] = mixed[64:]
            lse[h, b] = jnp.broadcast_to(top + jnp.log(total), (8, BLOCK))
            made.append(jnp.transpose(mixed).astype(jnp.bfloat16))
        owin[part, pl.ds(pl.multiple_of(i * BLOCK, BLOCK), BLOCK), :] = jnp.dot(
            jnp.concatenate(made, axis=1), gather, preferred_element_type=jnp.float32
        ).astype(jnp.bfloat16)

    for d in (1, 0, 2, 3):
        part = zt[d] if d < 3 else z
        pl.loop(0, 2)(functools.partial(attend, part))
        if d < 3:
            o_copy(d).start()
        on_y(5, {1: 0, 0: 1, 2: 2, 3: 3}[d])
    keep_o = pltpu.make_async_copy(owin.at[z], got.at[z], l_sem.at[2])
    keep_o.start()
    outs[8].start()
    outs[9].start()
    keep_o.wait()
    for d in range(3):
        o_copy(d).wait_recv()
    attn[...] = lane_windows([got[part] for part in range(4)])
    outs[10].start()
    own_x().wait_send()
    for d in range(3):
        z_kv(d).wait_send()
        z_q(d).wait_send()
        fwd_x(d).wait_send()
        o_copy(d).wait_send()
        vec(d, vec_peers[d]).wait_send()
    for u in (3, 4, 5):
        finish_recv(u)
    for u in range(6):
        finish_send(u)
    for item in outs:
        item.wait()


def forward(deal, lengths, tok, shards, small):
    rows, width = tok.shape
    bf, f32, d, v = jnp.bfloat16, jnp.float32, pltpu.SemaphoreType.DMA, pltpu.VMEM
    count = sum(item[1] for item in GATHER_PIECES)
    wide = shards[3].shape[1]
    deep = shards[5].shape[0]
    scratch = [v((rows, width), bf)]
    scratch += [v(item.shape, f32) for item in shards]
    scratch += [v(item.shape, f32) for item in small]
    scratch += [
        v((width, width), bf),
        v((width, width), bf),
        v((width, width), bf),
        v((width // 4, wide), bf),
        v((width // 4, width), bf),
        v((deep, width), bf),
        v((4, 16, 256), bf),
        v((16, width), f32),
        v((1, wide), f32),
        v((4, 2, BLOCK, 384), bf),
        v((4, rows, 256), bf),
        v((16, BLOCK, 384), bf),
        v((4, rows, 256), bf),
        v((3, 2, 1024, 128), bf),
        v((3, 2, 128, 1024), bf),
        v((384, 1024), bf),
        v((4, rows, 256), bf),
        v((4, rows, 256), bf),
        v((3, 8, 64, BLOCK), f32),
        v((3, 8, 8, BLOCK), f32),
        v((rows, width), bf),
        d((16,)),
        d((6,)),
        d((6,)),
        d((6,)),
    ]
    scratch += [d((count,))] * 8
    scratch += [d((3,))] * 6 + [d((4,)), d((4,)), d((3,)), d((3,)), d((3,)), d((11,))]
    return pl.pallas_call(
        forward_kernel,
        out_shape=[
            half(rows, width),
            half(4, rows, 256),
            half(3, 2, 1024, 128),
            half(3, 2, 128, 1024),
            full(3, 8, 64, BLOCK),
            full(3, 8, 8, BLOCK),
            half(width, width),
            half(width, width),
            half(width, width),
            half(width, width),
            half(width, wide),
            half(4 * deep, width),
            full(16, width),
            full(1, wide),
        ],
        in_specs=[pl.BlockSpec(memory_space=pltpu.SMEM)] * 2 + any_specs(16),
        out_specs=any_specs(14),
        scratch_shapes=scratch,
        compiler_params=pltpu.CompilerParams(
            collective_id=2, has_side_effects=True, vmem_limit_bytes=56 * 2**20
        ),
        cost_estimate=pl.CostEstimate(flops=10**10, bytes_accessed=10**8, transcendentals=0),
        name="forward",
    )(deal, lengths, tok, *shards, *small)


def body_fast(
    tokens,
    seq_lengths,
    deal,
    w_query,
    w_key,
    w_value,
    w_attn_out,
    b_query,
    b_value,
    b_attn_out,
    norm1_gain,
    norm1_bias,
    w_in,
    b_in,
    w_out,
    b_out,
    norm2_gain,
    norm2_bias,
    cotangent,
):
    inputs = tokens[0]
    width = inputs.shape[1]
    part = width // 4
    odd = lax.axis_index("fsdp") % 2 == 1
    deal_row = deal[0]
    lengths = seq_lengths[0]
    (
        attn_in,
        query_groups,
        pairs,
        pairs_turned,
        out_heads,
        log_totals,
        query_weight,
        key_weight,
        value_weight,
        mix_weight,
        inner_weight,
        outer_weight,
        vectors,
        inner_bias,
    ) = forward(
        deal_row,
        lengths,
        inputs,
        [w_key, w_value, w_query, w_in, w_attn_out, w_out],
        [
            item.reshape(1, -1)
            for item in (
                b_query,
                b_value,
                b_attn_out,
                norm1_gain,
                norm1_bias,
                b_out,
                norm2_gain,
                norm2_bias,
                b_in,
            )
        ],
    )
    mix_bias, gain_one, shift_one, outer_bias, gain_two, shift_two = (
        vectors[2 + i] for i in range(6)
    )
    inner_bias = inner_bias[0]
    residual_one = (
        inputs.astype(jnp.float32)
        + jnp.dot(attn_in, mix_weight, preferred_element_type=jnp.float32)
        + mix_bias
    )
    normal_one, normed_one, inverse_one = norm_forward(residual_one, gain_one, shift_one)
    normal_half = normal_one.astype(jnp.bfloat16)
    pre_act = jnp.dot(normal_half, inner_weight, preferred_element_type=jnp.float32) + inner_bias
    activated, gelu_pull = jax.vjp(exact_gelu, pre_act)
    hidden = activated.astype(jnp.bfloat16)
    residual_two = (
        normal_one
        + jnp.dot(hidden, outer_weight, preferred_element_type=jnp.float32)
        + outer_bias
    )
    layer_out, normed_two, inverse_two = norm_forward(residual_two, gain_two, shift_two)
    upstream = cotangent[0].astype(jnp.float32)
    grad_two, grad_gain_two, grad_shift_two = norm_backward(
        upstream, gain_two, normed_two, inverse_two
    )
    grad_branch = grad_two.astype(jnp.bfloat16)
    grad_outer_bias = jnp.sum(grad_branch.astype(jnp.float32), axis=0)
    grad_outer = jnp.einsum("tf,td->fd", hidden, grad_branch, preferred_element_type=jnp.float32)
    grad_hidden = jnp.einsum(
        "td,fd->tf", grad_branch, outer_weight, preferred_element_type=jnp.float32
    )
    grad_pre = gelu_pull(grad_hidden)[0].astype(jnp.bfloat16)
    grad_inner_bias = jnp.sum(grad_pre.astype(jnp.float32), axis=0)
    grad_inner = jnp.einsum("td,tf->df", normal_half, grad_pre, preferred_element_type=jnp.float32)
    grad_normal = grad_two + jnp.einsum(
        "tf,df->td", grad_pre, inner_weight, preferred_element_type=jnp.float32
    )
    grad_one, grad_gain_one, grad_shift_one = norm_backward(
        grad_normal, gain_one, normed_one, inverse_one
    )
    grad_attn = grad_one.astype(jnp.bfloat16)
    grad_mix_bias = jnp.sum(grad_attn.astype(jnp.float32), axis=0)
    grad_mix = jnp.einsum("td,te->de", attn_in, grad_attn, preferred_element_type=jnp.float32)
    grad_mixed = jnp.einsum(
        "te,de->td", grad_attn, mix_weight, preferred_element_type=jnp.float32
    ).astype(jnp.bfloat16)
    (
        grad_inputs,
        sum_outer,
        sum_inner,
        sum_mix,
        sum_query,
        sum_key,
        sum_value,
        sum_small,
    ) = backward(
        deal_row,
        lengths,
        deal_row // 8,
        grad_mixed,
        query_groups,
        out_heads,
        log_totals,
        pairs,
        pairs_turned,
        inputs,
        query_weight,
        key_weight,
        value_weight,
        grad_one,
        to_half(grad_outer),
        to_half(grad_inner),
        to_half(grad_mix),
        [
            item.reshape(1, -1)
            for item in (
                grad_mix_bias,
                grad_gain_one,
                grad_shift_one,
                grad_outer_bias,
                grad_gain_two,
                grad_shift_two,
                grad_inner_bias,
            )
        ],
    )
    sum_small = sum_small.astype(jnp.float32)
    small = jnp.where(odd, sum_small[:8, HEAD_DIM:], sum_small[:8, :part])
    others = small[2:]
    return (
        layer_out.astype(jnp.bfloat16)[None],
        grad_inputs[None],
        sum_query.astype(jnp.float32),
        sum_key.astype(jnp.float32),
        sum_value.astype(jnp.float32),
        sum_mix.astype(jnp.float32),
        small[0],
        small[1],
        others[0],
        others[1],
        others[2],
        sum_inner.astype(jnp.float32),
        sum_small[8:11].reshape(width),
        sum_outer.astype(jnp.float32),
        others[3],
        others[4],
        others[5],
    )


def solution(mesh):
    placed = (
        P("fsdp", "ctx", None),
        P("fsdp", None),
        P("fsdp", None),
        P("fsdp", None),
        P("fsdp", None),
        P("fsdp", None),
        P("fsdp", None),
        P("fsdp"),
        P("fsdp"),
        P("fsdp"),
        P("fsdp"),
        P("fsdp"),
        P("fsdp", None),
        P("fsdp"),
        P("fsdp", None),
        P("fsdp"),
        P("fsdp"),
        P("fsdp"),
        P("fsdp", "ctx", None),
    )
    fast = dict(mesh.shape) == {"ctx": 8, "fsdp": 4}
    return jax.shard_map(
        body_fast if fast else body,
        mesh=mesh,
        in_specs=placed,
        out_specs=(
            P("fsdp", "ctx", None),
            P("fsdp", "ctx", None),
            P("fsdp", None),
            P("fsdp", None),
            P("fsdp", None),
            P("fsdp", None),
            P("fsdp"),
            P("fsdp"),
            P("fsdp"),
            P("fsdp"),
            P("fsdp"),
            P("fsdp", None),
            P("fsdp"),
            P("fsdp", None),
            P("fsdp"),
            P("fsdp"),
            P("fsdp"),
        ),
        check_vma=False,
    )
```
